32 devices in a mesh: seq: 4 (over y, core), tensor: 8 (over z, x).
Axes of the slice: x: 2, y: 2, z: 4, core: 2. Of those that a mesh axis runs over, the one named last changes fastest.
Arguments:
- tokens: bfloat16 [128, 12288], P('tensor', 'seq'), may hold values from -6 to 6
- in_blocks: bfloat16 [4, 8, 288, 128, 128], P('seq', 'tensor'), may hold values from -0.109375 to 0.109375
- in_slots: int32 [4, 8, 288], P('seq', 'tensor'), may hold values from -1 to 575, as said below
- out_blocks: bfloat16 [8, 4, 288, 128, 128], P('tensor', 'seq'), may hold values from -0.078125 to 0.078125
- out_slots: int32 [8, 4, 288], P('tensor', 'seq'), may hold values from -1 to 575, as said below
- cotangent: bfloat16 [128, 12288], P('tensor', 'seq'), may hold values from -6 to 6
Outputs:
- output: bfloat16 [128, 12288], P('tensor', 'seq')
- grad_tokens: bfloat16 [128, 12288], P('tensor', 'seq')
- grad_in: float32 [4, 8, 288, 128, 128], P('seq', 'tensor')
- grad_out: float32 [8, 4, 288, 128, 128], P('tensor', 'seq')
The draws below stay inside these ranges and needn't reach their ends.
Inputs may be any that keep to these rules, and one draw needn't show every extreme that they name: `in_slots`: on every shard the 288 slots hold distinct block positions below 576, the filled slots first and -1 after them; every shard has at least one filled slot and some shard has all 288 filled. `out_slots`: on every shard the 288 slots hold distinct block positions below 576, the filled slots first and -1 after them; every shard has at least one filled slot and some shard has all 288 filled.
All inputs are finite; a program needn't handle non-finite values.
Results may differ from the reference program's by a relative error of at most 0.019.
Values may be sent and summed in bfloat16 or wider, within the bound.
No kernel may reach another device: no remote copies, remote signals or barrier semaphores. Data moves between devices by JAX's collectives and lax.ppermute only.
A program may use at most 192 MiB of HBM per device.

```python
import jax
import jax.numpy as jnp
from jax import lax

D = 12288
F = 24576
BLOCK = 128
TOKENS = 128
LOCAL_BLOCKS = 576
CAP = 288
N_SEQ = 4
N_TENSOR = 8


def slot_draw(key, lead_first, lead_second):
    shard_count = lead_first * lead_second
    count_key, order_key, pick_key = jax.random.split(key, 3)
    counts = jax.random.randint(count_key, (shard_count,), 1, CAP + 1)
    chosen = jax.random.randint(pick_key, (), 0, shard_count)
    counts = jnp.where(jnp.arange(shard_count) == chosen, CAP, counts)
    shard_keys = jax.random.split(order_key, shard_count)
    orders = jax.vmap(lambda shard_key: jax.random.permutation(shard_key, LOCAL_BLOCKS))(shard_keys)[:, :CAP]
    slot_list = jnp.where(jnp.arange(CAP)[None, :] < counts[:, None], orders, -1)
    return slot_list.reshape(lead_first, lead_second, CAP).astype(jnp.int32)


def draw_in_slots(key, part):
    return slot_draw(jax.random.fold_in(key, 11), N_SEQ, N_TENSOR)


def draw_out_slots(key, part):
    return slot_draw(jax.random.fold_in(key, 23), N_TENSOR, N_SEQ)


def block_scale(stream_key, shape, cuts, smallest, largest):
    def one(position, blocks):
        heights = jax.random.uniform(jax.random.fold_in(jax.random.fold_in(stream_key, 6), position), (blocks,), jnp.float32, smallest / len(cuts), largest / len(cuts))
        return jnp.repeat(jnp.exp(heights), shape[position] // blocks).reshape((-1,) + (1,) * (len(shape) - position - 1))

    factor_of = one(*cuts[0])
    for cut in cuts[1:]:
        factor_of = factor_of * one(*cut)
    return factor_of


def noise(stream_key, shape, deviation, bound, cuts=(), kind=jnp.bfloat16):
    gain = block_scale(stream_key, shape, cuts, -0.22, 0.18) if cuts else 1.0
    drawn = jax.random.normal(stream_key, shape, jnp.float32) * deviation * gain
    return jnp.minimum(jnp.maximum(drawn, -bound), bound).astype(kind)


def setup_inputs(seed: int = 0) -> dict:
    arg_keys = jax.random.split(jax.random.key(seed), 7)
    tokens = noise(arg_keys[0], (TOKENS, D), 1.0, 6.0, ((0, 8), (1, 4)))
    in_blocks = noise(arg_keys[1], (N_SEQ, N_TENSOR, CAP, BLOCK, BLOCK), (D // 4) ** -0.5, 0.109375, ((0, 4), (1, 8)))
    in_slots = draw_in_slots(jax.random.fold_in(arg_keys[6], 71), 0)
    out_blocks = noise(arg_keys[3], (N_TENSOR, N_SEQ, CAP, BLOCK, BLOCK), (F // 4) ** -0.5, 0.078125, ((0, 8), (1, 4)))
    out_slots = draw_out_slots(jax.random.fold_in(arg_keys[6], 71), 0)
    cotangent = noise(arg_keys[5], (TOKENS, D), 1.0, 6.0, ((0, 8), (1, 4)))
    return dict(tokens=tokens, in_blocks=in_blocks, in_slots=in_slots, out_blocks=out_blocks, out_slots=out_slots, cotangent=cotangent)


GELU_SCALE = 0.7978845608028654
GELU_CUBE = 0.044715
HIGHEST = lax.Precision.HIGHEST


def gelu_value(values):
    return 0.5 * values * (1.0 + jnp.tanh(GELU_SCALE * (values + GELU_CUBE * values * values * values)))


def gelu_slope(values):
    tangent = jnp.tanh(GELU_SCALE * (values + GELU_CUBE * values * values * values))
    return 0.5 * (1.0 + tangent) + 0.5 * values * (1.0 - tangent * tangent) * GELU_SCALE * (1.0 + 3.0 * GELU_CUBE * values * values)


def slot_tables(slot_list, col_blocks):
    filled = slot_list >= 0
    clipped = jnp.where(filled, slot_list, 0).astype(jnp.int32)
    return clipped // col_blocks, clipped % col_blocks, filled


def placement_table(index_of, filled, extent):
    return ((index_of[:, None] == jnp.arange(extent, dtype=jnp.int32)[None, :]) & filled[:, None]).astype(jnp.float32)


def forward_blocks(source, blocks, slot_list, row_blocks, col_blocks):
    length = source.shape[0]
    block_width = blocks.shape[-1]
    row_of, col_of, filled = slot_tables(slot_list, col_blocks)
    picked = jnp.take(source.reshape(length, row_blocks, block_width), row_of, axis=1)
    products = jnp.einsum("tsk,skn->tsn", picked.astype(jnp.float32), blocks.astype(jnp.float32), precision=HIGHEST)
    placed = jnp.einsum("tsn,sc->tcn", products, placement_table(col_of, filled, col_blocks), precision=HIGHEST)
    return placed.reshape(length, col_blocks * block_width)


def backward_blocks(source, blocks, slot_list, row_blocks, col_blocks):
    length = source.shape[0]
    block_width = blocks.shape[-1]
    row_of, col_of, filled = slot_tables(slot_list, col_blocks)
    picked = jnp.take(source.reshape(length, col_blocks, block_width), col_of, axis=1)
    products = jnp.einsum("tsn,skn->tsk", picked.astype(jnp.float32), blocks.astype(jnp.float32), precision=HIGHEST)
    placed = jnp.einsum("tsk,sr->trk", products, placement_table(row_of, filled, row_blocks), precision=HIGHEST)
    return placed.reshape(length, row_blocks * block_width)


def block_grads(left, right, slot_list, row_blocks, col_blocks):
    length = left.shape[0]
    block_width = right.shape[-1] // col_blocks
    row_of, col_of, filled = slot_tables(slot_list, col_blocks)
    left_picked = jnp.take(left.reshape(length, row_blocks, block_width), row_of, axis=1)
    right_picked = jnp.take(right.reshape(length, col_blocks, block_width), col_of, axis=1)
    grads = jnp.einsum("tsk,tsn->skn", left_picked.astype(jnp.float32), right_picked.astype(jnp.float32), precision=HIGHEST)
    return grads * filled[:, None, None].astype(jnp.float32)


def rounded(values):
    return lax.optimization_barrier(values.astype(jnp.bfloat16)).astype(jnp.float32)


def part_of(matrix, part_index, part_width):
    offset = (jnp.asarray(part_index, jnp.int32) * part_width).astype(jnp.int32)
    return lax.dynamic_slice_in_dim(matrix, offset, part_width, 1)


def stacked(pieces):
    return jnp.transpose(pieces, (1, 0, 2)).reshape(pieces.shape[1], pieces.shape[0] * pieces.shape[2])


def reference(tokens, in_blocks, in_slots, out_blocks, out_slots, cotangent):
    features = D // N_SEQ
    hidden_units = F // N_TENSOR
    row_blocks = features // BLOCK
    col_blocks = hidden_units // BLOCK
    seq_parts = jnp.arange(N_SEQ, dtype=jnp.int32)
    tensor_parts = jnp.arange(N_TENSOR, dtype=jnp.int32)

    def hidden_part(col_part):
        def accumulate(row_part, running):
            term = forward_blocks(part_of(tokens, row_part, features), in_blocks[row_part, col_part], in_slots[row_part, col_part], row_blocks, col_blocks)
            return running + rounded(term)
        return lax.fori_loop(0, N_SEQ, accumulate, jnp.zeros((TOKENS, hidden_units), jnp.float32))

    hidden = stacked(lax.map(hidden_part, tensor_parts))
    activated = gelu_value(hidden).astype(jnp.bfloat16)

    def output_part(row_part):
        def accumulate(col_part, running):
            term = forward_blocks(part_of(activated, col_part, hidden_units), out_blocks[col_part, row_part], out_slots[col_part, row_part], col_blocks, row_blocks)
            return running + rounded(term)
        return lax.fori_loop(0, N_TENSOR, accumulate, jnp.zeros((TOKENS, features), jnp.float32))

    output = stacked(lax.map(output_part, seq_parts)).astype(jnp.bfloat16)

    def grad_act_part(col_part):
        def accumulate(row_part, running):
            term = backward_blocks(part_of(cotangent, row_part, features), out_blocks[col_part, row_part], out_slots[col_part, row_part], col_blocks, row_blocks)
            return running + rounded(term)
        return lax.fori_loop(0, N_SEQ, accumulate, jnp.zeros((TOKENS, hidden_units), jnp.float32))

    grad_act = stacked(lax.map(grad_act_part, tensor_parts))
    grad_hidden = (grad_act * gelu_slope(hidden)).astype(jnp.bfloat16)

    def grad_token_part(row_part):
        def accumulate(col_part, running):
            term = backward_blocks(part_of(grad_hidden, col_part, hidden_units), in_blocks[row_part, col_part], in_slots[row_part, col_part], row_blocks, col_blocks)
            return running + rounded(term)
        return lax.fori_loop(0, N_TENSOR, accumulate, jnp.zeros((TOKENS, features), jnp.float32))

    grad_tokens = stacked(lax.map(grad_token_part, seq_parts)).astype(jnp.bfloat16)

    def grad_in_row(row_part):
        def grad_in_cell(col_part):
            return block_grads(part_of(tokens, row_part, features), part_of(grad_hidden, col_part, hidden_units), in_slots[row_part, col_part], row_blocks, col_blocks)
        return lax.map(grad_in_cell, tensor_parts)

    grad_in = lax.map(grad_in_row, seq_parts)

    def grad_out_row(col_part):
        def grad_out_cell(row_part):
            return block_grads(part_of(activated, col_part, hidden_units), part_of(cotangent, row_part, features), out_slots[col_part, row_part], col_blocks, row_blocks)
        return lax.map(grad_out_cell, seq_parts)

    grad_out = lax.map(grad_out_row, tensor_parts)
    return (output, grad_tokens, grad_in, grad_out)
```

```python
import functools

import jax
import jax.numpy as jnp
from jax import lax
from jax.experimental import pallas as pl
from jax.experimental.pallas import tpu as pltpu
from jax.sharding import PartitionSpec as P

GELU_SCALE = 0.7978845608028654
GELU_CUBE = 0.044715


def gelu_value(values):
    return (
        0.5
        * values
        * (1.0 + jnp.tanh(GELU_SCALE * (values + GELU_CUBE * values * values * values)))
    )


def gelu_slope(values):
    tangent = jnp.tanh(GELU_SCALE * (values + GELU_CUBE * values * values * values))
    return 0.5 * (1.0 + tangent) + 0.5 * values * (1.0 - tangent * tangent) * GELU_SCALE * (
        1.0 + 3.0 * GELU_CUBE * values * values
    )


def largest_divisor(number, limit):
    return max(d for d in range(1, limit + 1) if number % d == 0)


def load_pieces(piece_refs, offsets, store, width):
    for i, piece in enumerate(piece_refs):
        length = piece.shape[0]
        start = offsets(i, length)
        for b in range(piece.shape[1] // width):
            store[b, pl.ds(start, length), :] = piece[:, b * width : (b + 1) * width]


def block_product(pieces, in_rows, blocks, src, dst, info, n_dst, out_lengths, out_rows, transposed):
    cap, width = blocks.shape[0], blocks.shape[1]
    n_src = pieces[0].shape[1] // width
    tokens = sum(piece.shape[0] for piece in pieces)
    chunk = largest_divisor(cap, 32)
    unroll = largest_divisor(chunk, 8)
    steps = cap // chunk
    dims = (((1,), (1 if transposed else 0,)), ((), ()))
    zero_rows = jnp.zeros((1,), jnp.int32)
    in_arr = zero_rows if in_rows is None else in_rows
    out_arr = zero_rows if out_rows is None else out_rows
    n_in, n_out = len(pieces), len(out_lengths)

    def body(src_s, dst_s, info_s, in_s, out_s, *refs):
        piece_refs = refs[:n_in]
        w_ref = refs[n_in]
        out_refs = refs[n_in + 1 : n_in + 1 + n_out]
        xs, acc = refs[n_in + 1 + n_out :]
        step = pl.program_id(0)

        @pl.when(step == 0)
        def _():
            if in_rows is None:
                place = lambda i, length: i * length
            else:
                place = lambda i, length: pl.multiple_of(in_s[i], length)
            load_pieces(piece_refs, place, xs, width)
            acc[...] = jnp.zeros_like(acc)

        @pl.when(step <= info_s[0])
        def _():
            def some(g, carry):
                base = g * unroll
                terms = []
                for u in range(unroll):
                    k = step * chunk + base + u
                    terms.append(
                        lax.dot_general(
                            xs[src_s[k]], w_ref[base + u], dims, preferred_element_type=jnp.float32
                        )
                    )
                for u in range(unroll):
                    k = step * chunk + base + u
                    acc[dst_s[k]] += terms[u]
                return carry

            lax.fori_loop(0, chunk // unroll, some, 0)

        @pl.when(step == steps - 1)
        def _():
            at = 0
            for i, ref in enumerate(out_refs):
                lead = ref.shape[:-2]
                length = ref.shape[-2]
                for j in range(lead[0] if lead else 1):
                    start = at * length if out_rows is None else pl.multiple_of(out_s[at], length)
                    at += 1
                    for b in range(n_dst):
                        val = acc[b, pl.ds(start, length), :].astype(jnp.bfloat16)
                        if lead:
                            ref[j, :, b * width : (b + 1) * width] = val
                        else:
                            ref[:, b * width : (b + 1) * width] = val

    whole = lambda shape: pl.BlockSpec(shape, lambda i, *s: (0,) * len(shape))
    out_shapes = [shape + (n_dst * width,) for shape in out_lengths]
    return pl.pallas_call(
        body,
        grid_spec=pltpu.PrefetchScalarGridSpec(
            num_scalar_prefetch=5,
            grid=(steps,),
            in_specs=[whole(piece.shape) for piece in pieces]
            + [
                pl.BlockSpec(
                    (chunk, width, width), lambda i, s, d, info_s, a, b: (jnp.minimum(i, info_s[0]), 0, 0)
                )
            ],
            out_specs=[whole(shape) for shape in out_shapes],
            scratch_shapes=[
                pltpu.VMEM((n_src, tokens, width), jnp.bfloat16),
                pltpu.VMEM((n_dst + 1, tokens, width), jnp.float32),
            ],
        ),
        out_shape=[jax.ShapeDtypeStruct(shape, jnp.bfloat16) for shape in out_shapes],
        compiler_params=pltpu.CompilerParams(dimension_semantics=("arbitrary",)),
        cost_estimate=pl.CostEstimate(
            flops=2 * cap * tokens * width * width,
            bytes_accessed=cap * width * width * 2 + tokens * width * 2 * (n_src + n_dst),
            transcendentals=0,
        ),
        name="block_product",
    )(src, dst, info, in_arr, out_arr, *pieces, blocks)


def block_grads(left, left_rows, right, right_rows, rows, cols, cap):
    width = 128
    n_left, n_right = left[0].shape[1] // width, right[0].shape[1] // width
    tokens = sum(piece.shape[0] for piece in left)
    chunk = largest_divisor(cap, 32)
    unroll = largest_divisor(chunk, 8)
    steps = cap // chunk
    n_l, n_r = len(left), len(right)
    dims = (((1,), (0,)), ((), ()))
    zero_rows = jnp.zeros((1,), jnp.int32)
    left_arr = zero_rows if left_rows is None else left_rows
    right_arr = zero_rows if right_rows is None else right_rows

    def body(row_s, col_s, left_s, right_s, *refs):
        l_refs = refs[:n_l]
        r_refs = refs[n_l : n_l + n_r]
        out = refs[n_l + n_r]
        ls, lt, rs = refs[n_l + n_r + 1 :]
        step = pl.program_id(0)

        @pl.when(step == 0)
        def _():
            def place(given, table):
                if given is None:
                    return lambda i, length: i * length
                return lambda i, length: pl.multiple_of(table[i], length)

            load_pieces(l_refs, place(left_rows, left_s), ls, width)
            load_pieces(r_refs, place(right_rows, right_s), rs, width)
            rs[n_right] = jnp.zeros((tokens, width), rs.dtype)
            for b in range(n_left):
                lt[b] = ls[b].T

        def some(g, carry):
            base = g * unroll
            for u in range(unroll):
                k = step * chunk + base + u
                out[base + u] = lax.dot_general(
                    lt[row_s[k]], rs[col_s[k]], dims, preferred_element_type=jnp.float32
                )
            return carry

        lax.fori_loop(0, chunk // unroll, some, 0)

    whole = lambda shape: pl.BlockSpec(shape, lambda i, *s: (0,) * len(shape))
    return pl.pallas_call(
        body,
        grid_spec=pltpu.PrefetchScalarGridSpec(
            num_scalar_prefetch=4,
            grid=(steps,),
            in_specs=[whole(piece.shape) for piece in left] + [whole(piece.shape) for piece in right],
            out_specs=pl.BlockSpec((chunk, width, width), lambda i, *s: (i, 0, 0)),
            scratch_shapes=[
                pltpu.VMEM((n_left, tokens, width), jnp.bfloat16),
                pltpu.VMEM((n_left, width, tokens), jnp.bfloat16),
                pltpu.VMEM((n_right + 1, tokens, width), jnp.bfloat16),
            ],
        ),
        out_shape=jax.ShapeDtypeStruct((cap, width, width), jnp.float32),
        compiler_params=pltpu.CompilerParams(dimension_semantics=("arbitrary",)),
        cost_estimate=pl.CostEstimate(
            flops=2 * cap * tokens * width * width,
            bytes_accessed=cap * width * width * 4 + tokens * width * 2 * (n_left + n_right),
            transcendentals=0,
        ),
        name="block_grads",
    )(rows, cols, left_arr, right_arr, *left, *right)


def on_device(tokens, in_blocks, in_slots, out_blocks, out_slots, cotangent, *, hidden_total):
    w_in = in_blocks.reshape(in_blocks.shape[2:])
    w_out = out_blocks.reshape(out_blocks.shape[2:])
    slots_in = in_slots.reshape(-1)
    slots_out = out_slots.reshape(-1)
    width = w_in.shape[-1]
    cap = w_in.shape[0]
    tensor_count = lax.axis_size("tensor")
    seq_count = lax.axis_size("seq")
    feat_blocks = tokens.shape[1] // width
    hid_blocks = hidden_total // tensor_count // width
    tensor_rows = tokens.shape[0]
    token_count = tensor_rows * tensor_count
    seq_rows = token_count // seq_count
    far_t, far_s = tensor_count // 2, seq_count // 2

    def near_move(v, axis, count):
        return lax.ppermute(v, axis, [(i, i ^ 1) for i in range(count)])

    def far_move(v, axis, count, shift):
        half = count // 2
        pairs = [(o * 2 + c, ((o + shift) % half) * 2 + c) for o in range(half) for c in range(2)]
        return lax.ppermute(v, axis, pairs)

    me = lax.axis_index("seq")
    shifts = jnp.arange(seq_count, dtype=jnp.int32)
    far_of = (me // 2 + far_s - shifts // 2) % far_s
    seq_part = (far_of * 2 + (me % 2 + shifts % 2) % 2) * seq_rows
    near_order = jnp.concatenate([seq_part[0::2], seq_part[1::2]])

    def tables(slot_list, col_blocks, row_blocks):
        filled = slot_list >= 0
        safe = jnp.where(filled, slot_list, 0)
        row, col = safe // col_blocks, safe % col_blocks
        count = jnp.sum(filled.astype(jnp.int32))
        last = (count - 1) // largest_divisor(cap, 32)
        return (
            row,
            col,
            jnp.where(filled, row, row_blocks),
            jnp.where(filled, col, col_blocks),
            last[None],
        )

    in_row, in_col, in_row_dst, in_col_dst, in_last = tables(slots_in, hid_blocks, feat_blocks)
    out_row, out_col, out_row_dst, out_col_dst, out_last = tables(slots_out, feat_blocks, hid_blocks)

    def gather_panel(own):
        far = [own] + [far_move(own, "tensor", tensor_count, k) for k in range(1, far_t)]
        pieces = []
        for piece in far:
            pieces += [piece, near_move(piece, "tensor", tensor_count)]
        return pieces

    def sum_out(terms):
        keep, send = terms[0::2], terms[1::2]
        order = list(range(1, far_t)) + [0]
        got = {k: near_move(send[k], "tensor", tensor_count) for k in order}
        pair = {k: keep[k].astype(jnp.float32) + got[k].astype(jnp.float32) for k in order}
        total = pair[0]
        for k in range(1, far_t):
            moved = far_move(pair[k].astype(jnp.bfloat16), "tensor", tensor_count, far_t - k)
            total = total + moved.astype(jnp.float32)
        return total.astype(jnp.bfloat16)

    def sum_hidden(keep, send):
        got = near_move(send, "seq", seq_count)
        total = keep[0].astype(jnp.float32) + got[0].astype(jnp.float32)
        for k in range(1, far_s):
            pair = (keep[k].astype(jnp.float32) + got[k].astype(jnp.float32)).astype(jnp.bfloat16)
            total = total + far_move(pair, "seq", seq_count, far_s - k).astype(jnp.float32)
        return total

    def spread_hidden(own):
        pieces = []
        far = [own] + [far_move(own, "seq", seq_count, k) for k in range(1, far_s)]
        for piece in far:
            pieces += [piece, near_move(piece, "seq", seq_count)]
        return pieces

    hidden_lengths = [(far_s, seq_rows)] * 2
    token_lengths = [(tensor_rows,)] * tensor_count

    tok = gather_panel(tokens)
    cot = gather_panel(cotangent)
    keep_h, send_h = block_product(
        tok, None, w_in, in_row, in_col_dst, in_last, hid_blocks, hidden_lengths, near_order, False
    )
    keep_g, send_g = block_product(
        cot, None, w_out, out_col, out_row_dst, out_last, hid_blocks, hidden_lengths, near_order, True
    )
    hidden = sum_hidden(keep_h, send_h)
    activated = spread_hidden(gelu_value(hidden).astype(jnp.bfloat16))
    grad_act = sum_hidden(keep_g, send_g)
    grad_hidden = spread_hidden((grad_act * gelu_slope(hidden)).astype(jnp.bfloat16))

    output = sum_out(
        block_product(
            activated, seq_part, w_out, out_row, out_col_dst, out_last, feat_blocks, token_lengths, None, False
        )
    )
    grad_tokens = sum_out(
        block_product(
            grad_hidden, seq_part, w_in, in_col, in_row_dst, in_last, feat_blocks, token_lengths, None, True
        )
    )
    grad_out = block_grads(activated, seq_part, cot, None, out_row, out_col_dst, cap)
    grad_in = block_grads(tok, None, grad_hidden, seq_part, in_row, in_col_dst, cap)
    return (
        output,
        grad_tokens,
        grad_in.reshape(in_blocks.shape),
        grad_out.reshape(out_blocks.shape),
    )


HIDDEN_TOTAL = 24576


def solution(mesh):
    return jax.shard_map(
        functools.partial(on_device, hidden_total=HIDDEN_TOTAL),
        mesh=mesh,
        in_specs=(
            P("tensor", "seq"),
            P("seq", "tensor", None, None, None),
            P("seq", "tensor", None),
            P("tensor", "seq", None, None, None),
            P("tensor", "seq", None),
            P("tensor", "seq"),
        ),
        out_specs=(
            P("tensor", "seq"),
            P("tensor", "seq"),
            P("seq", "tensor", None, None, None),
            P("tensor", "seq", None, None, None),
        ),
        check_vma=False,
    )
```

```python
import jax
import jax.numpy as jnp
from jax import lax
from jax.experimental import pallas as pl
from jax.experimental.pallas import tpu as pltpu
from jax.sharding import PartitionSpec as P


GELU_SCALE = 0.7978845608028654
GELU_CUBE = 0.044715


def gelu_value(values):
    return (
        0.5
        * values
        * (1.0 + jnp.tanh(GELU_SCALE * (values + GELU_CUBE * values * values * values)))
    )


def gelu_slope(values):
    tangent = jnp.tanh(GELU_SCALE * (values + GELU_CUBE * values * values * values))
    return 0.5 * (1.0 + tangent) + 0.5 * values * (1.0 - tangent * tangent) * GELU_SCALE * (
        1.0 + 3.0 * GELU_CUBE * values * values
    )


def after(values, *earlier):
    return lax.optimization_barrier((values, earlier))[0]


def largest_divisor(number, limit):
    return max(d for d in range(1, limit + 1) if number % d == 0)


def load_pieces(piece_refs, offsets, store, width):
    for i, piece in enumerate(piece_refs):
        length = piece.shape[0]
        start = offsets(i, length)
        for b in range(piece.shape[1] // width):
            store[b, pl.ds(start, length), :] = piece[:, b * width : (b + 1) * width]


def pair_tables(jobs, weights):
    cap = jobs[0][0].shape[0]
    specs = [job[1:] for job in jobs]
    n = len(jobs)
    limits = [pair_limit(cap, rows if by_row else cols) for rows, cols, by_row in specs]

    def body(*refs):
        refs = refs[:n] + refs[n + len(weights) :]
        slot_refs, tables, pending = refs[:n], refs[n : 2 * n], refs[2 * n :]
        for (rows, cols, by_row), pend in zip(specs, pending):

            def clear(i, carry, pend=pend):
                pend[i] = -1
                return carry

            lax.fori_loop(0, (rows if by_row else cols) + 1, clear, 0)

        def one(k, counts):
            counts = list(counts)
            for t, (rows, cols, by_row) in enumerate(specs):
                pos = slot_refs[t][k]
                filled = pos >= 0
                safe = jnp.maximum(pos, 0)
                row = (safe * (-(-65536 // cols))) >> 16
                col = safe - row * cols
                key, src, end = (row, col, rows) if by_row else (col, row, cols)
                table, pend, limit = tables[t], pending[t], limits[t]
                key = jnp.where(filled, key, end)
                first = pend[key]
                word = k + src * 4096
                paired = jnp.logical_and(first >= 0, filled)
                at = counts[t]
                table[at] = first
                table[limit + at] = word
                table[2 * limit + at] = key
                pend[key] = jnp.where(first >= 0, -1, word)
                counts[t] = at + paired.astype(jnp.int32)
            return tuple(counts)

        counts = lax.fori_loop(0, cap, one, (jnp.int32(0),) * n)
        for t, (rows, cols, by_row) in enumerate(specs):
            table, pend, limit = tables[t], pending[t], limits[t]
            n_dst, n_src = (rows, cols) if by_row else (cols, rows)

            def rest(d, at, table=table, pend=pend, limit=limit, n_src=n_src):
                first = pend[d]
                table[at] = first
                table[limit + at] = n_src * 4096
                table[2 * limit + at] = d
                return at + (first >= 0).astype(jnp.int32)

            at = lax.fori_loop(0, n_dst, rest, counts[t])
            for u in range(PAIR_UNROLL):
                table[at + u] = n_src * 4096
                table[limit + at + u] = n_src * 4096
                table[2 * limit + at + u] = n_dst
            table[3 * limit] = (at + (PAIR_UNROLL - 1)) >> PAIR_SHIFT

    smem = pl.BlockSpec(memory_space=pltpu.SMEM)
    return pl.pallas_call(
        body,
        in_specs=[smem] * n + [pl.BlockSpec(memory_space=pltpu.VMEM)] * len(weights),
        out_specs=[smem] * n,
        out_shape=[jax.ShapeDtypeStruct((3 * limit + 1,), jnp.int32) for limit in limits],
        scratch_shapes=[pltpu.SMEM(((rows if by_row else cols) + 1,), jnp.int32) for rows, cols, by_row in specs],
        compiler_params=pltpu.CompilerParams(vmem_limit_bytes=1024 * 1024),
        name="pair_tables",
    )(*[job[0] for job in jobs], *weights)


PAIR_SHIFT = 4
PAIR_UNROLL = 1 << PAIR_SHIFT


def pair_limit(cap, n_dst):
    return (cap + n_dst) // 2 + PAIR_UNROLL + 1


def block_product(pieces, in_rows, blocks, table, n_dst, out_lengths, out_rows, transposed):
    cap, width = blocks.shape[0], blocks.shape[1]
    n_src = pieces[0].shape[1] // width
    tokens = sum(piece.shape[0] for piece in pieces)
    limit = pair_limit(cap, n_dst)
    dims = (((1,), (1 if transposed else 0,)), ((), ()))
    zero_rows = jnp.zeros((1,), jnp.int32)
    in_arr = zero_rows if in_rows is None else in_rows
    out_arr = zero_rows if out_rows is None else out_rows
    n_in, n_out = len(pieces), len(out_lengths)

    def body(table_s, in_s, out_s, *refs):
        piece_refs = refs[:n_in]
        w_ref = refs[n_in]
        out_refs = refs[n_in + 1 : n_in + 1 + n_out]
        xs, acc = refs[n_in + 1 + n_out :]
        if in_rows is None:
            place = lambda i, length: i * length
        else:
            place = lambda i, length: pl.multiple_of(in_s[i], length)
        load_pieces(piece_refs, place, xs, width)
        xs[n_src] = jnp.zeros((tokens, width), xs.dtype)
        acc[...] = jnp.zeros_like(acc)

        def some(g, carry):
            terms = []
            for u in range(PAIR_UNROLL):
                n = g * PAIR_UNROLL + u
                one, two = table_s[n], table_s[limit + n]
                left = jnp.concatenate([xs[one >> 12], xs[two >> 12]], axis=1)
                right = jnp.concatenate(
                    [w_ref[one & 4095], w_ref[two & 4095]], axis=1 if transposed else 0
                )
                terms.append(lax.dot_general(left, right, dims, preferred_element_type=jnp.float32))
            for u in range(PAIR_UNROLL):
                acc[table_s[2 * limit + g * PAIR_UNROLL + u]] += terms[u]
            return carry

        lax.fori_loop(0, table_s[3 * limit], some, 0)
        at = 0
        for ref in out_refs:
            lead = ref.shape[:-2]
            length = ref.shape[-2]
            for j in range(lead[0] if lead else 1):
                start = at * length if out_rows is None else pl.multiple_of(out_s[at], length)
                at += 1
                for b in range(n_dst):
                    val = acc[b, pl.ds(start, length), :].astype(jnp.bfloat16)
                    if lead:
                        ref[j, :, b * width : (b + 1) * width] = val
                    else:
                        ref[:, b * width : (b + 1) * width] = val

    smem = pl.BlockSpec(memory_space=pltpu.SMEM)
    vmem = pl.BlockSpec(memory_space=pltpu.VMEM)
    out_shapes = [shape + (n_dst * width,) for shape in out_lengths]
    return pl.pallas_call(
        body,
        in_specs=[smem] * 3 + [vmem] * (n_in + 1),
        out_specs=[vmem] * n_out,
        scratch_shapes=[
            pltpu.VMEM((n_src + 1, tokens, width), jnp.bfloat16),
            pltpu.VMEM((n_dst + 1, tokens, width), jnp.float32),
        ],
        out_shape=[jax.ShapeDtypeStruct(shape, jnp.bfloat16) for shape in out_shapes],
        compiler_params=pltpu.CompilerParams(vmem_limit_bytes=8 * 1024 * 1024),
        cost_estimate=pl.CostEstimate(
            flops=2 * cap * tokens * width * width,
            bytes_accessed=cap * width * width * 2 + tokens * width * 2 * (n_src + n_dst),
            transcendentals=0,
        ),
        name="block_product",
    )(table, in_arr, out_arr, *pieces, blocks)


def block_grads(left, left_rows, right, right_rows, rows, cols, cap):
    width = 128
    n_left, n_right = left[0].shape[1] // width, right[0].shape[1] // width
    tokens = sum(piece.shape[0] for piece in left)
    chunk = largest_divisor(cap, 48)
    unroll = chunk
    steps = cap // chunk
    n_l, n_r = len(left), len(right)
    dims = (((1,), (0,)), ((), ()))
    zero_rows = jnp.zeros((1,), jnp.int32)
    left_arr = zero_rows if left_rows is None else left_rows
    right_arr = zero_rows if right_rows is None else right_rows

    def body(row_s, col_s, left_s, right_s, *refs):
        l_refs = refs[:n_l]
        r_refs = refs[n_l : n_l + n_r]
        out = refs[n_l + n_r]
        ls, lt, rs = refs[n_l + n_r + 1 :]
        step = pl.program_id(0)

        @pl.when(step == 0)
        def _():
            def place(given, table):
                if given is None:
                    return lambda i, length: i * length
                return lambda i, length: pl.multiple_of(table[i], length)

            load_pieces(l_refs, place(left_rows, left_s), ls, width)
            load_pieces(r_refs, place(right_rows, right_s), rs, width)
            rs[n_right] = jnp.zeros((tokens, width), rs.dtype)
            for b in range(n_left):
                lt[b] = ls[b].T

        def some(g, carry):
            base = g * unroll
            for u in range(unroll):
                k = step * chunk + base + u
                out[base + u] = lax.dot_general(
                    lt[row_s[k]], rs[col_s[k]], dims, preferred_element_type=jnp.float32
                )
            return carry

        lax.fori_loop(0, chunk // unroll, some, 0)

    whole = lambda shape: pl.BlockSpec(shape, lambda i, *s: (0,) * len(shape))
    return pl.pallas_call(
        body,
        grid_spec=pltpu.PrefetchScalarGridSpec(
            num_scalar_prefetch=4,
            grid=(steps,),
            in_specs=[whole(piece.shape) for piece in left] + [whole(piece.shape) for piece in right],
            out_specs=pl.BlockSpec((chunk, width, width), lambda i, *s: (i, 0, 0)),
            scratch_shapes=[
                pltpu.VMEM((n_left, tokens, width), jnp.bfloat16),
                pltpu.VMEM((n_left, width, tokens), jnp.bfloat16),
                pltpu.VMEM((n_right + 1, tokens, width), jnp.bfloat16),
            ],
        ),
        out_shape=jax.ShapeDtypeStruct((cap, width, width), jnp.float32),
        compiler_params=pltpu.CompilerParams(
            dimension_semantics=("arbitrary",), vmem_limit_bytes=16 * 1024 * 1024
        ),
        cost_estimate=pl.CostEstimate(
            flops=2 * cap * tokens * width * width,
            bytes_accessed=cap * width * width * 4 + tokens * width * 2 * (n_left + n_right),
            transcendentals=0,
        ),
        name="block_grads",
    )(rows, cols, left_arr, right_arr, *left, *right)


def on_device(tokens, in_blocks, in_slots, out_blocks, out_slots, cotangent, *, hidden_total):
    w_in = in_blocks.reshape(in_blocks.shape[2:])
    w_out = out_blocks.reshape(out_blocks.shape[2:])
    slots_in = in_slots.reshape(-1)
    slots_out = out_slots.reshape(-1)
    width = w_in.shape[-1]
    cap = w_in.shape[0]
    tensor_count = lax.axis_size("tensor")
    seq_count = lax.axis_size("seq")
    feat_blocks = tokens.shape[1] // width
    hid_blocks = hidden_total // tensor_count // width
    tensor_rows = tokens.shape[0]
    token_count = tensor_rows * tensor_count
    seq_rows = token_count // seq_count
    far_t, far_s = tensor_count // 2, seq_count // 2

    def near_move(v, axis, count):
        return lax.ppermute(v, axis, [(i, i ^ 1) for i in range(count)])

    def far_move(v, axis, count, shift):
        half = count // 2
        pairs = [(o * 2 + c, ((o + shift) % half) * 2 + c) for o in range(half) for c in range(2)]
        return lax.ppermute(v, axis, pairs)

    me = lax.axis_index("seq")
    shifts = jnp.arange(seq_count, dtype=jnp.int32)
    far_of = (me // 2 + far_s - shifts // 2) % far_s
    seq_part = (far_of * 2 + (me % 2 + shifts % 2) % 2) * seq_rows
    near_order = jnp.concatenate([seq_part[0::2], seq_part[1::2]])

    def positions(slot_list, cols):
        filled = slot_list >= 0
        safe = jnp.where(filled, slot_list, 0)
        return safe // cols, jnp.where(filled, safe % cols, cols)

    in_row, in_col = positions(slots_in, hid_blocks)
    out_row, out_col = positions(slots_out, feat_blocks)

    def gather_far(own):
        return [own] + [far_move(own, "tensor", tensor_count, k) for k in range(1, far_t)]

    def gather_near(far):
        pieces = []
        for piece in far:
            pieces += [piece, near_move(piece, "tensor", tensor_count)]
        return pieces

    def send_near(terms):
        order = list(range(1, far_t)) + [0]
        got = {k: near_move(terms[2 * k + 1], "tensor", tensor_count) for k in order}
        return [got[k] for k in range(far_t)]

    def pair_out(terms, got):
        pair = [terms[2 * k].astype(jnp.float32) + got[k].astype(jnp.float32) for k in range(far_t)]
        return pair[0], [value.astype(jnp.bfloat16) for value in pair[1:]]

    def total_out(own, pairs):
        moved = [far_move(pairs[k - 1], "tensor", tensor_count, far_t - k) for k in range(1, far_t)]
        total = own
        for value in moved:
            total = total + value.astype(jnp.float32)
        return total.astype(jnp.bfloat16)

    def pair_hidden(keep, send):
        got = near_move(send, "seq", seq_count)
        pair = [keep[k].astype(jnp.float32) + got[k].astype(jnp.float32) for k in range(far_s)]
        return pair[0], [value.astype(jnp.bfloat16) for value in pair[1:]]

    def total_hidden(own, pairs, *earlier):
        moved = [far_move(pairs[k - 1], "seq", seq_count, far_s - k) for k in range(1, far_s)]
        total = own
        for value in moved:
            total = total + after(value, *earlier).astype(jnp.float32)
        return total

    def spread_far(own):
        return [own] + [far_move(own, "seq", seq_count, k) for k in range(1, far_s)]

    def spread_near(far):
        pieces = []
        for piece in far:
            pieces += [piece, near_move(piece, "seq", seq_count)]
        return pieces

    hidden_lengths = [(far_s, seq_rows)] * 2
    token_lengths = [(tensor_rows,)] * tensor_count

    tok_far = gather_far(tokens)
    (in_by_col,) = pair_tables([(slots_in, feat_blocks, hid_blocks, False)], [w_in])
    cot_far = gather_far(after(cotangent, tok_far[1:]))
    tok = gather_near(tok_far)
    cot = gather_near(cot_far)
    later_in, later_out = after((slots_in, slots_out), tok_far[1:])
    out_by_row, out_by_col, in_by_row = pair_tables(
        [
            (later_out, hid_blocks, feat_blocks, True),
            (later_out, hid_blocks, feat_blocks, False),
            (later_in, feat_blocks, hid_blocks, True),
        ],
        [w_out],
    )
    keep_h, send_h = block_product(
        tok, None, w_in, in_by_col, hid_blocks, hidden_lengths, near_order, False
    )
    own_h, pairs_h = pair_hidden(keep_h, send_h)
    keep_g, send_g = block_product(
        after(cot, pairs_h), None, w_out, out_by_row, hid_blocks, hidden_lengths, near_order, True
    )
    hidden = total_hidden(own_h, pairs_h)
    own_act = gelu_value(hidden).astype(jnp.bfloat16)
    act_far = spread_far(own_act)
    activated = spread_near(act_far)
    own_g, pairs_g = pair_hidden(keep_g, send_g)
    grad_act = total_hidden(own_g, pairs_g, own_act)
    own_gh = (grad_act * gelu_slope(hidden)).astype(jnp.bfloat16)
    gh_far = spread_far(own_gh)
    grad_hidden = spread_near(gh_far)

    terms_o = block_product(
        after(activated, own_gh), seq_part, w_out, out_by_col, feat_blocks, token_lengths, None, False
    )
    got_o = send_near(terms_o)
    terms_t = block_product(
        after(grad_hidden, terms_o), seq_part, w_in, in_by_row, feat_blocks, token_lengths, None, True
    )
    got_t = send_near(terms_t)
    own_o, pairs_o = pair_out(terms_o, after(got_o, terms_t))
    grad_out = block_grads(after(activated, pairs_o), seq_part, cot, None, out_row, out_col, cap)
    own_t, pairs_t = pair_out(terms_t, after(got_t, grad_out))
    grad_in = block_grads(tok, None, after(grad_hidden, pairs_t), seq_part, in_row, in_col, cap)
    output = total_out(own_o, pairs_o)
    grad_tokens = total_out(own_t, pairs_t)
    return (
        output,
        grad_tokens,
        grad_in.reshape(in_blocks.shape),
        grad_out.reshape(out_blocks.shape),
    )


HIDDEN_TOTAL = 24576


def solution(mesh):
    def program(*args):
        return on_device(*args, hidden_total=HIDDEN_TOTAL)

    return jax.shard_map(
        program,
        mesh=mesh,
        in_specs=(
            P("tensor", "seq"),
            P("seq", "tensor", None, None, None),
            P("seq", "tensor", None),
            P("tensor", "seq", None, None, None),
            P("tensor", "seq", None),
            P("tensor", "seq"),
        ),
        out_specs=(
            P("tensor", "seq"),
            P("tensor", "seq"),
            P("seq", "tensor", None, None, None),
            P("tensor", "seq", None, None, None),
        ),
        check_vma=False,
    )
```

```python
import jax
import jax.numpy as jnp
from jax import lax
from jax.experimental import pallas as pl
from jax.experimental.pallas import tpu as pltpu
from jax.sharding import PartitionSpec as P


GELU_SCALE = 0.7978845608028654
GELU_CUBE = 0.044715


def gelu_value(values):
    return (
        0.5
        * values
        * (1.0 + jnp.tanh(GELU_SCALE * (values + GELU_CUBE * values * values * values)))
    )


def gelu_slope(values):
    tangent = jnp.tanh(GELU_SCALE * (values + GELU_CUBE * values * values * values))
    return 0.5 * (1.0 + tangent) + 0.5 * values * (1.0 - tangent * tangent) * GELU_SCALE * (
        1.0 + 3.0 * GELU_CUBE * values * values
    )


def after(values, *earlier):
    return lax.optimization_barrier((values, earlier))[0]


def largest_divisor(number, limit):
    return max(d for d in range(1, limit + 1) if number % d == 0)


def load_pieces(piece_refs, offsets, store, width):
    for i, piece in enumerate(piece_refs):
        length = piece.shape[0]
        start = offsets(i, length)
        for b in range(piece.shape[1] // width):
            store[b, pl.ds(start, length), :] = piece[:, b * width : (b + 1) * width]


def pair_tables(jobs, weights=()):
    cap = jobs[0][0].shape[0]
    specs = [job[1:] for job in jobs]
    n, m = len(jobs), len(weights)
    limits = [pair_limit(cap, rows if by_row else cols) for rows, cols, by_row in specs]

    def body(*refs):
        slot_refs, far, tables, near = refs[:n], refs[n : n + m], refs[n + m : 2 * n + m], refs[2 * n + m : 2 * n + 2 * m]
        pending, sems = refs[2 * n + 2 * m : 3 * n + 2 * m], refs[3 * n + 2 * m :]
        copies = [pltpu.make_async_copy(*copy) for copy in zip(far, near, sems)]
        for copy in copies:
            copy.start()
        for (rows, cols, by_row), pend in zip(specs, pending):

            def clear(i, carry, pend=pend):
                pend[i] = -1
                return carry

            lax.fori_loop(0, (rows if by_row else cols) + 1, clear, 0)

        step = largest_divisor(cap, 8)

        def some(g, counts):
            counts = list(counts)
            for t, (rows, cols, by_row) in enumerate(specs):
                table, pend, limit = tables[t], pending[t], limits[t]
                entries = []
                for u in range(step):
                    k = g * step + u
                    pos = slot_refs[t][k]
                    filled = pos >= 0
                    safe = jnp.maximum(pos, 0)
                    row = (safe * (-(-65536 // cols))) >> 16
                    col = safe - row * cols
                    key, src, end = (row, col, rows) if by_row else (col, row, cols)
                    entries.append((jnp.where(filled, key, end), k + src * 4096, filled))
                for key, word, filled in entries:
                    first = pend[key]
                    at = counts[t]
                    table[at] = first
                    table[limit + at] = word
                    table[2 * limit + at] = key
                    pend[key] = jnp.where(first >= 0, -1, word)
                    counts[t] = at + jnp.logical_and(first >= 0, filled).astype(jnp.int32)
            return tuple(counts)

        counts = lax.fori_loop(0, cap // step, some, (jnp.int32(0),) * n)
        for t, (rows, cols, by_row) in enumerate(specs):
            table, pend, limit = tables[t], pending[t], limits[t]
            n_dst, n_src = (rows, cols) if by_row else (cols, rows)

            def rest(d, at, table=table, pend=pend, limit=limit, n_src=n_src):
                first = pend[d]
                table[at] = first
                table[limit + at] = n_src * 4096
                table[2 * limit + at] = d
                return at + (first >= 0).astype(jnp.int32)

            at = lax.fori_loop(0, n_dst, rest, counts[t])
            for u in range(PAIR_UNROLL):
                table[at + u] = n_src * 4096
                table[limit + at + u] = n_src * 4096
                table[2 * limit + at + u] = n_dst
            table[3 * limit] = counts[t]
            table[3 * limit + 1] = (at + (PAIR_UNROLL - 1)) >> PAIR_SHIFT
        for copy in copies:
            copy.wait()

    smem = pl.BlockSpec(memory_space=pltpu.SMEM)
    return pl.pallas_call(
        body,
        in_specs=[smem] * n + [pl.BlockSpec(memory_space=pltpu.HBM)] * m,
        out_specs=[smem] * n + [pl.BlockSpec(memory_space=pltpu.VMEM)] * m,
        out_shape=[jax.ShapeDtypeStruct((3 * limit + 2,), jnp.int32) for limit in limits]
        + [jax.ShapeDtypeStruct(weight.shape, weight.dtype) for weight in weights],
        scratch_shapes=[pltpu.SMEM(((rows if by_row else cols) + 1,), jnp.int32) for rows, cols, by_row in specs]
        + [pltpu.SemaphoreType.DMA] * m,
        compiler_params=pltpu.CompilerParams(vmem_limit_bytes=1024 * 1024),
        name="pair_tables",
    )(*[job[0] for job in jobs], *weights)


PAIR_SHIFT = 4
PAIR_UNROLL = 1 << PAIR_SHIFT


def pair_limit(cap, n_dst):
    return (cap + n_dst) // 2 + PAIR_UNROLL + 1


def block_product(pieces, in_rows, blocks, table, n_dst, out_lengths, out_rows, transposed, stage=()):
    cap, width = blocks.shape[0], blocks.shape[1]
    n_src = pieces[0].shape[1] // width
    tokens = sum(piece.shape[0] for piece in pieces)
    limit = pair_limit(cap, n_dst)
    dims = (((1,), (1 if transposed else 0,)), ((), ()))
    zero_rows = jnp.zeros((1,), jnp.int32)
    in_arr = zero_rows if in_rows is None else in_rows
    static_out = isinstance(out_rows, list)
    out_arr = zero_rows if static_out else out_rows
    n_in, n_out, m = len(pieces), len(out_lengths), len(stage)

    def body(table_s, in_s, out_s, *refs):
        piece_refs = refs[:n_in]
        w_ref = refs[n_in]
        far = refs[n_in + 1 : n_in + 1 + m]
        refs = refs[n_in + 1 + m :]
        out_refs, near = refs[:n_out], refs[n_out : n_out + m]
        xs, acc = refs[n_out + m : n_out + m + 2]
        copies = [pltpu.make_async_copy(*copy) for copy in zip(far, near, refs[n_out + m + 2 :])]
        for copy in copies:
            copy.start()
        if in_rows is None:
            place = lambda i, length: i * length
        else:
            place = lambda i, length: pl.multiple_of(in_s[i], length)
        load_pieces(piece_refs, place, xs, width)
        xs[n_src] = jnp.zeros((tokens, width), xs.dtype)
        acc[...] = jnp.zeros_like(acc)

        def some(g, carry):
            terms = []
            for u in range(PAIR_UNROLL):
                n = g * PAIR_UNROLL + u
                one, two = table_s[n], table_s[limit + n]
                left = jnp.concatenate([xs[one >> 12], xs[two >> 12]], axis=1)
                right = jnp.concatenate(
                    [w_ref[one & 4095], w_ref[two & 4095]], axis=1 if transposed else 0
                )
                terms.append(lax.dot_general(left, right, dims, preferred_element_type=jnp.float32))
            for u in range(PAIR_UNROLL):
                acc[table_s[2 * limit + g * PAIR_UNROLL + u]] += terms[u]
            return carry

        lax.fori_loop(0, table_s[3 * limit + 1], some, 0)
        at = 0
        for ref in out_refs:
            lead = ref.shape[:-2]
            length = ref.shape[-2]
            for j in range(lead[0] if lead else 1):
                start = out_rows[at] if static_out else pl.multiple_of(out_s[at], length)
                at += 1
                for b in range(n_dst):
                    val = acc[b, pl.ds(start, length), :].astype(jnp.bfloat16)
                    if lead:
                        ref[j, :, b * width : (b + 1) * width] = val
                    else:
                        ref[:, b * width : (b + 1) * width] = val
        for copy in copies:
            copy.wait()

    smem = pl.BlockSpec(memory_space=pltpu.SMEM)
    vmem = pl.BlockSpec(memory_space=pltpu.VMEM)
    out_shapes = [shape + (n_dst * width,) for shape in out_lengths]
    return pl.pallas_call(
        body,
        in_specs=[smem] * 3 + [vmem] * (n_in + 1) + [pl.BlockSpec(memory_space=pltpu.HBM)] * m,
        out_specs=[vmem] * (n_out + m),
        scratch_shapes=[
            pltpu.VMEM((n_src + 1, tokens, width), jnp.bfloat16),
            pltpu.VMEM((n_dst + 1, tokens, width), jnp.float32),
        ]
        + [pltpu.SemaphoreType.DMA] * m,
        out_shape=[jax.ShapeDtypeStruct(shape, jnp.bfloat16) for shape in out_shapes]
        + [jax.ShapeDtypeStruct(array.shape, array.dtype) for array in stage],
        compiler_params=pltpu.CompilerParams(vmem_limit_bytes=8 * 1024 * 1024),
        cost_estimate=pl.CostEstimate(
            flops=2 * cap * tokens * width * width,
            bytes_accessed=cap * width * width * 2 + tokens * width * 2 * (n_src + n_dst),
            transcendentals=0,
        ),
        name="block_product",
    )(table, in_arr, out_arr, *pieces, blocks, *stage)


def block_grads(left, left_rows, right, right_rows, rows, cols, cap):
    width = 128
    n_left, n_right = left[0].shape[1] // width, right[0].shape[1] // width
    tokens = sum(piece.shape[0] for piece in left)
    chunk = largest_divisor(cap, 48)
    unroll = chunk
    steps = cap // chunk
    n_l, n_r = len(left), len(right)
    dims = (((1,), (0,)), ((), ()))
    zero_rows = jnp.zeros((1,), jnp.int32)
    left_arr = zero_rows if left_rows is None else left_rows
    right_arr = zero_rows if right_rows is None else right_rows

    def body(row_s, col_s, left_s, right_s, *refs):
        l_refs = refs[:n_l]
        r_refs = refs[n_l : n_l + n_r]
        out = refs[n_l + n_r]
        ls, lt, rs = refs[n_l + n_r + 1 :]
        step = pl.program_id(0)

        @pl.when(step == 0)
        def _():
            def place(given, table):
                if given is None:
                    return lambda i, length: i * length
                return lambda i, length: pl.multiple_of(table[i], length)

            load_pieces(l_refs, place(left_rows, left_s), ls, width)
            load_pieces(r_refs, place(right_rows, right_s), rs, width)
            rs[n_right] = jnp.zeros((tokens, width), rs.dtype)
            for b in range(n_left):
                lt[b] = ls[b].T

        def some(g, carry):
            base = g * unroll
            for u in range(unroll):
                k = step * chunk + base + u
                out[base + u] = lax.dot_general(
                    lt[row_s[k]], rs[col_s[k]], dims, preferred_element_type=jnp.float32
                )
            return carry

        lax.fori_loop(0, chunk // unroll, some, 0)

    whole = lambda shape: pl.BlockSpec(shape, lambda i, *s: (0,) * len(shape))
    return pl.pallas_call(
        body,
        grid_spec=pltpu.PrefetchScalarGridSpec(
            num_scalar_prefetch=4,
            grid=(steps,),
            in_specs=[whole(piece.shape) for piece in left] + [whole(piece.shape) for piece in right],
            out_specs=pl.BlockSpec((chunk, width, width), lambda i, *s: (i, 0, 0)),
            scratch_shapes=[
                pltpu.VMEM((n_left, tokens, width), jnp.bfloat16),
                pltpu.VMEM((n_left, width, tokens), jnp.bfloat16),
                pltpu.VMEM((n_right + 1, tokens, width), jnp.bfloat16),
            ],
        ),
        out_shape=jax.ShapeDtypeStruct((cap, width, width), jnp.float32),
        compiler_params=pltpu.CompilerParams(
            dimension_semantics=("arbitrary",), vmem_limit_bytes=16 * 1024 * 1024
        ),
        cost_estimate=pl.CostEstimate(
            flops=2 * cap * tokens * width * width,
            bytes_accessed=cap * width * width * 4 + tokens * width * 2 * (n_left + n_right),
            transcendentals=0,
        ),
        name="block_grads",
    )(rows, cols, left_arr, right_arr, *left, *right)


def on_device(tokens, in_blocks, in_slots, out_blocks, out_slots, cotangent, *, hidden_total):
    w_in = in_blocks.reshape(in_blocks.shape[2:])
    w_out = out_blocks.reshape(out_blocks.shape[2:])
    w_in = pltpu.with_memory_space_constraint(w_in, pltpu.HBM)
    w_out = pltpu.with_memory_space_constraint(w_out, pltpu.HBM)
    slots_in = in_slots.reshape(-1)
    slots_out = out_slots.reshape(-1)
    width = w_in.shape[-1]
    cap = w_in.shape[0]
    tensor_count = lax.axis_size("tensor")
    seq_count = lax.axis_size("seq")
    feat_blocks = tokens.shape[1] // width
    hid_blocks = hidden_total // tensor_count // width
    tensor_rows = tokens.shape[0]
    token_count = tensor_rows * tensor_count
    seq_rows = token_count // seq_count
    far_t, far_s = tensor_count // 2, seq_count // 2

    def near_move(v, axis, count):
        return lax.ppermute(v, axis, [(i, i ^ 1) for i in range(count)])

    def far_move(v, axis, count, shift):
        half = count // 2
        pairs = [(o * 2 + c, ((o + shift) % half) * 2 + c) for o in range(half) for c in range(2)]
        return lax.ppermute(v, axis, pairs)

    me = lax.axis_index("seq")
    shifts = jnp.arange(seq_count, dtype=jnp.int32)
    far_of = (me // 2 + far_s - shifts // 2) % far_s
    seq_part = (far_of * 2 + (me % 2 + shifts % 2) % 2) * seq_rows
    near_order = jnp.concatenate([seq_part[0::2], seq_part[1::2]])

    def positions(slot_list, cols):
        filled = slot_list >= 0
        safe = jnp.where(filled, slot_list, 0)
        return safe // cols, jnp.where(filled, safe % cols, cols)

    in_row, in_col = positions(slots_in, hid_blocks)
    out_row, out_col = positions(slots_out, feat_blocks)

    def gather_far(own):
        return [own] + [far_move(own, "tensor", tensor_count, k) for k in range(1, far_t)]

    def gather_near(far):
        pieces = []
        for piece in far:
            pieces += [piece, near_move(piece, "tensor", tensor_count)]
        return pieces

    def pair_out(keep, got):
        pair = [keep[k].astype(jnp.float32) + got[k].astype(jnp.float32) for k in range(far_t)]
        return pair[0], [value.astype(jnp.bfloat16) for value in pair[1:]]

    def total_out(own, pairs):
        moved = [far_move(pairs[k - 1], "tensor", tensor_count, far_t - k) for k in range(1, far_t)]
        total = own
        for value in moved:
            total = total + value.astype(jnp.float32)
        return total.astype(jnp.bfloat16)

    def pair_hidden(keep, send):
        got = near_move(send, "seq", seq_count)
        pair = [keep[k].astype(jnp.float32) + got[k].astype(jnp.float32) for k in range(far_s)]
        return pair[0], [value.astype(jnp.bfloat16) for value in pair[1:]]

    def total_hidden(own, pairs, *earlier):
        moved = [far_move(pairs[k - 1], "seq", seq_count, far_s - k) for k in range(1, far_s)]
        total = own
        for value in moved:
            total = total + after(value, *earlier).astype(jnp.float32)
        return total

    def spread_far(own):
        return [own] + [far_move(own, "seq", seq_count, k) for k in range(1, far_s)]

    def spread_near(far):
        pieces = []
        for piece in far:
            pieces += [piece, near_move(piece, "seq", seq_count)]
        return pieces

    hidden_lengths = [(far_s, seq_rows)] * 2
    token_lengths = [(far_t, tensor_rows)] * 2
    token_rows = [(2 * k + flip) * tensor_rows for flip in range(2) for k in range(far_t)]

    tok_far = gather_far(tokens)
    in_by_col, w_in_near = pair_tables([(slots_in, feat_blocks, hid_blocks, False)], [w_in])
    cot_far = gather_far(cotangent)
    tok = gather_near(tok_far)
    cot = gather_near(cot_far)
    out_by_row, w_out_near = pair_tables(
        [(after(slots_out, tok_far[1:]), hid_blocks, feat_blocks, True)], [w_out]
    )
    keep_h, send_h = block_product(
        after(tok, out_by_row), None, w_in_near, in_by_col, hid_blocks, hidden_lengths, near_order, False
    )
    own_h, pairs_h = pair_hidden(keep_h, send_h)
    keep_g, send_g = block_product(
        after(cot, pairs_h), None, w_out_near, out_by_row, hid_blocks, hidden_lengths, near_order, True
    )
    later_in, later_out = after((slots_in, slots_out), keep_g)
    out_by_col, in_by_row = pair_tables(
        [(later_out, hid_blocks, feat_blocks, False), (later_in, feat_blocks, hid_blocks, True)]
    )
    hidden = total_hidden(own_h, pairs_h)
    own_act = gelu_value(hidden).astype(jnp.bfloat16)
    act_far = spread_far(own_act)
    activated = spread_near(act_far)
    own_g, pairs_g = pair_hidden(keep_g, send_g)
    grad_act = total_hidden(own_g, pairs_g, own_act)
    own_gh = (grad_act * gelu_slope(hidden)).astype(jnp.bfloat16)
    gh_far = spread_far(own_gh)
    grad_hidden = spread_near(gh_far)

    keep_o, send_o, w_in_near = block_product(
        after(activated, own_gh),
        seq_part,
        w_out_near,
        out_by_col,
        feat_blocks,
        token_lengths,
        token_rows,
        False,
        [w_in],
    )
    got_o = near_move(send_o, "tensor", tensor_count)
    keep_t, send_t = block_product(
        after(grad_hidden, keep_o), seq_part, w_in_near, in_by_row, feat_blocks, token_lengths, token_rows, True
    )
    got_t = near_move(send_t, "tensor", tensor_count)
    own_o, pairs_o = pair_out(keep_o, after(got_o, keep_t))
    grad_out = block_grads(after(activated, pairs_o), seq_part, cot, None, out_row, out_col, cap)
    own_t, pairs_t = pair_out(keep_t, after(got_t, grad_out))
    grad_in = block_grads(tok, None, after(grad_hidden, pairs_t), seq_part, in_row, in_col, cap)
    output = total_out(own_o, pairs_o)
    grad_tokens = total_out(own_t, pairs_t)
    return (
        output,
        grad_tokens,
        grad_in.reshape(in_blocks.shape),
        grad_out.reshape(out_blocks.shape),
    )


HIDDEN_TOTAL = 24576


def solution(mesh):
    def program(*args):
        return on_device(*args, hidden_total=HIDDEN_TOTAL)

    return jax.shard_map(
        program,
        mesh=mesh,
        in_specs=(
            P("tensor", "seq"),
            P("seq", "tensor", None, None, None),
            P("seq", "tensor", None),
            P("tensor", "seq", None, None, None),
            P("tensor", "seq", None),
            P("tensor", "seq"),
        ),
        out_specs=(
            P("tensor", "seq"),
            P("tensor", "seq"),
            P("seq", "tensor", None, None, None),
            P("tensor", "seq", None, None, None),
        ),
        check_vma=False,
    )
```

```python
import jax
import jax.numpy as jnp
from jax import lax
from jax.experimental import pallas as pl
from jax.experimental.pallas import tpu as pltpu
from jax.sharding import PartitionSpec as P


GELU_SCALE = 0.7978845608028654
GELU_CUBE = 0.044715


def gelu_value(values):
    return (
        0.5
        * values
        * (1.0 + jnp.tanh(GELU_SCALE * (values + GELU_CUBE * values * values * values)))
    )


def gelu_slope(values):
    tangent = jnp.tanh(GELU_SCALE * (values + GELU_CUBE * values * values * values))
    return 0.5 * (1.0 + tangent) + 0.5 * values * (1.0 - tangent * tangent) * GELU_SCALE * (
        1.0 + 3.0 * GELU_CUBE * values * values
    )


def after(values, *earlier):
    return lax.optimization_barrier((values, earlier))[0]


def largest_divisor(number, limit):
    return max(d for d in range(1, limit + 1) if number % d == 0)


def load_pieces(piece_refs, offsets, store, width):
    for i, piece in enumerate(piece_refs):
        length = piece.shape[0]
        start = offsets(i, length)
        for b in range(piece.shape[1] // width):
            store[b, pl.ds(start, length), :] = piece[:, b * width : (b + 1) * width]


def pair_tables(jobs, weights=()):
    cap = jobs[0][0].shape[-1]
    specs = [job[1:] for job in jobs]
    n, m = len(jobs), len(weights)
    limits = [pair_limit(cap, rows if by_row else cols) for rows, cols, by_row in specs]

    def body(*refs):
        slot_refs, far, tables, near = refs[:n], refs[n : n + m], refs[n + m : 2 * n + m], refs[2 * n + m : 2 * n + 2 * m]
        pending, sems = refs[2 * n + 2 * m : 3 * n + 2 * m], refs[3 * n + 2 * m :]
        copies = [pltpu.make_async_copy(*copy) for copy in zip(far, near, sems)]
        for copy in copies:
            copy.start()
        for (rows, cols, by_row), pend in zip(specs, pending):

            def clear(i, carry, pend=pend):
                pend[i] = -1
                return carry

            lax.fori_loop(0, (rows if by_row else cols) + 1, clear, 0)

        step = largest_divisor(cap, 8)

        def some(g, counts):
            counts = list(counts)
            for t, (rows, cols, by_row) in enumerate(specs):
                table, pend, limit = tables[t], pending[t], limits[t]
                entries = []
                for u in range(step):
                    k = g * step + u
                    pos = slot_refs[t][0, 0, k]
                    filled = pos >= 0
                    safe = jnp.maximum(pos, 0)
                    row = (safe * (-(-65536 // cols))) >> 16
                    col = safe - row * cols
                    key, src, end = (row, col, rows) if by_row else (col, row, cols)
                    entries.append((jnp.where(filled, key, end), k + src * 4096, filled))
                for key, word, filled in entries:
                    first = pend[key]
                    at = counts[t]
                    table[at] = first
                    table[limit + at] = word
                    table[2 * limit + at] = key
                    pend[key] = jnp.where(first >= 0, -1, word)
                    counts[t] = at + jnp.logical_and(first >= 0, filled).astype(jnp.int32)
            return tuple(counts)

        counts = lax.fori_loop(0, cap // step, some, (jnp.int32(0),) * n)
        for t, (rows, cols, by_row) in enumerate(specs):
            table, pend, limit = tables[t], pending[t], limits[t]
            n_dst, n_src = (rows, cols) if by_row else (cols, rows)

            def rest(d, at, table=table, pend=pend, limit=limit, n_src=n_src):
                first = pend[d]
                table[at] = first
                table[limit + at] = n_src * 4096
                table[2 * limit + at] = d
                return at + (first >= 0).astype(jnp.int32)

            at = lax.fori_loop(0, n_dst, rest, counts[t])
            for u in range(PAIR_UNROLL):
                table[at + u] = n_src * 4096
                table[limit + at + u] = n_src * 4096
                table[2 * limit + at + u] = n_dst
            table[3 * limit] = counts[t]
            table[3 * limit + 1] = (at + (PAIR_UNROLL - 1)) >> PAIR_SHIFT
        for copy in copies:
            copy.wait()

    smem = pl.BlockSpec(memory_space=pltpu.SMEM)
    return pl.pallas_call(
        body,
        in_specs=[smem] * n + [pl.BlockSpec(memory_space=pltpu.HBM)] * m,
        out_specs=[smem] * n + [pl.BlockSpec(memory_space=pltpu.VMEM)] * m,
        out_shape=[jax.ShapeDtypeStruct((3 * limit + 2,), jnp.int32) for limit in limits]
        + [jax.ShapeDtypeStruct(weight.shape, weight.dtype) for weight in weights],
        scratch_shapes=[pltpu.SMEM(((rows if by_row else cols) + 1,), jnp.int32) for rows, cols, by_row in specs]
        + [pltpu.SemaphoreType.DMA] * m,
        compiler_params=pltpu.CompilerParams(vmem_limit_bytes=1024 * 1024),
        name="pair_tables",
    )(*[job[0] for job in jobs], *weights)


PAIR_SHIFT = 4
PAIR_UNROLL = 1 << PAIR_SHIFT


def pair_limit(cap, n_dst):
    return (cap + n_dst) // 2 + PAIR_UNROLL + 1


def block_product(pieces, in_rows, blocks, table, n_dst, out_lengths, out_rows, transposed, stage=()):
    cap, width = blocks.shape[0], blocks.shape[1]
    n_src = pieces[0].shape[1] // width
    tokens = sum(piece.shape[0] for piece in pieces)
    limit = pair_limit(cap, n_dst)
    dims = (((1,), (1 if transposed else 0,)), ((), ()))
    zero_rows = jnp.zeros((1,), jnp.int32)
    in_arr = zero_rows if in_rows is None else in_rows
    static_out = isinstance(out_rows, list)
    out_arr = zero_rows if static_out else out_rows
    n_in, n_out, m = len(pieces), len(out_lengths), len(stage)

    def body(table_s, in_s, out_s, *refs):
        piece_refs = refs[:n_in]
        w_ref = refs[n_in]
        far = refs[n_in + 1 : n_in + 1 + m]
        refs = refs[n_in + 1 + m :]
        out_refs, near = refs[:n_out], refs[n_out : n_out + m]
        xs, acc = refs[n_out + m : n_out + m + 2]
        copies = [pltpu.make_async_copy(*copy) for copy in zip(far, near, refs[n_out + m + 2 :])]
        for copy in copies:
            copy.start()
        if in_rows is None:
            place = lambda i, length: i * length
        else:
            place = lambda i, length: pl.multiple_of(in_s[i], length)
        load_pieces(piece_refs, place, xs, width)
        xs[n_src] = jnp.zeros((tokens, width), xs.dtype)
        acc[...] = jnp.zeros_like(acc)

        def some(g, carry):
            terms = []
            for u in range(PAIR_UNROLL):
                n = g * PAIR_UNROLL + u
                one, two = table_s[n], table_s[limit + n]
                left = jnp.concatenate([xs[one >> 12], xs[two >> 12]], axis=1)
                right = jnp.concatenate(
                    [w_ref[one & 4095], w_ref[two & 4095]], axis=1 if transposed else 0
                )
                terms.append(lax.dot_general(left, right, dims, preferred_element_type=jnp.float32))
            for u in range(PAIR_UNROLL):
                acc[table_s[2 * limit + g * PAIR_UNROLL + u]] += terms[u]
            return carry

        lax.fori_loop(0, table_s[3 * limit + 1], some, 0)
        at = 0
        for ref in out_refs:
            lead = ref.shape[:-2]
            length = ref.shape[-2]
            for j in range(lead[0] if lead else 1):
                start = out_rows[at] if static_out else pl.multiple_of(out_s[at], length)
                at += 1
                for b in range(n_dst):
                    val = acc[b, pl.ds(start, length), :].astype(jnp.bfloat16)
                    if lead:
                        ref[j, :, b * width : (b + 1) * width] = val
                    else:
                        ref[:, b * width : (b + 1) * width] = val
        for copy in copies:
            copy.wait()

    smem = pl.BlockSpec(memory_space=pltpu.SMEM)
    vmem = pl.BlockSpec(memory_space=pltpu.VMEM)
    out_shapes = [shape + (n_dst * width,) for shape in out_lengths]
    return pl.pallas_call(
        body,
        in_specs=[smem] * 3 + [vmem] * (n_in + 1) + [pl.BlockSpec(memory_space=pltpu.HBM)] * m,
        out_specs=[vmem] * (n_out + m),
        scratch_shapes=[
            pltpu.VMEM((n_src + 1, tokens, width), jnp.bfloat16),
            pltpu.VMEM((n_dst + 1, tokens, width), jnp.float32),
        ]
        + [pltpu.SemaphoreType.DMA] * m,
        out_shape=[jax.ShapeDtypeStruct(shape, jnp.bfloat16) for shape in out_shapes]
        + [jax.ShapeDtypeStruct(array.shape, array.dtype) for array in stage],
        compiler_params=pltpu.CompilerParams(vmem_limit_bytes=8 * 1024 * 1024),
        cost_estimate=pl.CostEstimate(
            flops=2 * cap * tokens * width * width,
            bytes_accessed=cap * width * width * 2 + tokens * width * 2 * (n_src + n_dst),
            transcendentals=0,
        ),
        name="block_product",
    )(table, in_arr, out_arr, *pieces, blocks, *stage)


def block_grads(left, left_rows, right, right_rows, slots, part=0, parts=1, base=None):
    width, cap = 128, slots.shape[-1]
    n_left, n_right = left[0].shape[1] // width, right[0].shape[1] // width
    tokens = sum(piece.shape[0] for piece in left)
    chunk = largest_divisor(cap, 48)
    unroll = chunk
    steps = cap // chunk // parts
    skip = part * steps
    n_l, n_r = len(left), len(right)
    dims = (((1,), (0,)), ((), ()))
    zero_rows = jnp.zeros((1,), jnp.int32)
    left_arr = zero_rows if left_rows is None else left_rows
    right_arr = zero_rows if right_rows is None else right_rows

    def body(slot_s, left_s, right_s, *refs):
        l_refs = refs[:n_l]
        r_refs = refs[n_l : n_l + n_r]
        out, ls, lt, rs = refs[len(refs) - 4 :]
        step = pl.program_id(0)

        @pl.when(step == 0)
        def _():
            def place(given, table):
                if given is None:
                    return lambda i, length: i * length
                return lambda i, length: pl.multiple_of(table[i], length)

            load_pieces(l_refs, place(left_rows, left_s), ls, width)
            load_pieces(r_refs, place(right_rows, right_s), rs, width)
            rs[n_right] = jnp.zeros((tokens, width), rs.dtype)
            for b in range(n_left):
                lt[b] = ls[b].T

        def some(g, carry):
            at = g * unroll
            for u in range(unroll):
                k = (step + skip) * chunk + at + u
                pos = slot_s[0, 0, k]
                safe = jnp.maximum(pos, 0)
                row = (safe * (-(-65536 // n_right))) >> 16
                col = jnp.where(pos >= 0, safe - row * n_right, n_right)
                out[at + u] = lax.dot_general(
                    lt[row], rs[col], dims, preferred_element_type=jnp.float32
                )
            return carry

        lax.fori_loop(0, chunk // unroll, some, 0)

    extra = [] if base is None else [base]
    whole = lambda shape: pl.BlockSpec(shape, lambda i, *s: (0,) * len(shape))
    return pl.pallas_call(
        body,
        grid_spec=pltpu.PrefetchScalarGridSpec(
            num_scalar_prefetch=3,
            grid=(steps,),
            in_specs=[whole(piece.shape) for piece in left]
            + [whole(piece.shape) for piece in right]
            + [pl.BlockSpec(memory_space=pltpu.HBM)] * len(extra),
            out_specs=pl.BlockSpec((chunk, width, width), lambda i, *s: (i + skip, 0, 0)),
            scratch_shapes=[
                pltpu.VMEM((n_left, tokens, width), jnp.bfloat16),
                pltpu.VMEM((n_left, width, tokens), jnp.bfloat16),
                pltpu.VMEM((n_right + 1, tokens, width), jnp.bfloat16),
            ],
        ),
        out_shape=jax.ShapeDtypeStruct((cap, width, width), jnp.float32),
        compiler_params=pltpu.CompilerParams(
            dimension_semantics=("arbitrary",), vmem_limit_bytes=16 * 1024 * 1024
        ),
        cost_estimate=pl.CostEstimate(
            flops=2 * cap * tokens * width * width,
            bytes_accessed=cap * width * width * 4 + tokens * width * 2 * (n_left + n_right),
            transcendentals=0,
        ),
        input_output_aliases={3 + n_l + n_r: 0} if extra else {},
        name="block_grads",
    )(slots, left_arr, right_arr, *left, *right, *extra)


def on_device(tokens, in_blocks, in_slots, out_blocks, out_slots, cotangent, *, hidden_total):
    w_in = in_blocks.reshape(in_blocks.shape[2:])
    w_out = out_blocks.reshape(out_blocks.shape[2:])
    w_in = pltpu.with_memory_space_constraint(w_in, pltpu.HBM)
    w_out = pltpu.with_memory_space_constraint(w_out, pltpu.HBM)
    slots_in = in_slots
    slots_out = out_slots.reshape(in_slots.shape)
    width = w_in.shape[-1]
    cap = w_in.shape[0]
    tensor_count = lax.axis_size("tensor")
    seq_count = lax.axis_size("seq")
    feat_blocks = tokens.shape[1] // width
    hid_blocks = hidden_total // tensor_count // width
    tensor_rows = tokens.shape[0]
    token_count = tensor_rows * tensor_count
    seq_rows = token_count // seq_count
    far_t, far_s = tensor_count // 2, seq_count // 2

    def near_move(v, axis, count):
        return lax.ppermute(v, axis, [(i, i ^ 1) for i in range(count)])

    def far_move(v, axis, count, shift):
        half = count // 2
        pairs = [(o * 2 + c, ((o + shift) % half) * 2 + c) for o in range(half) for c in range(2)]
        return lax.ppermute(v, axis, pairs)

    me = lax.axis_index("seq")
    shifts = jnp.arange(seq_count, dtype=jnp.int32)
    far_of = (me // 2 + far_s - shifts // 2) % far_s
    seq_part = (far_of * 2 + (me % 2 + shifts % 2) % 2) * seq_rows
    near_order = jnp.concatenate([seq_part[0::2], seq_part[1::2]])

    def gather_far(own):
        return [own] + [far_move(own, "tensor", tensor_count, k) for k in range(1, far_t)]

    def gather_near(far):
        pieces = []
        for piece in far:
            pieces += [piece, near_move(piece, "tensor", tensor_count)]
        return pieces

    def pair_out(keep, got):
        pair = [keep[k].astype(jnp.float32) + got[k].astype(jnp.float32) for k in range(far_t)]
        return pair[0], [value.astype(jnp.bfloat16) for value in pair[1:]]

    def total_out(own, pairs):
        moved = [far_move(pairs[k - 1], "tensor", tensor_count, far_t - k) for k in range(1, far_t)]
        total = own
        for value in moved:
            total = total + value.astype(jnp.float32)
        return total.astype(jnp.bfloat16)

    def pair_hidden(keep, send):
        got = near_move(send, "seq", seq_count)
        pair = [keep[k].astype(jnp.float32) + got[k].astype(jnp.float32) for k in range(far_s)]
        return pair[0], [value.astype(jnp.bfloat16) for value in pair[1:]]

    def total_hidden(own, pairs, *earlier):
        moved = [far_move(pairs[k - 1], "seq", seq_count, far_s - k) for k in range(1, far_s)]
        total = own
        for value in moved:
            total = total + after(value, *earlier).astype(jnp.float32)
        return total

    def spread_far(own):
        return [own] + [far_move(own, "seq", seq_count, k) for k in range(1, far_s)]

    def spread_near(far):
        pieces = []
        for piece in far:
            pieces += [piece, near_move(piece, "seq", seq_count)]
        return pieces

    hidden_lengths = [(far_s, seq_rows)] * 2
    token_lengths = [(far_t, tensor_rows)] * 2
    token_rows = [(2 * k + flip) * tensor_rows for flip in range(2) for k in range(far_t)]

    tok_far = gather_far(tokens)
    in_by_col, out_by_row, w_in_near = pair_tables(
        [(in_slots, feat_blocks, hid_blocks, False), (slots_out, hid_blocks, feat_blocks, True)],
        [w_in],
    )
    cot_far = gather_far(cotangent)
    tok = gather_near(tok_far)
    cot = gather_near(cot_far)
    keep_h, send_h, w_out_near = block_product(
        tok, None, w_in_near, in_by_col, hid_blocks, hidden_lengths, near_order, False, [w_out]
    )
    own_h, pairs_h = pair_hidden(keep_h, send_h)
    keep_g, send_g = block_product(
        after(cot, pairs_h), None, w_out_near, out_by_row, hid_blocks, hidden_lengths, near_order, True
    )
    later_in, later_out = after((slots_in, slots_out), keep_g)
    out_by_col, in_by_row = pair_tables(
        [(later_out, hid_blocks, feat_blocks, False), (later_in, feat_blocks, hid_blocks, True)]
    )
    hidden = total_hidden(own_h, pairs_h)
    own_act = gelu_value(hidden).astype(jnp.bfloat16)
    own_g, pairs_g = pair_hidden(keep_g, send_g)
    act_far = spread_far(after(own_act, pairs_g))
    activated = spread_near(act_far)
    grad_act = total_hidden(own_g, pairs_g, own_act, out_by_col)
    own_gh = (grad_act * gelu_slope(hidden)).astype(jnp.bfloat16)
    gh_far = spread_far(own_gh)
    grad_hidden = spread_near(gh_far)

    keep_o, send_o, w_in_near = block_product(
        after(activated, own_gh),
        seq_part,
        w_out_near,
        out_by_col,
        feat_blocks,
        token_lengths,
        token_rows,
        False,
        [w_in],
    )
    got_o = near_move(send_o, "tensor", tensor_count)
    keep_t, send_t = block_product(
        after(grad_hidden, keep_o), seq_part, w_in_near, in_by_row, feat_blocks, token_lengths, token_rows, True
    )
    got_t = near_move(send_t, "tensor", tensor_count)
    parts = 2 if cap % 96 == 0 else 1
    act_t = after(activated, keep_t)
    grad_out = block_grads(act_t, seq_part, cot, None, slots_out, 0, parts)
    own_o, pairs_o = pair_out(keep_o, after(got_o, grad_out))
    for part in range(1, parts):
        grad_out = block_grads(
            after(act_t, pairs_o), seq_part, cot, None, slots_out, part, parts, grad_out
        )
    own_t, pairs_t = pair_out(keep_t, after(got_t, grad_out))
    grad_in = block_grads(tok, None, after(grad_hidden, pairs_t), seq_part, slots_in)
    output = total_out(own_o, pairs_o)
    grad_tokens = total_out(own_t, pairs_t)
    return (
        output,
        grad_tokens,
        grad_in.reshape(in_blocks.shape),
        grad_out.reshape(out_blocks.shape),
    )


HIDDEN_TOTAL = 24576


def solution(mesh):
    def program(*args):
        return on_device(*args, hidden_total=HIDDEN_TOTAL)

    return jax.shard_map(
        program,
        mesh=mesh,
        in_specs=(
            P("tensor", "seq"),
            P("seq", "tensor", None, None, None),
            P("seq", "tensor", None),
            P("tensor", "seq", None, None, None),
            P("tensor", "seq", None),
            P("tensor", "seq"),
        ),
        out_specs=(
            P("tensor", "seq"),
            P("tensor", "seq"),
            P("seq", "tensor", None, None, None),
            P("tensor", "seq", None, None, None),
        ),
        check_vma=False,
    )
```

```python
import jax
import jax.numpy as jnp
from jax import lax
from jax.experimental import pallas as pl
from jax.experimental.pallas import tpu as pltpu
from jax.sharding import PartitionSpec as P


GELU_SCALE = 0.7978845608028654
GELU_CUBE = 0.044715


def gelu_value(values):
    return (
        0.5
        * values
        * (1.0 + jnp.tanh(GELU_SCALE * (values + GELU_CUBE * values * values * values)))
    )


def gelu_slope(values):
    tangent = jnp.tanh(GELU_SCALE * (values + GELU_CUBE * values * values * values))
    return 0.5 * (1.0 + tangent) + 0.5 * values * (1.0 - tangent * tangent) * GELU_SCALE * (
        1.0 + 3.0 * GELU_CUBE * values * values
    )


def after(values, *earlier):
    return lax.optimization_barrier((values, earlier))[0]


def largest_divisor(number, limit):
    return max(d for d in range(1, limit + 1) if number % d == 0)


def load_pieces(piece_refs, offsets, store, width):
    for i, piece in enumerate(piece_refs):
        length = piece.shape[0]
        start = offsets(i, length)
        for b in range(piece.shape[1] // width):
            store[b, pl.ds(start, length), :] = piece[:, b * width : (b + 1) * width]


def pair_tables(jobs, weights=()):
    cap = jobs[0][0].shape[-1]
    specs = [job[1:] for job in jobs]
    n, m = len(jobs), len(weights)
    limits = [pair_limit(cap, rows if by_row else cols) for rows, cols, by_row in specs]

    def body(*refs):
        slot_refs, far, tables, near = refs[:n], refs[n : n + m], refs[n + m : 2 * n + m], refs[2 * n + m : 2 * n + 2 * m]
        pending, sems = refs[2 * n + 2 * m : 3 * n + 2 * m], refs[3 * n + 2 * m :]
        copies = [pltpu.make_async_copy(*copy) for copy in zip(far, near, sems)]
        for copy in copies:
            copy.start()
        for (rows, cols, by_row), pend in zip(specs, pending):

            def clear(i, carry, pend=pend):
                pend[i] = -1
                return carry

            lax.fori_loop(0, (rows if by_row else cols) + 1, clear, 0)

        step = largest_divisor(cap, 8)

        def some(g, counts):
            counts = list(counts)
            for t, (rows, cols, by_row) in enumerate(specs):
                table, pend, limit = tables[t], pending[t], limits[t]
                entries = []
                for u in range(step):
                    k = g * step + u
                    pos = slot_refs[t][0, 0, k]
                    filled = pos >= 0
                    safe = jnp.maximum(pos, 0)
                    row = (safe * (-(-65536 // cols))) >> 16
                    col = safe - row * cols
                    key, src, end = (row, col, rows) if by_row else (col, row, cols)
                    entries.append((jnp.where(filled, key, end), k + src * 4096, filled))
                for key, word, filled in entries:
                    first = pend[key]
                    at = counts[t]
                    table[at] = first
                    table[limit + at] = word
                    table[2 * limit + at] = key
                    pend[key] = jnp.where(first >= 0, -1, word)
                    counts[t] = at + jnp.logical_and(first >= 0, filled).astype(jnp.int32)
            return tuple(counts)

        counts = lax.fori_loop(0, cap // step, some, (jnp.int32(0),) * n)
        for t, (rows, cols, by_row) in enumerate(specs):
            table, pend, limit = tables[t], pending[t], limits[t]
            n_dst, n_src = (rows, cols) if by_row else (cols, rows)

            def rest(d, at, table=table, pend=pend, limit=limit, n_src=n_src):
                first = pend[d]
                table[at] = first
                table[limit + at] = n_src * 4096
                table[2 * limit + at] = d
                return at + (first >= 0).astype(jnp.int32)

            at = lax.fori_loop(0, n_dst, rest, counts[t])
            for u in range(PAIR_UNROLL):
                table[at + u] = n_src * 4096
                table[limit + at + u] = n_src * 4096
                table[2 * limit + at + u] = n_dst
            table[3 * limit] = counts[t]
            table[3 * limit + 1] = (at + (PAIR_UNROLL - 1)) >> PAIR_SHIFT
        for copy in copies:
            copy.wait()

    smem = pl.BlockSpec(memory_space=pltpu.SMEM)
    return pl.pallas_call(
        body,
        in_specs=[smem] * n + [pl.BlockSpec(memory_space=pltpu.HBM)] * m,
        out_specs=[smem] * n + [pl.BlockSpec(memory_space=pltpu.VMEM)] * m,
        out_shape=[jax.ShapeDtypeStruct((3 * limit + 2,), jnp.int32) for limit in limits]
        + [jax.ShapeDtypeStruct(weight.shape, weight.dtype) for weight in weights],
        scratch_shapes=[pltpu.SMEM(((rows if by_row else cols) + 1,), jnp.int32) for rows, cols, by_row in specs]
        + [pltpu.SemaphoreType.DMA] * m,
        compiler_params=pltpu.CompilerParams(vmem_limit_bytes=1024 * 1024),
        name="pair_tables",
    )(*[job[0] for job in jobs], *weights)


PAIR_SHIFT = 4
PAIR_UNROLL = 1 << PAIR_SHIFT


def pair_limit(cap, n_dst):
    return (cap + n_dst) // 2 + PAIR_UNROLL + 1


def block_product(pieces, in_rows, blocks, table, n_dst, out_lengths, out_rows, transposed, stage=()):
    cap, width = blocks.shape[0], blocks.shape[1]
    n_src = pieces[0].shape[1] // width
    tokens = sum(piece.shape[0] for piece in pieces)
    limit = pair_limit(cap, n_dst)
    dims = (((1,), (1 if transposed else 0,)), ((), ()))
    zero_rows = jnp.zeros((1,), jnp.int32)
    in_arr = zero_rows if in_rows is None else in_rows
    static_out = isinstance(out_rows, list)
    out_arr = zero_rows if static_out else out_rows
    n_in, n_out, m = len(pieces), len(out_lengths), len(stage)

    def body(table_s, in_s, out_s, *refs):
        piece_refs = refs[:n_in]
        w_ref = refs[n_in]
        far = refs[n_in + 1 : n_in + 1 + m]
        refs = refs[n_in + 1 + m :]
        out_refs, near = refs[:n_out], refs[n_out : n_out + m]
        xs, acc = refs[n_out + m : n_out + m + 2]
        copies = [pltpu.make_async_copy(*copy) for copy in zip(far, near, refs[n_out + m + 2 :])]
        for copy in copies:
            copy.start()
        if in_rows is None:
            place = lambda i, length: i * length
        else:
            place = lambda i, length: pl.multiple_of(in_s[i], length)
        load_pieces(piece_refs, place, xs, width)
        xs[n_src] = jnp.zeros((tokens, width), xs.dtype)
        acc[...] = jnp.zeros_like(acc)

        def some(g, carry):
            terms = []
            for u in range(PAIR_UNROLL):
                n = g * PAIR_UNROLL + u
                one, two = table_s[n], table_s[limit + n]
                left = jnp.concatenate([xs[one >> 12], xs[two >> 12]], axis=1)
                right = jnp.concatenate(
                    [w_ref[one & 4095], w_ref[two & 4095]], axis=1 if transposed else 0
                )
                terms.append(lax.dot_general(left, right, dims, preferred_element_type=jnp.float32))
            for u in range(PAIR_UNROLL):
                acc[table_s[2 * limit + g * PAIR_UNROLL + u]] += terms[u]
            return carry

        lax.fori_loop(0, table_s[3 * limit + 1], some, 0)
        at = 0
        for ref in out_refs:
            lead = ref.shape[:-2]
            length = ref.shape[-2]
            for j in range(lead[0] if lead else 1):
                start = out_rows[at] if static_out else pl.multiple_of(out_s[at], length)
                at += 1
                for b in range(n_dst):
                    val = acc[b, pl.ds(start, length), :].astype(jnp.bfloat16)
                    if lead:
                        ref[j, :, b * width : (b + 1) * width] = val
                    else:
                        ref[:, b * width : (b + 1) * width] = val
        for copy in copies:
            copy.wait()

    smem = pl.BlockSpec(memory_space=pltpu.SMEM)
    vmem = pl.BlockSpec(memory_space=pltpu.VMEM)
    out_shapes = [shape + (n_dst * width,) for shape in out_lengths]
    return pl.pallas_call(
        body,
        in_specs=[smem] * 3 + [vmem] * (n_in + 1) + [pl.BlockSpec(memory_space=pltpu.HBM)] * m,
        out_specs=[vmem] * (n_out + m),
        scratch_shapes=[
            pltpu.VMEM((n_src + 1, tokens, width), jnp.bfloat16),
            pltpu.VMEM((n_dst + 1, tokens, width), jnp.float32),
        ]
        + [pltpu.SemaphoreType.DMA] * m,
        out_shape=[jax.ShapeDtypeStruct(shape, jnp.bfloat16) for shape in out_shapes]
        + [jax.ShapeDtypeStruct(array.shape, array.dtype) for array in stage],
        compiler_params=pltpu.CompilerParams(vmem_limit_bytes=8 * 1024 * 1024),
        cost_estimate=pl.CostEstimate(
            flops=2 * cap * tokens * width * width,
            bytes_accessed=cap * width * width * 2 + tokens * width * 2 * (n_src + n_dst),
            transcendentals=0,
        ),
        name="block_product",
    )(table, in_arr, out_arr, *pieces, blocks, *stage)


def block_grads(left, left_rows, right, right_rows, slots, part=0, parts=1, base=None):
    width, cap = 128, slots.shape[-1]
    n_left, n_right = left[0].shape[1] // width, right[0].shape[1] // width
    tokens = sum(piece.shape[0] for piece in left)
    chunk = largest_divisor(cap, 48)
    unroll = chunk
    steps = cap // chunk // parts
    skip = part * steps
    n_l, n_r = len(left), len(right)
    dims = (((1,), (0,)), ((), ()))
    zero_rows = jnp.zeros((1,), jnp.int32)
    left_arr = zero_rows if left_rows is None else left_rows
    right_arr = zero_rows if right_rows is None else right_rows

    def body(slot_s, left_s, right_s, *refs):
        l_refs = refs[:n_l]
        r_refs = refs[n_l : n_l + n_r]
        out, ls, lt, rs = refs[len(refs) - 4 :]
        step = pl.program_id(0)

        @pl.when(step == 0)
        def _():
            def place(given, table):
                if given is None:
                    return lambda i, length: i * length
                return lambda i, length: pl.multiple_of(table[i], length)

            load_pieces(l_refs, place(left_rows, left_s), ls, width)
            load_pieces(r_refs, place(right_rows, right_s), rs, width)
            rs[n_right] = jnp.zeros((tokens, width), rs.dtype)
            for b in range(n_left):
                lt[b] = ls[b].T

        def some(g, carry):
            at = g * unroll
            for u in range(unroll):
                k = (step + skip) * chunk + at + u
                pos = slot_s[0, 0, k]
                safe = jnp.maximum(pos, 0)
                row = (safe * (-(-65536 // n_right))) >> 16
                col = jnp.where(pos >= 0, safe - row * n_right, n_right)
                out[at + u] = lax.dot_general(
                    lt[row], rs[col], dims, preferred_element_type=jnp.float32
                )
            return carry

        lax.fori_loop(0, chunk // unroll, some, 0)

    extra = [] if base is None else [base]
    whole = lambda shape: pl.BlockSpec(shape, lambda i, *s: (0,) * len(shape))
    return pl.pallas_call(
        body,
        grid_spec=pltpu.PrefetchScalarGridSpec(
            num_scalar_prefetch=3,
            grid=(steps,),
            in_specs=[whole(piece.shape) for piece in left]
            + [whole(piece.shape) for piece in right]
            + [pl.BlockSpec(memory_space=pltpu.HBM)] * len(extra),
            out_specs=pl.BlockSpec((chunk, width, width), lambda i, *s: (i + skip, 0, 0)),
            scratch_shapes=[
                pltpu.VMEM((n_left, tokens, width), jnp.bfloat16),
                pltpu.VMEM((n_left, width, tokens), jnp.bfloat16),
                pltpu.VMEM((n_right + 1, tokens, width), jnp.bfloat16),
            ],
        ),
        out_shape=jax.ShapeDtypeStruct((cap, width, width), jnp.float32),
        compiler_params=pltpu.CompilerParams(
            dimension_semantics=("arbitrary",), vmem_limit_bytes=16 * 1024 * 1024
        ),
        cost_estimate=pl.CostEstimate(
            flops=2 * cap * tokens * width * width,
            bytes_accessed=cap * width * width * 4 + tokens * width * 2 * (n_left + n_right),
            transcendentals=0,
        ),
        input_output_aliases={3 + n_l + n_r: 0} if extra else {},
        name="block_grads",
    )(slots, left_arr, right_arr, *left, *right, *extra)


def on_device(tokens, in_blocks, in_slots, out_blocks, out_slots, cotangent, *, hidden_total):
    w_in = in_blocks.reshape(in_blocks.shape[2:])
    w_out = out_blocks.reshape(out_blocks.shape[2:])
    w_in = pltpu.with_memory_space_constraint(w_in, pltpu.HBM)
    w_out = pltpu.with_memory_space_constraint(w_out, pltpu.HBM)
    slots_in = in_slots
    slots_out = out_slots.reshape(in_slots.shape)
    width = w_in.shape[-1]
    cap = w_in.shape[0]
    tensor_count = lax.axis_size("tensor")
    seq_count = lax.axis_size("seq")
    feat_blocks = tokens.shape[1] // width
    hid_blocks = hidden_total // tensor_count // width
    tensor_rows = tokens.shape[0]
    token_count = tensor_rows * tensor_count
    seq_rows = token_count // seq_count
    far_t, far_s = tensor_count // 2, seq_count // 2

    def near_move(v, axis, count):
        return lax.ppermute(v, axis, [(i, i ^ 1) for i in range(count)])

    def far_move(v, axis, count, shift):
        half = count // 2
        pairs = [(o * 2 + c, ((o + shift) % half) * 2 + c) for o in range(half) for c in range(2)]
        return lax.ppermute(v, axis, pairs)

    me = lax.axis_index("seq")
    shifts = jnp.arange(seq_count, dtype=jnp.int32)
    far_of = (me // 2 + far_s - shifts // 2) % far_s
    seq_part = (far_of * 2 + (me % 2 + shifts % 2) % 2) * seq_rows
    near_order = jnp.concatenate([seq_part[0::2], seq_part[1::2]])

    def gather_far(own):
        return [own] + [far_move(own, "tensor", tensor_count, k) for k in range(1, far_t)]

    def gather_near(far):
        pieces = []
        for piece in far:
            pieces += [piece, near_move(piece, "tensor", tensor_count)]
        return pieces

    def pair_out(keep, got):
        pair = [keep[k].astype(jnp.float32) + got[k].astype(jnp.float32) for k in range(far_t)]
        return pair[0], [value.astype(jnp.bfloat16) for value in pair[1:]]

    def total_out(own, pairs):
        moved = [far_move(pairs[k - 1], "tensor", tensor_count, far_t - k) for k in range(1, far_t)]
        total = own
        for value in moved:
            total = total + value.astype(jnp.float32)
        return total.astype(jnp.bfloat16)

    def pair_hidden(keep, send):
        got = near_move(send, "seq", seq_count)
        pair = [keep[k].astype(jnp.float32) + got[k].astype(jnp.float32) for k in range(far_s)]
        return pair[0], [value.astype(jnp.bfloat16) for value in pair[1:]]

    def total_hidden(own, pairs, *earlier):
        moved = [far_move(pairs[k - 1], "seq", seq_count, far_s - k) for k in range(1, far_s)]
        total = own
        for value in moved:
            total = total + after(value, *earlier).astype(jnp.float32)
        return total

    def spread_far(own):
        return [own] + [far_move(own, "seq", seq_count, k) for k in range(1, far_s)]

    def spread_near(far):
        pieces = []
        for piece in far:
            pieces += [piece, near_move(piece, "seq", seq_count)]
        return pieces

    hidden_lengths = [(far_s, seq_rows)] * 2
    token_lengths = [(far_t, tensor_rows)] * 2
    token_rows = [(2 * k + flip) * tensor_rows for flip in range(2) for k in range(far_t)]

    tok_far = gather_far(tokens)
    cot_far = gather_far(cotangent)
    tok = gather_near(tok_far)
    cot = gather_near(cot_far)
    first_in, first_out = after((slots_in, slots_out), tok_far[1:])
    in_by_col, out_by_row, w_in_near = pair_tables(
        [(first_in, feat_blocks, hid_blocks, False), (first_out, hid_blocks, feat_blocks, True)], [w_in]
    )
    keep_h, send_h, w_out_near = block_product(
        tok, None, w_in_near, in_by_col, hid_blocks, hidden_lengths, near_order, False, [w_out]
    )
    own_h, pairs_h = pair_hidden(keep_h, send_h)
    keep_g, send_g = block_product(
        after(cot, pairs_h), None, w_out_near, out_by_row, hid_blocks, hidden_lengths, near_order, True
    )
    later_in, later_out = after((slots_in, slots_out), keep_g)
    out_by_col, in_by_row = pair_tables(
        [(later_out, hid_blocks, feat_blocks, False), (later_in, feat_blocks, hid_blocks, True)]
    )
    hidden = total_hidden(own_h, pairs_h)
    own_act = gelu_value(hidden).astype(jnp.bfloat16)
    own_g, pairs_g = pair_hidden(keep_g, send_g)
    act_far = spread_far(after(own_act, pairs_g))
    grad_act = total_hidden(own_g, pairs_g, own_act, out_by_col)
    own_gh = (grad_act * gelu_slope(hidden)).astype(jnp.bfloat16)
    activated = spread_near([act_far[0]] + after(act_far[1:], own_gh))
    gh_far = spread_far(own_gh)
    grad_hidden = spread_near(gh_far)

    keep_o, send_o, w_in_near = block_product(
        after(activated, own_gh),
        seq_part,
        w_out_near,
        out_by_col,
        feat_blocks,
        token_lengths,
        token_rows,
        False,
        [w_in],
    )
    got_o = near_move(send_o, "tensor", tensor_count)
    keep_t, send_t = block_product(
        after(grad_hidden, keep_o), seq_part, w_in_near, in_by_row, feat_blocks, token_lengths, token_rows, True
    )
    got_t = near_move(send_t, "tensor", tensor_count)
    parts = 2 if cap % 96 == 0 else 1
    act_t = after(activated, keep_t)
    grad_out = block_grads(act_t, seq_part, cot, None, slots_out, 0, parts)
    own_o, pairs_o = pair_out(keep_o, after(got_o, grad_out))
    for part in range(1, parts):
        grad_out = block_grads(
            after(act_t, pairs_o), seq_part, cot, None, slots_out, part, parts, grad_out
        )
    own_t, pairs_t = pair_out(keep_t, after(got_t, grad_out))
    grad_in = block_grads(tok, None, after(grad_hidden, pairs_t), seq_part, slots_in)
    output = total_out(own_o, pairs_o)
    grad_tokens = total_out(own_t, pairs_t)
    return (
        output,
        grad_tokens,
        grad_in.reshape(in_blocks.shape),
        grad_out.reshape(out_blocks.shape),
    )


HIDDEN_TOTAL = 24576


def solution(mesh):
    def program(*args):
        return on_device(*args, hidden_total=HIDDEN_TOTAL)

    return jax.shard_map(
        program,
        mesh=mesh,
        in_specs=(
            P("tensor", "seq"),
            P("seq", "tensor", None, None, None),
            P("seq", "tensor", None),
            P("tensor", "seq", None, None, None),
            P("tensor", "seq", None),
            P("tensor", "seq"),
        ),
        out_specs=(
            P("tensor", "seq"),
            P("tensor", "seq"),
            P("seq", "tensor", None, None, None),
            P("tensor", "seq", None, None, None),
        ),
        check_vma=False,
    )
```

```python
import jax
import jax.numpy as jnp
from jax import lax
from jax.experimental import pallas as pl
from jax.experimental.pallas import tpu as pltpu
from jax.sharding import PartitionSpec as P


GELU_SCALE = 0.7978845608028654
GELU_CUBE = 0.044715


def gelu_value(values):
    return (
        0.5
        * values
        * (1.0 + jnp.tanh(GELU_SCALE * (values + GELU_CUBE * values * values * values)))
    )


def gelu_slope(values):
    tangent = jnp.tanh(GELU_SCALE * (values + GELU_CUBE * values * values * values))
    return 0.5 * (1.0 + tangent) + 0.5 * values * (1.0 - tangent * tangent) * GELU_SCALE * (
        1.0 + 3.0 * GELU_CUBE * values * values
    )


def after(values, *earlier):
    return lax.optimization_barrier((values, earlier))[0]


def largest_divisor(number, limit):
    return max(d for d in range(1, limit + 1) if number % d == 0)


def load_pieces(piece_refs, offsets, store, width):
    for i, piece in enumerate(piece_refs):
        length = piece.shape[0]
        start = offsets(i, length)
        for b in range(piece.shape[1] // width):
            store[b, pl.ds(start, length), :] = piece[:, b * width : (b + 1) * width]


def pair_tables(jobs, weights):
    cap = jobs[0][0].shape[-1]
    lanes = -(-cap // 128) * 128
    specs = [job[1:] for job in jobs]
    n, m = len(jobs), len(weights)
    limits = [pair_limit(cap, rows if by_row else cols) for rows, cols, by_row in specs]

    def body(*refs):
        slot_refs, far, tables, near = refs[:n], refs[n : n + m], refs[n + m : 2 * n + m], refs[2 * n + m : 2 * n + 2 * m]
        padded, sems = refs[2 * n + 2 * m], refs[2 * n + 2 * m + 1 :]
        copies = [pltpu.make_async_copy(*copy) for copy in zip(far, near, sems)]
        for copy in copies:
            copy.start()
        iota = lambda shape, dim: lax.broadcasted_iota(jnp.int32, shape, dim)
        matmul = lambda x, y, dim: lax.dot_general(
            x.astype(jnp.bfloat16),
            y.astype(jnp.bfloat16),
            (((1,), (dim,)), ((), ())),
            preferred_element_type=jnp.float32,
        )
        flag = lambda x: jnp.where(x, 1.0, 0.0)
        upto = flag(iota((lanes, lanes), 0) <= iota((lanes, lanes), 1))
        index = iota((1, lanes), 1)
        for t, (rows, cols, by_row) in enumerate(specs):
            n_dst, n_src = (rows, cols) if by_row else (cols, rows)
            dst_pad, limit = -(-n_dst // 16) * 16, limits[t]
            padded[...] = jnp.full((1, lanes), -1, jnp.int32)
            padded[:, :cap] = slot_refs[t][0]
            pos = padded[...]
            filled = pos >= 0
            safe = jnp.maximum(pos, 0)
            row = (safe * (-(-65536 // cols))) >> 16
            col = safe - row * cols
            key, src = (row, col) if by_row else (col, row)
            key = jnp.where(filled, key, -1)
            hot = flag(iota((dst_pad, lanes), 0) == key)
            running = matmul(hot, upto, 0)
            rank = jnp.sum(hot * running, axis=0, keepdims=True).astype(jnp.int32) - 1
            count = running[:, lanes - 1 :].astype(jnp.int32)
            pairs = ((count + 1) >> 1).astype(jnp.float32)
            below = flag(iota((dst_pad, dst_pad), 1) < iota((dst_pad, dst_pad), 0))
            start = matmul(below, jnp.broadcast_to(pairs, (dst_pad, 128)), 0)[:, :1]
            first = jnp.sum(hot * start, axis=0, keepdims=True).astype(jnp.int32)
            place = jnp.where(filled, first + (rank >> 1), -1)
            line = iota((16, lanes), 0)
            facts = jnp.where(line == 0, index >> 4, jnp.where(line == 1, index & 15, jnp.where(line == 2, src + 1, key + 1)))
            facts = facts.astype(jnp.float32)
            got = []
            for side in range(2):
                goes = flag(iota((limit, lanes), 0) == jnp.where((rank & 1) == side, place, -1))
                got.append(matmul(facts, goes, 1).astype(jnp.int32))
            for side in range(2):
                words = got[side]
                there = words[2:3] > 0
                word = words[0:1] * 16 + words[1:2] + (words[2:3] - 1) * 4096
                tables[t][side : side + 1] = jnp.where(there, word, n_src * 4096)
            keys = got[0][3:4]
            tables[t][2:3] = jnp.where(keys > 0, keys - 1, n_dst)
            total = jnp.sum(pairs, axis=0, keepdims=True).astype(jnp.int32)
            tables[t][3:4] = jnp.broadcast_to((total + (PAIR_UNROLL - 1)) >> PAIR_SHIFT, (1, limit))
        for copy in copies:
            copy.wait()

    vmem = pl.BlockSpec(memory_space=pltpu.VMEM)
    return pl.pallas_call(
        body,
        in_specs=[vmem] * n + [pl.BlockSpec(memory_space=pltpu.HBM)] * m,
        out_specs=[vmem] * (n + m),
        out_shape=[jax.ShapeDtypeStruct((4, limit), jnp.int32) for limit in limits]
        + [jax.ShapeDtypeStruct(weight.shape, weight.dtype) for weight in weights],
        scratch_shapes=[pltpu.VMEM((1, lanes), jnp.int32)] + [pltpu.SemaphoreType.DMA] * m,
        compiler_params=pltpu.CompilerParams(vmem_limit_bytes=8 * 1024 * 1024),
        name="pair_tables",
    )(*[job[0] for job in jobs], *weights)


PAIR_SHIFT = 4
PAIR_UNROLL = 1 << PAIR_SHIFT


def pair_limit(cap, n_dst):
    return -(-((cap + n_dst) // 2 + PAIR_UNROLL) // 128) * 128


def block_product(pieces, in_rows, blocks, table, n_dst, out_lengths, out_rows, transposed, stage=()):
    cap, width = blocks.shape[0], blocks.shape[1]
    n_src = pieces[0].shape[1] // width
    tokens = sum(piece.shape[0] for piece in pieces)
    dims = (((1,), (1 if transposed else 0,)), ((), ()))
    zero_rows = jnp.zeros((1,), jnp.int32)
    in_arr = zero_rows if in_rows is None else in_rows
    static_out = isinstance(out_rows, list)
    out_arr = zero_rows if static_out else out_rows
    n_in, n_out, m = len(pieces), len(out_lengths), len(stage)

    def body(table_s, in_s, out_s, *refs):
        piece_refs = refs[:n_in]
        w_ref = refs[n_in]
        far = refs[n_in + 1 : n_in + 1 + m]
        refs = refs[n_in + 1 + m :]
        out_refs, near = refs[:n_out], refs[n_out : n_out + m]
        xs, acc = refs[n_out + m : n_out + m + 2]
        copies = [pltpu.make_async_copy(*copy) for copy in zip(far, near, refs[n_out + m + 2 :])]
        for copy in copies:
            copy.start()
        if in_rows is None:
            place = lambda i, length: i * length
        else:
            place = lambda i, length: pl.multiple_of(in_s[i], length)
        load_pieces(piece_refs, place, xs, width)
        xs[n_src] = jnp.zeros((tokens, width), xs.dtype)
        acc[...] = jnp.zeros_like(acc)

        def some(g, carry):
            terms = []
            for u in range(PAIR_UNROLL):
                n = g * PAIR_UNROLL + u
                one, two = table_s[0, n], table_s[1, n]
                left = jnp.concatenate([xs[one >> 12], xs[two >> 12]], axis=1)
                right = jnp.concatenate(
                    [w_ref[one & 4095], w_ref[two & 4095]], axis=1 if transposed else 0
                )
                terms.append(lax.dot_general(left, right, dims, preferred_element_type=jnp.float32))
            for u in range(PAIR_UNROLL):
                acc[table_s[2, g * PAIR_UNROLL + u]] += terms[u]
            return carry

        lax.fori_loop(0, table_s[3, 0], some, 0)
        at = 0
        for ref in out_refs:
            lead = ref.shape[:-2]
            length = ref.shape[-2]
            for j in range(lead[0] if lead else 1):
                start = out_rows[at] if static_out else pl.multiple_of(out_s[at], length)
                at += 1
                for b in range(n_dst):
                    val = acc[b, pl.ds(start, length), :].astype(jnp.bfloat16)
                    if lead:
                        ref[j, :, b * width : (b + 1) * width] = val
                    else:
                        ref[:, b * width : (b + 1) * width] = val
        for copy in copies:
            copy.wait()

    smem = pl.BlockSpec(memory_space=pltpu.SMEM)
    vmem = pl.BlockSpec(memory_space=pltpu.VMEM)
    out_shapes = [shape + (n_dst * width,) for shape in out_lengths]
    return pl.pallas_call(
        body,
        in_specs=[smem] * 3 + [vmem] * (n_in + 1) + [pl.BlockSpec(memory_space=pltpu.HBM)] * m,
        out_specs=[vmem] * (n_out + m),
        scratch_shapes=[
            pltpu.VMEM((n_src + 1, tokens, width), jnp.bfloat16),
            pltpu.VMEM((n_dst + 1, tokens, width), jnp.float32),
        ]
        + [pltpu.SemaphoreType.DMA] * m,
        out_shape=[jax.ShapeDtypeStruct(shape, jnp.bfloat16) for shape in out_shapes]
        + [jax.ShapeDtypeStruct(array.shape, array.dtype) for array in stage],
        compiler_params=pltpu.CompilerParams(vmem_limit_bytes=8 * 1024 * 1024),
        cost_estimate=pl.CostEstimate(
            flops=2 * cap * tokens * width * width,
            bytes_accessed=cap * width * width * 2 + tokens * width * 2 * (n_src + n_dst),
            transcendentals=0,
        ),
        name="block_product",
    )(table, in_arr, out_arr, *pieces, blocks, *stage)


def block_grads(left, left_rows, right, right_rows, slots, part=0, parts=1, base=None):
    width, cap = 128, slots.shape[-1]
    n_left, n_right = left[0].shape[1] // width, right[0].shape[1] // width
    tokens = sum(piece.shape[0] for piece in left)
    chunk = largest_divisor(cap, 48)
    unroll = chunk
    steps = cap // chunk // parts
    skip = part * steps
    n_l, n_r = len(left), len(right)
    dims = (((1,), (0,)), ((), ()))
    zero_rows = jnp.zeros((1,), jnp.int32)
    left_arr = zero_rows if left_rows is None else left_rows
    right_arr = zero_rows if right_rows is None else right_rows

    def body(slot_s, left_s, right_s, *refs):
        l_refs = refs[:n_l]
        r_refs = refs[n_l : n_l + n_r]
        out, ls, lt, rs = refs[len(refs) - 4 :]
        step = pl.program_id(0)

        @pl.when(step == 0)
        def _():
            def place(given, table):
                if given is None:
                    return lambda i, length: i * length
                return lambda i, length: pl.multiple_of(table[i], length)

            load_pieces(l_refs, place(left_rows, left_s), ls, width)
            load_pieces(r_refs, place(right_rows, right_s), rs, width)
            rs[n_right] = jnp.zeros((tokens, width), rs.dtype)
            for b in range(n_left):
                lt[b] = ls[b].T

        def some(g, carry):
            at = g * unroll
            for u in range(unroll):
                k = (step + skip) * chunk + at + u
                pos = slot_s[0, 0, k]
                safe = jnp.maximum(pos, 0)
                row = (safe * (-(-65536 // n_right))) >> 16
                col = jnp.where(pos >= 0, safe - row * n_right, n_right)
                out[at + u] = lax.dot_general(
                    lt[row], rs[col], dims, preferred_element_type=jnp.float32
                )
            return carry

        lax.fori_loop(0, chunk // unroll, some, 0)

    extra = [] if base is None else [base]
    whole = lambda shape: pl.BlockSpec(shape, lambda i, *s: (0,) * len(shape))
    return pl.pallas_call(
        body,
        grid_spec=pltpu.PrefetchScalarGridSpec(
            num_scalar_prefetch=3,
            grid=(steps,),
            in_specs=[whole(piece.shape) for piece in left]
            + [whole(piece.shape) for piece in right]
            + [pl.BlockSpec(memory_space=pltpu.HBM)] * len(extra),
            out_specs=pl.BlockSpec((chunk, width, width), lambda i, *s: (i + skip, 0, 0)),
            scratch_shapes=[
                pltpu.VMEM((n_left, tokens, width), jnp.bfloat16),
                pltpu.VMEM((n_left, width, tokens), jnp.bfloat16),
                pltpu.VMEM((n_right + 1, tokens, width), jnp.bfloat16),
            ],
        ),
        out_shape=jax.ShapeDtypeStruct((cap, width, width), jnp.float32),
        compiler_params=pltpu.CompilerParams(
            dimension_semantics=("arbitrary",), vmem_limit_bytes=16 * 1024 * 1024
        ),
        cost_estimate=pl.CostEstimate(
            flops=2 * cap * tokens * width * width,
            bytes_accessed=cap * width * width * 4 + tokens * width * 2 * (n_left + n_right),
            transcendentals=0,
        ),
        input_output_aliases={3 + n_l + n_r: 0} if extra else {},
        name="block_grads",
    )(slots, left_arr, right_arr, *left, *right, *extra)


def on_device(tokens, in_blocks, in_slots, out_blocks, out_slots, cotangent, *, hidden_total):
    w_in = in_blocks.reshape(in_blocks.shape[2:])
    w_out = out_blocks.reshape(out_blocks.shape[2:])
    w_in = pltpu.with_memory_space_constraint(w_in, pltpu.HBM)
    w_out = pltpu.with_memory_space_constraint(w_out, pltpu.HBM)
    slots_in = in_slots
    slots_out = out_slots.reshape(in_slots.shape)
    width = w_in.shape[-1]
    cap = w_in.shape[0]
    tensor_count = lax.axis_size("tensor")
    seq_count = lax.axis_size("seq")
    feat_blocks = tokens.shape[1] // width
    hid_blocks = hidden_total // tensor_count // width
    tensor_rows = tokens.shape[0]
    token_count = tensor_rows * tensor_count
    seq_rows = token_count // seq_count
    far_t, far_s = tensor_count // 2, seq_count // 2

    def near_move(v, axis, count):
        return lax.ppermute(v, axis, [(i, i ^ 1) for i in range(count)])

    def far_move(v, axis, count, shift):
        half = count // 2
        pairs = [(o * 2 + c, ((o + shift) % half) * 2 + c) for o in range(half) for c in range(2)]
        return lax.ppermute(v, axis, pairs)

    me = lax.axis_index("seq")
    shifts = jnp.arange(seq_count, dtype=jnp.int32)
    far_of = (me // 2 + far_s - shifts // 2) % far_s
    seq_part = (far_of * 2 + (me % 2 + shifts % 2) % 2) * seq_rows
    near_order = jnp.concatenate([seq_part[0::2], seq_part[1::2]])

    def gather_far(own):
        return [own] + [far_move(own, "tensor", tensor_count, k) for k in range(1, far_t)]

    def gather_near(far):
        pieces = []
        for piece in far:
            pieces += [piece, near_move(piece, "tensor", tensor_count)]
        return pieces

    def pair_out(keep, got):
        pair = [keep[k].astype(jnp.float32) + got[k].astype(jnp.float32) for k in range(far_t)]
        return pair[0], [value.astype(jnp.bfloat16) for value in pair[1:]]

    def total_out(own, pairs):
        moved = [far_move(pairs[k - 1], "tensor", tensor_count, far_t - k) for k in range(1, far_t)]
        total = own
        for value in moved:
            total = total + value.astype(jnp.float32)
        return total.astype(jnp.bfloat16)

    def pair_hidden(keep, send):
        got = near_move(send, "seq", seq_count)
        pair = [keep[k].astype(jnp.float32) + got[k].astype(jnp.float32) for k in range(far_s)]
        return pair[0], [value.astype(jnp.bfloat16) for value in pair[1:]]

    def total_hidden(own, pairs, *earlier):
        moved = [far_move(pairs[k - 1], "seq", seq_count, far_s - k) for k in range(1, far_s)]
        total = own
        for value in moved:
            total = total + after(value, *earlier).astype(jnp.float32)
        return total

    def spread_far(own):
        return [own] + [far_move(own, "seq", seq_count, k) for k in range(1, far_s)]

    def spread_near(far):
        pieces = []
        for piece in far:
            pieces += [piece, near_move(piece, "seq", seq_count)]
        return pieces

    hidden_lengths = [(far_s, seq_rows)] * 2
    token_lengths = [(far_t, tensor_rows)] * 2
    token_rows = [(2 * k + flip) * tensor_rows for flip in range(2) for k in range(far_t)]

    tok_far = gather_far(tokens)
    cot_far = gather_far(cotangent)
    tok = gather_near(tok_far)
    cot = gather_near(cot_far)
    first_in, first_out = after((slots_in, slots_out), tok_far[1:])
    in_by_col, out_by_row, out_by_col, in_by_row, w_in_near = pair_tables(
        [
            (first_in, feat_blocks, hid_blocks, False),
            (first_out, hid_blocks, feat_blocks, True),
            (first_out, hid_blocks, feat_blocks, False),
            (first_in, feat_blocks, hid_blocks, True),
        ],
        [w_in],
    )
    keep_h, send_h, w_out_near = block_product(
        tok, None, w_in_near, in_by_col, hid_blocks, hidden_lengths, near_order, False, [w_out]
    )
    own_h, pairs_h = pair_hidden(keep_h, send_h)
    keep_g, send_g = block_product(
        after(cot, pairs_h), None, w_out_near, out_by_row, hid_blocks, hidden_lengths, near_order, True
    )
    hidden = total_hidden(own_h, pairs_h)
    own_act = gelu_value(hidden).astype(jnp.bfloat16)
    own_g, pairs_g = pair_hidden(keep_g, send_g)
    act_far = spread_far(after(own_act, pairs_g))
    grad_act = total_hidden(own_g, pairs_g, own_act)
    own_gh = (grad_act * gelu_slope(hidden)).astype(jnp.bfloat16)
    activated = spread_near([act_far[0]] + after(act_far[1:], own_gh))
    gh_far = spread_far(own_gh)
    grad_hidden = spread_near(gh_far)

    keep_o, send_o, w_in_near = block_product(
        after(activated, own_gh),
        seq_part,
        w_out_near,
        out_by_col,
        feat_blocks,
        token_lengths,
        token_rows,
        False,
        [w_in],
    )
    got_o = near_move(send_o, "tensor", tensor_count)
    keep_t, send_t = block_product(
        after(grad_hidden, keep_o), seq_part, w_in_near, in_by_row, feat_blocks, token_lengths, token_rows, True
    )
    got_t = near_move(send_t, "tensor", tensor_count)
    parts = 2 if cap % 96 == 0 else 1
    act_t = after(activated, keep_t)
    grad_out = block_grads(act_t, seq_part, cot, None, slots_out, 0, parts)
    own_o, pairs_o = pair_out(keep_o, after(got_o, grad_out))
    for part in range(1, parts):
        grad_out = block_grads(
            after(act_t, pairs_o), seq_part, cot, None, slots_out, part, parts, grad_out
        )
    own_t, pairs_t = pair_out(keep_t, after(got_t, grad_out))
    grad_in = block_grads(tok, None, after(grad_hidden, pairs_t), seq_part, slots_in)
    output = total_out(own_o, pairs_o)
    grad_tokens = total_out(own_t, pairs_t)
    return (
        output,
        grad_tokens,
        grad_in.reshape(in_blocks.shape),
        grad_out.reshape(out_blocks.shape),
    )


HIDDEN_TOTAL = 24576


def solution(mesh):
    def program(*args):
        return on_device(*args, hidden_total=HIDDEN_TOTAL)

    return jax.shard_map(
        program,
        mesh=mesh,
        in_specs=(
            P("tensor", "seq"),
            P("seq", "tensor", None, None, None),
            P("seq", "tensor", None),
            P("tensor", "seq", None, None, None),
            P("tensor", "seq", None),
            P("tensor", "seq"),
        ),
        out_specs=(
            P("tensor", "seq"),
            P("tensor", "seq"),
            P("seq", "tensor", None, None, None),
            P("tensor", "seq", None, None, None),
        ),
        check_vma=False,
    )
```

```python
import jax
import jax.numpy as jnp
from jax import lax
from jax.experimental import pallas as pl
from jax.experimental.pallas import tpu as pltpu
from jax.sharding import PartitionSpec as P


GELU_SCALE = 0.7978845608028654
GELU_CUBE = 0.044715


def gelu_value(values):
    return (
        0.5
        * values
        * (1.0 + jnp.tanh(GELU_SCALE * (values + GELU_CUBE * values * values * values)))
    )


def gelu_slope(values):
    tangent = jnp.tanh(GELU_SCALE * (values + GELU_CUBE * values * values * values))
    return 0.5 * (1.0 + tangent) + 0.5 * values * (1.0 - tangent * tangent) * GELU_SCALE * (
        1.0 + 3.0 * GELU_CUBE * values * values
    )


def after(values, *earlier):
    return lax.optimization_barrier((values, earlier))[0]


def largest_divisor(number, limit):
    return max(d for d in range(1, limit + 1) if number % d == 0)


def load_pieces(piece_refs, offsets, store, width):
    for i, piece in enumerate(piece_refs):
        length = piece.shape[0]
        start = offsets(i, length)
        for b in range(piece.shape[1] // width):
            store[b, pl.ds(start, length), :] = piece[:, b * width : (b + 1) * width]


def pair_tables(jobs, weights):
    cap = jobs[0][0].shape[-1]
    lanes = -(-cap // 128) * 128
    specs = [job[1:] for job in jobs]
    n, m = len(jobs), len(weights)
    limits = [pair_limit(cap, rows if by_row else cols) for rows, cols, by_row in specs]

    def body(*refs):
        slot_refs, far, tables, near = refs[:n], refs[n : n + m], refs[n + m : 2 * n + m], refs[2 * n + m : 2 * n + 2 * m]
        padded, listed = refs[2 * n + 2 * m : 2 * n + 2 * m + 2]
        sems, list_sems = refs[2 * n + 2 * m + 2 : 2 * n + 3 * m + 2], refs[2 * n + 3 * m + 2 :]
        lists = [pltpu.make_async_copy(slot_refs[t], listed.at[t], list_sems[t]) for t in range(n)]
        copies = [pltpu.make_async_copy(*copy) for copy in zip(far, near, sems)]
        for copy in lists + copies:
            copy.start()
        iota = lambda shape, dim: lax.broadcasted_iota(jnp.int32, shape, dim)
        matmul = lambda x, y, dim: lax.dot_general(
            x.astype(jnp.bfloat16),
            y.astype(jnp.bfloat16),
            (((1,), (dim,)), ((), ())),
            preferred_element_type=jnp.float32,
        )
        flag = lambda x: jnp.where(x, 1.0, 0.0)
        upto = flag(iota((lanes, lanes), 0) <= iota((lanes, lanes), 1))
        index = iota((1, lanes), 1)
        for t, (rows, cols, by_row) in enumerate(specs):
            n_dst, n_src = (rows, cols) if by_row else (cols, rows)
            dst_pad, limit = -(-n_dst // 16) * 16, limits[t]
            padded[...] = jnp.full((1, lanes), -1, jnp.int32)
            lists[t].wait()
            padded[:, :cap] = listed[t, 0]
            pos = padded[...]
            filled = pos >= 0
            safe = jnp.maximum(pos, 0)
            row = (safe * (-(-65536 // cols))) >> 16
            col = safe - row * cols
            key, src = (row, col) if by_row else (col, row)
            key = jnp.where(filled, key, -1)
            hot = flag(iota((dst_pad, lanes), 0) == key)
            running = matmul(hot, upto, 0)
            rank = jnp.sum(hot * running, axis=0, keepdims=True).astype(jnp.int32) - 1
            count = running[:, lanes - 1 :].astype(jnp.int32)
            pairs = ((count + 1) >> 1).astype(jnp.float32)
            below = flag(iota((dst_pad, dst_pad), 1) < iota((dst_pad, dst_pad), 0))
            start = matmul(below, jnp.broadcast_to(pairs, (dst_pad, 128)), 0)[:, :1]
            first = jnp.sum(hot * start, axis=0, keepdims=True).astype(jnp.int32)
            place = jnp.where(filled, first + (rank >> 1), -1)
            line = iota((16, lanes), 0)
            facts = jnp.where(line == 0, index >> 4, jnp.where(line == 1, index & 15, jnp.where(line == 2, src + 1, key + 1)))
            facts = facts.astype(jnp.float32)
            got = []
            for side in range(2):
                goes = flag(iota((limit, lanes), 0) == jnp.where((rank & 1) == side, place, -1))
                got.append(matmul(facts, goes, 1).astype(jnp.int32))
            for side in range(2):
                words = got[side]
                there = words[2:3] > 0
                word = words[0:1] * 16 + words[1:2] + (words[2:3] - 1) * 4096
                tables[t][side : side + 1] = jnp.where(there, word, n_src * 4096)
            keys = got[0][3:4]
            tables[t][2:3] = jnp.where(keys > 0, keys - 1, n_dst)
            total = jnp.sum(pairs, axis=0, keepdims=True).astype(jnp.int32)
            tables[t][3:4] = jnp.broadcast_to((total + (PAIR_UNROLL - 1)) >> PAIR_SHIFT, (1, limit))
        for copy in copies:
            copy.wait()

    vmem = pl.BlockSpec(memory_space=pltpu.VMEM)
    return pl.pallas_call(
        body,
        in_specs=[pl.BlockSpec(memory_space=pltpu.HBM)] * (n + m),
        out_specs=[vmem] * (n + m),
        out_shape=[jax.ShapeDtypeStruct((4, limit), jnp.int32) for limit in limits]
        + [jax.ShapeDtypeStruct(weight.shape, weight.dtype) for weight in weights],
        scratch_shapes=[pltpu.VMEM((1, lanes), jnp.int32), pltpu.VMEM((n, 1, 1, cap), jnp.int32)]
        + [pltpu.SemaphoreType.DMA] * (m + n),
        compiler_params=pltpu.CompilerParams(vmem_limit_bytes=8 * 1024 * 1024),
        name="pair_tables",
    )(*[pltpu.with_memory_space_constraint(job[0], pltpu.HBM) for job in jobs], *weights)


PAIR_SHIFT = 4
PAIR_UNROLL = 1 << PAIR_SHIFT


def pair_limit(cap, n_dst):
    return -(-((cap + n_dst) // 2 + PAIR_UNROLL) // 128) * 128


def block_product(pieces, in_rows, blocks, table, n_dst, out_lengths, out_rows, transposed, stage=()):
    cap, width = blocks.shape[0], blocks.shape[1]
    n_src = pieces[0].shape[1] // width
    tokens = sum(piece.shape[0] for piece in pieces)
    dims = (((1,), (1 if transposed else 0,)), ((), ()))
    zero_rows = jnp.zeros((1,), jnp.int32)
    in_arr = zero_rows if in_rows is None else in_rows
    static_out = isinstance(out_rows, list)
    out_arr = zero_rows if static_out else out_rows
    n_in, n_out, m = len(pieces), len(out_lengths), len(stage)

    def body(table_s, in_s, out_s, *refs):
        piece_refs = refs[:n_in]
        w_ref = refs[n_in]
        far = refs[n_in + 1 : n_in + 1 + m]
        refs = refs[n_in + 1 + m :]
        out_refs, near = refs[:n_out], refs[n_out : n_out + m]
        xs, acc = refs[n_out + m : n_out + m + 2]
        copies = [pltpu.make_async_copy(*copy) for copy in zip(far, near, refs[n_out + m + 2 :])]
        for copy in copies:
            copy.start()
        if in_rows is None:
            place = lambda i, length: i * length
        else:
            place = lambda i, length: pl.multiple_of(in_s[i], length)
        load_pieces(piece_refs, place, xs, width)
        xs[n_src] = jnp.zeros((tokens, width), xs.dtype)
        acc[...] = jnp.zeros_like(acc)

        def some(g, carry):
            terms = []
            for u in range(PAIR_UNROLL):
                n = g * PAIR_UNROLL + u
                one, two = table_s[0, n], table_s[1, n]
                left = jnp.concatenate([xs[one >> 12], xs[two >> 12]], axis=1)
                right = jnp.concatenate(
                    [w_ref[one & 4095], w_ref[two & 4095]], axis=1 if transposed else 0
                )
                terms.append(lax.dot_general(left, right, dims, preferred_element_type=jnp.float32))
            for u in range(PAIR_UNROLL):
                acc[table_s[2, g * PAIR_UNROLL + u]] += terms[u]
            return carry

        lax.fori_loop(0, table_s[3, 0], some, 0)
        at = 0
        for ref in out_refs:
            lead = ref.shape[:-2]
            length = ref.shape[-2]
            for j in range(lead[0] if lead else 1):
                start = out_rows[at] if static_out else pl.multiple_of(out_s[at], length)
                at += 1
                for b in range(n_dst):
                    val = acc[b, pl.ds(start, length), :].astype(jnp.bfloat16)
                    if lead:
                        ref[j, :, b * width : (b + 1) * width] = val
                    else:
                        ref[:, b * width : (b + 1) * width] = val
        for copy in copies:
            copy.wait()

    smem = pl.BlockSpec(memory_space=pltpu.SMEM)
    vmem = pl.BlockSpec(memory_space=pltpu.VMEM)
    out_shapes = [shape + (n_dst * width,) for shape in out_lengths]
    return pl.pallas_call(
        body,
        in_specs=[smem] * 3 + [vmem] * (n_in + 1) + [pl.BlockSpec(memory_space=pltpu.HBM)] * m,
        out_specs=[vmem] * (n_out + m),
        scratch_shapes=[
            pltpu.VMEM((n_src + 1, tokens, width), jnp.bfloat16),
            pltpu.VMEM((n_dst + 1, tokens, width), jnp.float32),
        ]
        + [pltpu.SemaphoreType.DMA] * m,
        out_shape=[jax.ShapeDtypeStruct(shape, jnp.bfloat16) for shape in out_shapes]
        + [jax.ShapeDtypeStruct(array.shape, array.dtype) for array in stage],
        compiler_params=pltpu.CompilerParams(vmem_limit_bytes=8 * 1024 * 1024),
        cost_estimate=pl.CostEstimate(
            flops=2 * cap * tokens * width * width,
            bytes_accessed=cap * width * width * 2 + tokens * width * 2 * (n_src + n_dst),
            transcendentals=0,
        ),
        name="block_product",
    )(table, in_arr, out_arr, *pieces, blocks, *stage)


def block_grads(left, left_rows, right, right_rows, slots, part=0, parts=1, base=None):
    width, cap = 128, slots.shape[-1]
    n_left, n_right = left[0].shape[1] // width, right[0].shape[1] // width
    tokens = sum(piece.shape[0] for piece in left)
    chunk = largest_divisor(cap, 48)
    unroll = chunk
    steps = cap // chunk // parts
    skip = part * steps
    n_l, n_r = len(left), len(right)
    dims = (((1,), (0,)), ((), ()))
    zero_rows = jnp.zeros((1,), jnp.int32)
    left_arr = zero_rows if left_rows is None else left_rows
    right_arr = zero_rows if right_rows is None else right_rows

    def body(slot_s, left_s, right_s, *refs):
        l_refs = refs[:n_l]
        r_refs = refs[n_l : n_l + n_r]
        out, ls, lt, rs = refs[len(refs) - 4 :]
        step = pl.program_id(0)

        @pl.when(step == 0)
        def _():
            def place(given, table):
                if given is None:
                    return lambda i, length: i * length
                return lambda i, length: pl.multiple_of(table[i], length)

            load_pieces(l_refs, place(left_rows, left_s), ls, width)
            load_pieces(r_refs, place(right_rows, right_s), rs, width)
            rs[n_right] = jnp.zeros((tokens, width), rs.dtype)
            for b in range(n_left):
                lt[b] = ls[b].T

        def some(g, carry):
            at = g * unroll
            for u in range(unroll):
                k = (step + skip) * chunk + at + u
                pos = slot_s[0, 0, k]
                safe = jnp.maximum(pos, 0)
                row = (safe * (-(-65536 // n_right))) >> 16
                col = jnp.where(pos >= 0, safe - row * n_right, n_right)
                out[at + u] = lax.dot_general(
                    lt[row], rs[col], dims, preferred_element_type=jnp.float32
                )
            return carry

        lax.fori_loop(0, chunk // unroll, some, 0)

    extra = [] if base is None else [base]
    whole = lambda shape: pl.BlockSpec(shape, lambda i, *s: (0,) * len(shape))
    return pl.pallas_call(
        body,
        grid_spec=pltpu.PrefetchScalarGridSpec(
            num_scalar_prefetch=3,
            grid=(steps,),
            in_specs=[whole(piece.shape) for piece in left]
            + [whole(piece.shape) for piece in right]
            + [pl.BlockSpec(memory_space=pltpu.HBM)] * len(extra),
            out_specs=pl.BlockSpec((chunk, width, width), lambda i, *s: (i + skip, 0, 0)),
            scratch_shapes=[
                pltpu.VMEM((n_left, tokens, width), jnp.bfloat16),
                pltpu.VMEM((n_left, width, tokens), jnp.bfloat16),
                pltpu.VMEM((n_right + 1, tokens, width), jnp.bfloat16),
            ],
        ),
        out_shape=jax.ShapeDtypeStruct((cap, width, width), jnp.float32),
        compiler_params=pltpu.CompilerParams(
            dimension_semantics=("arbitrary",), vmem_limit_bytes=16 * 1024 * 1024
        ),
        cost_estimate=pl.CostEstimate(
            flops=2 * cap * tokens * width * width,
            bytes_accessed=cap * width * width * 4 + tokens * width * 2 * (n_left + n_right),
            transcendentals=0,
        ),
        input_output_aliases={3 + n_l + n_r: 0} if extra else {},
        name="block_grads",
    )(slots, left_arr, right_arr, *left, *right, *extra)


def on_device(tokens, in_blocks, in_slots, out_blocks, out_slots, cotangent, *, hidden_total):
    w_in = in_blocks.reshape(in_blocks.shape[2:])
    w_out = out_blocks.reshape(out_blocks.shape[2:])
    w_in = pltpu.with_memory_space_constraint(w_in, pltpu.HBM)
    w_out = pltpu.with_memory_space_constraint(w_out, pltpu.HBM)
    slots_in = in_slots
    slots_out = out_slots.reshape(in_slots.shape)
    width = w_in.shape[-1]
    cap = w_in.shape[0]
    tensor_count = lax.axis_size("tensor")
    seq_count = lax.axis_size("seq")
    feat_blocks = tokens.shape[1] // width
    hid_blocks = hidden_total // tensor_count // width
    tensor_rows = tokens.shape[0]
    token_count = tensor_rows * tensor_count
    seq_rows = token_count // seq_count
    far_t, far_s = tensor_count // 2, seq_count // 2

    def near_move(v, axis, count):
        return lax.ppermute(v, axis, [(i, i ^ 1) for i in range(count)])

    def far_move(v, axis, count, shift):
        half = count // 2
        pairs = [(o * 2 + c, ((o + shift) % half) * 2 + c) for o in range(half) for c in range(2)]
        return lax.ppermute(v, axis, pairs)

    me = lax.axis_index("seq")
    shifts = jnp.arange(seq_count, dtype=jnp.int32)
    far_of = (me // 2 + far_s - shifts // 2) % far_s
    seq_part = (far_of * 2 + (me % 2 + shifts % 2) % 2) * seq_rows
    near_order = jnp.concatenate([seq_part[0::2], seq_part[1::2]])

    def gather_far(own):
        return [own] + [far_move(own, "tensor", tensor_count, k) for k in range(1, far_t)]

    def gather_near(far):
        pieces = []
        for piece in far:
            pieces += [piece, near_move(piece, "tensor", tensor_count)]
        return pieces

    def pair_out(keep, got):
        pair = [keep[k].astype(jnp.float32) + got[k].astype(jnp.float32) for k in range(far_t)]
        return pair[0], [value.astype(jnp.bfloat16) for value in pair[1:]]

    def total_out(own, pairs):
        moved = [far_move(pairs[k - 1], "tensor", tensor_count, far_t - k) for k in range(1, far_t)]
        total = own
        for value in moved:
            total = total + value.astype(jnp.float32)
        return total.astype(jnp.bfloat16)

    def total_out_halving(own, pairs):
        parts = [own] + [value.astype(jnp.float32) for value in pairs]
        while len(parts) > 1:
            half = len(parts) // 2
            sent = jnp.stack([value.astype(jnp.bfloat16) for value in parts[half:]])
            moved = far_move(sent, "tensor", tensor_count, far_t - half)
            parts = [parts[k] + moved[k].astype(jnp.float32) for k in range(half)]
        return parts[0].astype(jnp.bfloat16)

    def pair_hidden(keep, send):
        got = near_move(send, "seq", seq_count)
        pair = [keep[k].astype(jnp.float32) + got[k].astype(jnp.float32) for k in range(far_s)]
        return pair[0], [value.astype(jnp.bfloat16) for value in pair[1:]]

    def total_hidden(own, pairs, *earlier):
        moved = [far_move(pairs[k - 1], "seq", seq_count, far_s - k) for k in range(1, far_s)]
        total = own
        for value in moved:
            total = total + after(value, *earlier).astype(jnp.float32)
        return total

    def spread_far(own):
        return [own] + [far_move(own, "seq", seq_count, k) for k in range(1, far_s)]

    def spread_near(far):
        pieces = []
        for piece in far:
            pieces += [piece, near_move(piece, "seq", seq_count)]
        return pieces

    hidden_lengths = [(far_s, seq_rows)] * 2
    token_lengths = [(far_t, tensor_rows)] * 2
    token_rows = [(2 * k + flip) * tensor_rows for flip in range(2) for k in range(far_t)]

    tok_far = gather_far(tokens)
    cot_far = gather_far(cotangent)
    tok = gather_near(tok_far)
    cot = gather_near(cot_far)
    first_in, first_out = after((slots_in, slots_out), tok_far[1:])
    in_by_col, out_by_row, out_by_col, in_by_row, w_in_near = pair_tables(
        [
            (first_in, feat_blocks, hid_blocks, False),
            (first_out, hid_blocks, feat_blocks, True),
            (first_out, hid_blocks, feat_blocks, False),
            (first_in, feat_blocks, hid_blocks, True),
        ],
        [w_in],
    )
    keep_h, send_h, w_out_near = block_product(
        tok, None, w_in_near, in_by_col, hid_blocks, hidden_lengths, near_order, False, [w_out]
    )
    own_h, pairs_h = pair_hidden(keep_h, send_h)
    keep_g, send_g = block_product(
        after(cot, pairs_h), None, w_out_near, out_by_row, hid_blocks, hidden_lengths, near_order, True
    )
    hidden = total_hidden(own_h, pairs_h)
    own_act = gelu_value(hidden).astype(jnp.bfloat16)
    own_g, pairs_g = pair_hidden(keep_g, send_g)
    act_far = spread_far(after(own_act, pairs_g))
    grad_act = total_hidden(own_g, pairs_g, own_act)
    own_gh = (grad_act * gelu_slope(hidden)).astype(jnp.bfloat16)
    activated = spread_near([act_far[0]] + after(act_far[1:], own_gh))
    gh_far = spread_far(own_gh)
    grad_hidden = spread_near(gh_far)

    keep_o, send_o, w_in_near = block_product(
        after(activated, own_gh),
        seq_part,
        w_out_near,
        out_by_col,
        feat_blocks,
        token_lengths,
        token_rows,
        False,
        [w_in],
    )
    got_o = near_move(send_o, "tensor", tensor_count)
    keep_t, send_t = block_product(
        after(grad_hidden, keep_o), seq_part, w_in_near, in_by_row, feat_blocks, token_lengths, token_rows, True
    )
    got_t = near_move(send_t, "tensor", tensor_count)
    parts = 2 if cap % 96 == 0 else 1
    act_t = after(activated, keep_t)
    grad_out = block_grads(act_t, seq_part, cot, None, slots_out, 0, parts)
    own_o, pairs_o = pair_out(keep_o, after(got_o, grad_out))
    for part in range(1, parts):
        grad_out = block_grads(
            after(act_t, pairs_o), seq_part, cot, None, slots_out, part, parts, grad_out
        )
    own_t, pairs_t = pair_out(keep_t, after(got_t, grad_out))
    grad_in = block_grads(tok, None, after(grad_hidden, pairs_t), seq_part, slots_in)
    output = total_out_halving(own_o, pairs_o)
    grad_tokens = total_out(own_t, pairs_t)
    return (
        output,
        grad_tokens,
        grad_in.reshape(in_blocks.shape),
        grad_out.reshape(out_blocks.shape),
    )


HIDDEN_TOTAL = 24576


def solution(mesh):
    def program(*args):
        return on_device(*args, hidden_total=HIDDEN_TOTAL)

    return jax.shard_map(
        program,
        mesh=mesh,
        in_specs=(
            P("tensor", "seq"),
            P("seq", "tensor", None, None, None),
            P("seq", "tensor", None),
            P("tensor", "seq", None, None, None),
            P("tensor", "seq", None),
            P("tensor", "seq"),
        ),
        out_specs=(
            P("tensor", "seq"),
            P("tensor", "seq"),
            P("seq", "tensor", None, None, None),
            P("tensor", "seq", None, None, None),
        ),
        check_vma=False,
    )
```

```python
import jax
import jax.numpy as jnp
from jax import lax
from jax.experimental import pallas as pl
from jax.experimental.pallas import tpu as pltpu
from jax.sharding import PartitionSpec as P


GELU_SCALE = 0.7978845608028654
GELU_CUBE = 0.044715


def gelu_value(values):
    return (
        0.5
        * values
        * (1.0 + jnp.tanh(GELU_SCALE * (values + GELU_CUBE * values * values * values)))
    )


def gelu_slope(values):
    tangent = jnp.tanh(GELU_SCALE * (values + GELU_CUBE * values * values * values))
    return 0.5 * (1.0 + tangent) + 0.5 * values * (1.0 - tangent * tangent) * GELU_SCALE * (
        1.0 + 3.0 * GELU_CUBE * values * values
    )


def after(values, *earlier):
    return lax.optimization_barrier((values, earlier))[0]


def largest_divisor(number, limit):
    return max(d for d in range(1, limit + 1) if number % d == 0)


def load_pieces(piece_refs, offsets, store, width):
    for i, piece in enumerate(piece_refs):
        length = piece.shape[0]
        start = offsets(i, length)
        for b in range(piece.shape[1] // width):
            store[b, pl.ds(start, length), :] = piece[:, b * width : (b + 1) * width]


def pair_tables(jobs, weights):
    cap = jobs[0][0].shape[-1]
    lanes = -(-cap // 128) * 128
    specs = [job[1:] for job in jobs]
    n, m = len(jobs), len(weights)
    limits = [pair_limit(cap, rows if by_row else cols) for rows, cols, by_row in specs]

    def body(*refs):
        slot_refs, far, tables, near = refs[:n], refs[n : n + m], refs[n + m : 2 * n + m], refs[2 * n + m : 2 * n + 2 * m]
        padded, listed = refs[2 * n + 2 * m : 2 * n + 2 * m + 2]
        sems, list_sems = refs[2 * n + 2 * m + 2 : 2 * n + 3 * m + 2], refs[2 * n + 3 * m + 2 :]
        lists = [pltpu.make_async_copy(slot_refs[t], listed.at[t], list_sems[t]) for t in range(n)]
        copies = [pltpu.make_async_copy(*copy) for copy in zip(far, near, sems)]
        for copy in lists + copies:
            copy.start()
        iota = lambda shape, dim: lax.broadcasted_iota(jnp.int32, shape, dim)
        matmul = lambda x, y, dim: lax.dot_general(
            x.astype(jnp.bfloat16),
            y.astype(jnp.bfloat16),
            (((1,), (dim,)), ((), ())),
            preferred_element_type=jnp.float32,
        )
        flag = lambda x: jnp.where(x, 1.0, 0.0)
        upto = flag(iota((lanes, lanes), 0) <= iota((lanes, lanes), 1))
        index = iota((1, lanes), 1)
        for t, (rows, cols, by_row) in enumerate(specs):
            n_dst, n_src = (rows, cols) if by_row else (cols, rows)
            dst_pad, limit = -(-n_dst // 16) * 16, limits[t]
            padded[...] = jnp.full((1, lanes), -1, jnp.int32)
            lists[t].wait()
            padded[:, :cap] = listed[t, 0]
            pos = padded[...]
            filled = pos >= 0
            safe = jnp.maximum(pos, 0)
            row = (safe * (-(-65536 // cols))) >> 16
            col = safe - row * cols
            key, src = (row, col) if by_row else (col, row)
            key = jnp.where(filled, key, -1)
            hot = flag(iota((dst_pad, lanes), 0) == key)
            running = matmul(hot, upto, 0)
            rank = jnp.sum(hot * running, axis=0, keepdims=True).astype(jnp.int32) - 1
            count = running[:, lanes - 1 :].astype(jnp.int32)
            pairs = ((count + 1) >> 1).astype(jnp.float32)
            below = flag(iota((dst_pad, dst_pad), 1) < iota((dst_pad, dst_pad), 0))
            start = matmul(below, jnp.broadcast_to(pairs, (dst_pad, 128)), 0)[:, :1]
            first = jnp.sum(hot * start, axis=0, keepdims=True).astype(jnp.int32)
            place = jnp.where(filled, first + (rank >> 1), -1)
            line = iota((16, lanes), 0)
            facts = jnp.where(line == 0, index >> 4, jnp.where(line == 1, index & 15, jnp.where(line == 2, src + 1, key + 1)))
            facts = facts.astype(jnp.float32)
            got = []
            for side in range(2):
                goes = flag(iota((limit, lanes), 0) == jnp.where((rank & 1) == side, place, -1))
                got.append(matmul(facts, goes, 1).astype(jnp.int32))
            for side in range(2):
                words = got[side]
                there = words[2:3] > 0
                word = words[0:1] * 16 + words[1:2] + (words[2:3] - 1) * 4096
                tables[t][side : side + 1] = jnp.where(there, word, n_src * 4096)
            keys = got[0][3:4]
            tables[t][2:3] = jnp.where(keys > 0, keys - 1, n_dst)
            total = jnp.sum(pairs, axis=0, keepdims=True).astype(jnp.int32)
            tables[t][3:4] = jnp.broadcast_to((total + (PAIR_UNROLL - 1)) >> PAIR_SHIFT, (1, limit))
        for copy in copies:
            copy.wait()

    vmem = pl.BlockSpec(memory_space=pltpu.VMEM)
    return pl.pallas_call(
        body,
        in_specs=[pl.BlockSpec(memory_space=pltpu.HBM)] * (n + m),
        out_specs=[vmem] * (n + m),
        out_shape=[jax.ShapeDtypeStruct((4, limit), jnp.int32) for limit in limits]
        + [jax.ShapeDtypeStruct(weight.shape, weight.dtype) for weight in weights],
        scratch_shapes=[pltpu.VMEM((1, lanes), jnp.int32), pltpu.VMEM((n, 1, 1, cap), jnp.int32)]
        + [pltpu.SemaphoreType.DMA] * (m + n),
        compiler_params=pltpu.CompilerParams(vmem_limit_bytes=8 * 1024 * 1024),
        name="pair_tables",
    )(*[pltpu.with_memory_space_constraint(job[0], pltpu.HBM) for job in jobs], *weights)


PAIR_SHIFT = 4
PAIR_UNROLL = 1 << PAIR_SHIFT


def pair_limit(cap, n_dst):
    return -(-((cap + n_dst) // 2 + PAIR_UNROLL) // 128) * 128


def block_product(pieces, in_rows, blocks, table, n_dst, out_lengths, out_rows, transposed, stage=()):
    cap, width = blocks.shape[0], blocks.shape[1]
    n_src = pieces[0].shape[1] // width
    tokens = sum(piece.shape[0] for piece in pieces)
    dims = (((1,), (1 if transposed else 0,)), ((), ()))
    zero_rows = jnp.zeros((1,), jnp.int32)
    in_arr = zero_rows if in_rows is None else in_rows
    static_out = isinstance(out_rows, list)
    out_arr = zero_rows if static_out else out_rows
    n_in, n_out, m = len(pieces), len(out_lengths), len(stage)

    def body(table_s, in_s, out_s, *refs):
        piece_refs = refs[:n_in]
        w_ref = refs[n_in]
        far = refs[n_in + 1 : n_in + 1 + m]
        refs = refs[n_in + 1 + m :]
        out_refs, near = refs[:n_out], refs[n_out : n_out + m]
        xs, acc = refs[n_out + m : n_out + m + 2]
        copies = [pltpu.make_async_copy(*copy) for copy in zip(far, near, refs[n_out + m + 2 :])]
        for copy in copies:
            copy.start()
        if in_rows is None:
            place = lambda i, length: i * length
        else:
            place = lambda i, length: pl.multiple_of(in_s[i], length)
        load_pieces(piece_refs, place, xs, width)
        xs[n_src] = jnp.zeros((tokens, width), xs.dtype)
        acc[...] = jnp.zeros_like(acc)

        def some(g, carry):
            terms = []
            for u in range(PAIR_UNROLL):
                n = g * PAIR_UNROLL + u
                one, two = table_s[0, n], table_s[1, n]
                left = jnp.concatenate([xs[one >> 12], xs[two >> 12]], axis=1)
                right = jnp.concatenate(
                    [w_ref[one & 4095], w_ref[two & 4095]], axis=1 if transposed else 0
                )
                terms.append(lax.dot_general(left, right, dims, preferred_element_type=jnp.float32))
            for u in range(PAIR_UNROLL):
                acc[table_s[2, g * PAIR_UNROLL + u]] += terms[u]
            return carry

        lax.fori_loop(0, table_s[3, 0], some, 0)
        at = 0
        for ref in out_refs:
            lead = ref.shape[:-2]
            length = ref.shape[-2]
            for j in range(lead[0] if lead else 1):
                start = out_rows[at] if static_out else pl.multiple_of(out_s[at], length)
                at += 1
                for b in range(n_dst):
                    val = acc[b, pl.ds(start, length), :].astype(jnp.bfloat16)
                    if lead:
                        ref[j, :, b * width : (b + 1) * width] = val
                    else:
                        ref[:, b * width : (b + 1) * width] = val
        for copy in copies:
            copy.wait()

    smem = pl.BlockSpec(memory_space=pltpu.SMEM)
    vmem = pl.BlockSpec(memory_space=pltpu.VMEM)
    out_shapes = [shape + (n_dst * width,) for shape in out_lengths]
    return pl.pallas_call(
        body,
        in_specs=[smem] * 3 + [vmem] * (n_in + 1) + [pl.BlockSpec(memory_space=pltpu.HBM)] * m,
        out_specs=[vmem] * (n_out + m),
        scratch_shapes=[
            pltpu.VMEM((n_src + 1, tokens, width), jnp.bfloat16),
            pltpu.VMEM((n_dst + 1, tokens, width), jnp.float32),
        ]
        + [pltpu.SemaphoreType.DMA] * m,
        out_shape=[jax.ShapeDtypeStruct(shape, jnp.bfloat16) for shape in out_shapes]
        + [jax.ShapeDtypeStruct(array.shape, array.dtype) for array in stage],
        compiler_params=pltpu.CompilerParams(vmem_limit_bytes=8 * 1024 * 1024),
        cost_estimate=pl.CostEstimate(
            flops=2 * cap * tokens * width * width,
            bytes_accessed=cap * width * width * 2 + tokens * width * 2 * (n_src + n_dst),
            transcendentals=0,
        ),
        name="block_product",
    )(table, in_arr, out_arr, *pieces, blocks, *stage)


def block_grads(left, left_rows, right, right_rows, slots, part=0, parts=1, base=None):
    width, cap = 128, slots.shape[-1]
    n_left, n_right = left[0].shape[1] // width, right[0].shape[1] // width
    tokens = sum(piece.shape[0] for piece in left)
    chunk = largest_divisor(cap, 48)
    unroll = chunk
    steps = cap // chunk // parts
    skip = part * steps
    n_l, n_r = len(left), len(right)
    dims = (((1,), (0,)), ((), ()))
    zero_rows = jnp.zeros((1,), jnp.int32)
    left_arr = zero_rows if left_rows is None else left_rows
    right_arr = zero_rows if right_rows is None else right_rows

    def body(slot_s, left_s, right_s, *refs):
        l_refs = refs[:n_l]
        r_refs = refs[n_l : n_l + n_r]
        out, ls, lt, rs = refs[len(refs) - 4 :]
        step = pl.program_id(0)

        @pl.when(step == 0)
        def _():
            def place(given, table):
                if given is None:
                    return lambda i, length: i * length
                return lambda i, length: pl.multiple_of(table[i], length)

            load_pieces(l_refs, place(left_rows, left_s), ls, width)
            load_pieces(r_refs, place(right_rows, right_s), rs, width)
            rs[n_right] = jnp.zeros((tokens, width), rs.dtype)
            for b in range(n_left):
                lt[b] = ls[b].T

        def some(g, carry):
            at = g * unroll
            for u in range(unroll):
                k = (step + skip) * chunk + at + u
                pos = slot_s[0, 0, k]
                safe = jnp.maximum(pos, 0)
                row = (safe * (-(-65536 // n_right))) >> 16
                col = jnp.where(pos >= 0, safe - row * n_right, n_right)
                out[at + u] = lax.dot_general(
                    lt[row], rs[col], dims, preferred_element_type=jnp.float32
                )
            return carry

        lax.fori_loop(0, chunk // unroll, some, 0)

    extra = [] if base is None else [base]
    whole = lambda shape: pl.BlockSpec(shape, lambda i, *s: (0,) * len(shape))
    return pl.pallas_call(
        body,
        grid_spec=pltpu.PrefetchScalarGridSpec(
            num_scalar_prefetch=3,
            grid=(steps,),
            in_specs=[whole(piece.shape) for piece in left]
            + [whole(piece.shape) for piece in right]
            + [pl.BlockSpec(memory_space=pltpu.HBM)] * len(extra),
            out_specs=pl.BlockSpec((chunk, width, width), lambda i, *s: (i + skip, 0, 0)),
            scratch_shapes=[
                pltpu.VMEM((n_left, tokens, width), jnp.bfloat16),
                pltpu.VMEM((n_left, width, tokens), jnp.bfloat16),
                pltpu.VMEM((n_right + 1, tokens, width), jnp.bfloat16),
            ],
        ),
        out_shape=jax.ShapeDtypeStruct((cap, width, width), jnp.float32),
        compiler_params=pltpu.CompilerParams(
            dimension_semantics=("arbitrary",), vmem_limit_bytes=16 * 1024 * 1024
        ),
        cost_estimate=pl.CostEstimate(
            flops=2 * cap * tokens * width * width,
            bytes_accessed=cap * width * width * 4 + tokens * width * 2 * (n_left + n_right),
            transcendentals=0,
        ),
        input_output_aliases={3 + n_l + n_r: 0} if extra else {},
        name="block_grads",
    )(slots, left_arr, right_arr, *left, *right, *extra)


def on_device(tokens, in_blocks, in_slots, out_blocks, out_slots, cotangent, *, hidden_total):
    w_in = in_blocks.reshape(in_blocks.shape[2:])
    w_out = out_blocks.reshape(out_blocks.shape[2:])
    w_in = pltpu.with_memory_space_constraint(w_in, pltpu.HBM)
    w_out = pltpu.with_memory_space_constraint(w_out, pltpu.HBM)
    slots_in = in_slots
    slots_out = out_slots.reshape(in_slots.shape)
    width = w_in.shape[-1]
    cap = w_in.shape[0]
    tensor_count = lax.axis_size("tensor")
    seq_count = lax.axis_size("seq")
    feat_blocks = tokens.shape[1] // width
    hid_blocks = hidden_total // tensor_count // width
    tensor_rows = tokens.shape[0]
    token_count = tensor_rows * tensor_count
    seq_rows = token_count // seq_count
    far_t, far_s = tensor_count // 2, seq_count // 2

    def near_move(v, axis, count):
        return lax.ppermute(v, axis, [(i, i ^ 1) for i in range(count)])

    def far_move(v, axis, count, shift):
        half = count // 2
        pairs = [(o * 2 + c, ((o + shift) % half) * 2 + c) for o in range(half) for c in range(2)]
        return lax.ppermute(v, axis, pairs)

    me = lax.axis_index("seq")
    shifts = jnp.arange(seq_count, dtype=jnp.int32)
    far_of = (me // 2 + far_s - shifts // 2) % far_s
    seq_part = (far_of * 2 + (me % 2 + shifts % 2) % 2) * seq_rows
    near_order = jnp.concatenate([seq_part[0::2], seq_part[1::2]])

    def gather_far(own):
        return [own] + [far_move(own, "tensor", tensor_count, k) for k in range(1, far_t)]

    def gather_near(far):
        pieces = []
        for piece in far:
            pieces += [piece, near_move(piece, "tensor", tensor_count)]
        return pieces

    def pair_out(keep, got):
        pair = [keep[k].astype(jnp.float32) + got[k].astype(jnp.float32) for k in range(far_t)]
        return pair[0], [value.astype(jnp.bfloat16) for value in pair[1:]]

    def total_out(own, pairs):
        moved = [far_move(pairs[k - 1], "tensor", tensor_count, far_t - k) for k in range(1, far_t)]
        total = own
        for value in moved:
            total = total + value.astype(jnp.float32)
        return total.astype(jnp.bfloat16)

    def total_out_halving(own, pairs):
        if far_t == 4:
            sent = jnp.stack([pairs[0], pairs[2]])
            pairing = [(o * 2 + c, (o ^ 1) * 2 + c) for o in range(far_t) for c in range(2)]
            moved = lax.ppermute(sent, "tensor", pairing).astype(jnp.float32)
            odd = (lax.axis_index("tensor") // 2) % 2 == 1
            own = own + jnp.where(odd, moved[1], moved[0])
            rest = pairs[1].astype(jnp.float32) + jnp.where(odd, moved[0], moved[1])
            moved = far_move(rest.astype(jnp.bfloat16), "tensor", tensor_count, 2)
            return (own + moved.astype(jnp.float32)).astype(jnp.bfloat16)
        parts = [own] + [value.astype(jnp.float32) for value in pairs]
        while len(parts) > 1:
            half = len(parts) // 2
            sent = jnp.stack([value.astype(jnp.bfloat16) for value in parts[half:]])
            moved = far_move(sent, "tensor", tensor_count, far_t - half)
            parts = [parts[k] + moved[k].astype(jnp.float32) for k in range(half)]
        return parts[0].astype(jnp.bfloat16)

    def pair_hidden(keep, send):
        got = near_move(send, "seq", seq_count)
        pair = [keep[k].astype(jnp.float32) + got[k].astype(jnp.float32) for k in range(far_s)]
        return pair[0], [value.astype(jnp.bfloat16) for value in pair[1:]]

    def total_hidden(own, pairs, *earlier):
        moved = [far_move(pairs[k - 1], "seq", seq_count, far_s - k) for k in range(1, far_s)]
        total = own
        for value in moved:
            total = total + after(value, *earlier).astype(jnp.float32)
        return total

    def spread_far(own):
        return [own] + [far_move(own, "seq", seq_count, k) for k in range(1, far_s)]

    def spread_near(far):
        pieces = []
        for piece in far:
            pieces += [piece, near_move(piece, "seq", seq_count)]
        return pieces

    hidden_lengths = [(far_s, seq_rows)] * 2
    token_lengths = [(far_t, tensor_rows)] * 2
    token_rows = [(2 * k + flip) * tensor_rows for flip in range(2) for k in range(far_t)]

    tok_far = gather_far(tokens)
    cot_far = gather_far(cotangent)
    tok = gather_near(tok_far)
    cot = gather_near(cot_far)
    first_in, first_out = after((slots_in, slots_out), tok_far[1:])
    in_by_col, out_by_row, out_by_col, in_by_row, w_in_near = pair_tables(
        [
            (first_in, feat_blocks, hid_blocks, False),
            (first_out, hid_blocks, feat_blocks, True),
            (first_out, hid_blocks, feat_blocks, False),
            (first_in, feat_blocks, hid_blocks, True),
        ],
        [w_in],
    )
    keep_h, send_h, w_out_near = block_product(
        tok, None, w_in_near, in_by_col, hid_blocks, hidden_lengths, near_order, False, [w_out]
    )
    own_h, pairs_h = pair_hidden(keep_h, send_h)
    keep_g, send_g = block_product(
        after(cot, pairs_h), None, w_out_near, out_by_row, hid_blocks, hidden_lengths, near_order, True
    )
    hidden = total_hidden(own_h, pairs_h)
    own_act = gelu_value(hidden).astype(jnp.bfloat16)
    own_g, pairs_g = pair_hidden(keep_g, send_g)
    act_far = spread_far(after(own_act, pairs_g))
    grad_act = total_hidden(own_g, pairs_g, own_act)
    own_gh = (grad_act * gelu_slope(hidden)).astype(jnp.bfloat16)
    activated = spread_near([act_far[0]] + after(act_far[1:], own_gh))
    gh_far = spread_far(own_gh)
    grad_hidden = spread_near(gh_far)

    keep_o, send_o, w_in_near = block_product(
        after(activated, own_gh),
        seq_part,
        w_out_near,
        out_by_col,
        feat_blocks,
        token_lengths,
        token_rows,
        False,
        [w_in],
    )
    got_o = near_move(send_o, "tensor", tensor_count)
    keep_t, send_t = block_product(
        after(grad_hidden, keep_o), seq_part, w_in_near, in_by_row, feat_blocks, token_lengths, token_rows, True
    )
    got_t = near_move(send_t, "tensor", tensor_count)
    parts = 2 if cap % 96 == 0 else 1
    act_t = after(activated, keep_t)
    grad_out = block_grads(act_t, seq_part, cot, None, slots_out, 0, parts)
    own_o, pairs_o = pair_out(keep_o, after(got_o, grad_out))
    for part in range(1, parts):
        grad_out = block_grads(
            after(act_t, pairs_o), seq_part, cot, None, slots_out, part, parts, grad_out
        )
    own_t, pairs_t = pair_out(keep_t, after(got_t, grad_out))
    grad_in = block_grads(tok, None, after(grad_hidden, pairs_t), seq_part, slots_in)
    output = total_out_halving(own_o, pairs_o)
    grad_tokens = total_out(own_t, pairs_t)
    return (
        output,
        grad_tokens,
        grad_in.reshape(in_blocks.shape),
        grad_out.reshape(out_blocks.shape),
    )


HIDDEN_TOTAL = 24576


def solution(mesh):
    def program(*args):
        return on_device(*args, hidden_total=HIDDEN_TOTAL)

    return jax.shard_map(
        program,
        mesh=mesh,
        in_specs=(
            P("tensor", "seq"),
            P("seq", "tensor", None, None, None),
            P("seq", "tensor", None),
            P("tensor", "seq", None, None, None),
            P("tensor", "seq", None),
            P("tensor", "seq"),
        ),
        out_specs=(
            P("tensor", "seq"),
            P("tensor", "seq"),
            P("seq", "tensor", None, None, None),
            P("tensor", "seq", None, None, None),
        ),
        check_vma=False,
    )
```

```python
import jax
import jax.numpy as jnp
from jax import lax
from jax.experimental import pallas as pl
from jax.experimental.pallas import tpu as pltpu
from jax.sharding import PartitionSpec as P


GELU_SCALE = 0.7978845608028654
GELU_CUBE = 0.044715


def gelu_value(values):
    return (
        0.5
        * values
        * (1.0 + jnp.tanh(GELU_SCALE * (values + GELU_CUBE * values * values * values)))
    )


def gelu_slope(values):
    tangent = jnp.tanh(GELU_SCALE * (values + GELU_CUBE * values * values * values))
    return 0.5 * (1.0 + tangent) + 0.5 * values * (1.0 - tangent * tangent) * GELU_SCALE * (
        1.0 + 3.0 * GELU_CUBE * values * values
    )


def after(values, *earlier):
    return lax.optimization_barrier((values, earlier))[0]


def largest_divisor(number, limit):
    return max(d for d in range(1, limit + 1) if number % d == 0)


def load_pieces(piece_refs, offsets, store, width):
    for i, piece in enumerate(piece_refs):
        length = piece.shape[0]
        start = offsets(i, length)
        for b in range(piece.shape[1] // width):
            store[b, pl.ds(start, length), :] = piece[:, b * width : (b + 1) * width]


def pair_tables(jobs, weights):
    cap = jobs[0][0].shape[-1]
    lanes = -(-cap // 128) * 128
    specs = [job[1:] for job in jobs]
    n, m = len(jobs), len(weights)
    limits = [pair_limit(cap, rows if by_row else cols) for rows, cols, by_row in specs]

    def body(*refs):
        slot_refs, far, tables, near = refs[:n], refs[n : n + m], refs[n + m : 2 * n + m], refs[2 * n + m : 2 * n + 2 * m]
        padded, listed = refs[2 * n + 2 * m : 2 * n + 2 * m + 2]
        sems, list_sems = refs[2 * n + 2 * m + 2 : 2 * n + 3 * m + 2], refs[2 * n + 3 * m + 2 :]
        lists = [pltpu.make_async_copy(slot_refs[t], listed.at[t], list_sems[t]) for t in range(n)]
        copies = [pltpu.make_async_copy(*copy) for copy in zip(far, near, sems)]
        for copy in lists + copies:
            copy.start()
        iota = lambda shape, dim: lax.broadcasted_iota(jnp.int32, shape, dim)
        matmul = lambda x, y, dim: lax.dot_general(
            x.astype(jnp.bfloat16),
            y.astype(jnp.bfloat16),
            (((1,), (dim,)), ((), ())),
            preferred_element_type=jnp.float32,
        )
        flag = lambda x: jnp.where(x, 1.0, 0.0)
        upto = flag(iota((lanes, lanes), 0) <= iota((lanes, lanes), 1))
        index = iota((1, lanes), 1)
        for t, (rows, cols, by_row) in enumerate(specs):
            n_dst, n_src = (rows, cols) if by_row else (cols, rows)
            dst_pad, limit = -(-n_dst // 16) * 16, limits[t]
            padded[...] = jnp.full((1, lanes), -1, jnp.int32)
            lists[t].wait()
            padded[:, :cap] = listed[t, 0]
            pos = padded[...]
            filled = pos >= 0
            safe = jnp.maximum(pos, 0)
            row = (safe * (-(-65536 // cols))) >> 16
            col = safe - row * cols
            key, src = (row, col) if by_row else (col, row)
            key = jnp.where(filled, key, -1)
            hot = flag(iota((dst_pad, lanes), 0) == key)
            running = matmul(hot, upto, 0)
            rank = jnp.sum(hot * running, axis=0, keepdims=True).astype(jnp.int32) - 1
            count = running[:, lanes - 1 :].astype(jnp.int32)
            pairs = ((count + 1) >> 1).astype(jnp.float32)
            below = flag(iota((dst_pad, dst_pad), 1) < iota((dst_pad, dst_pad), 0))
            start = matmul(below, jnp.broadcast_to(pairs, (dst_pad, 128)), 0)[:, :1]
            first = jnp.sum(hot * start, axis=0, keepdims=True).astype(jnp.int32)
            place = jnp.where(filled, first + (rank >> 1), -1)
            line = iota((16, lanes), 0)
            facts = jnp.where(line == 0, index >> 4, jnp.where(line == 1, index & 15, jnp.where(line == 2, src + 1, key + 1)))
            facts = facts.astype(jnp.float32)
            got = []
            for side in range(2):
                goes = flag(iota((limit, lanes), 0) == jnp.where((rank & 1) == side, place, -1))
                got.append(matmul(facts, goes, 1).astype(jnp.int32))
            for side in range(2):
                words = got[side]
                there = words[2:3] > 0
                word = words[0:1] * 16 + words[1:2] + (words[2:3] - 1) * 4096
                tables[t][side : side + 1] = jnp.where(there, word, n_src * 4096)
            keys = got[0][3:4]
            tables[t][2:3] = jnp.where(keys > 0, keys - 1, n_dst)
            total = jnp.sum(pairs, axis=0, keepdims=True).astype(jnp.int32)
            tables[t][3:4] = jnp.broadcast_to((total + (PAIR_UNROLL - 1)) >> PAIR_SHIFT, (1, limit))
        for copy in copies:
            copy.wait()

    vmem = pl.BlockSpec(memory_space=pltpu.VMEM)
    return pl.pallas_call(
        body,
        in_specs=[pl.BlockSpec(memory_space=pltpu.HBM)] * (n + m),
        out_specs=[vmem] * (n + m),
        out_shape=[jax.ShapeDtypeStruct((4, limit), jnp.int32) for limit in limits]
        + [jax.ShapeDtypeStruct(weight.shape, weight.dtype) for weight in weights],
        scratch_shapes=[pltpu.VMEM((1, lanes), jnp.int32), pltpu.VMEM((n, 1, 1, cap), jnp.int32)]
        + [pltpu.SemaphoreType.DMA] * (m + n),
        compiler_params=pltpu.CompilerParams(vmem_limit_bytes=8 * 1024 * 1024),
        name="pair_tables",
    )(*[pltpu.with_memory_space_constraint(job[0], pltpu.HBM) for job in jobs], *weights)


PAIR_SHIFT = 4
PAIR_UNROLL = 1 << PAIR_SHIFT


def pair_limit(cap, n_dst):
    return -(-((cap + n_dst) // 2 + PAIR_UNROLL) // 128) * 128


def block_product(pieces, in_rows, blocks, table, n_dst, out_lengths, out_rows, transposed, stage=()):
    cap, width = blocks.shape[0], blocks.shape[1]
    n_src = pieces[0].shape[1] // width
    tokens = sum(piece.shape[0] for piece in pieces)
    dims = (((1,), (1 if transposed else 0,)), ((), ()))
    zero_rows = jnp.zeros((1,), jnp.int32)
    in_arr = zero_rows if in_rows is None else in_rows
    static_out = isinstance(out_rows, list)
    out_arr = zero_rows if static_out else out_rows
    n_in, n_out, m = len(pieces), len(out_lengths), len(stage)

    def body(table_s, in_s, out_s, *refs):
        piece_refs = refs[:n_in]
        w_ref = refs[n_in]
        far = refs[n_in + 1 : n_in + 1 + m]
        refs = refs[n_in + 1 + m :]
        out_refs, near = refs[:n_out], refs[n_out : n_out + m]
        xs, acc = refs[n_out + m : n_out + m + 2]
        copies = [pltpu.make_async_copy(*copy) for copy in zip(far, near, refs[n_out + m + 2 :])]
        for copy in copies:
            copy.start()
        if in_rows is None:
            place = lambda i, length: i * length
        else:
            place = lambda i, length: pl.multiple_of(in_s[i], length)
        load_pieces(piece_refs, place, xs, width)
        xs[n_src] = jnp.zeros((tokens, width), xs.dtype)
        acc[...] = jnp.zeros_like(acc)

        def some(g, carry):
            terms = []
            for u in range(PAIR_UNROLL):
                n = g * PAIR_UNROLL + u
                one, two = table_s[0, n], table_s[1, n]
                left = jnp.concatenate([xs[one >> 12], xs[two >> 12]], axis=1)
                right = jnp.concatenate(
                    [w_ref[one & 4095], w_ref[two & 4095]], axis=1 if transposed else 0
                )
                terms.append(lax.dot_general(left, right, dims, preferred_element_type=jnp.float32))
            for u in range(PAIR_UNROLL):
                acc[table_s[2, g * PAIR_UNROLL + u]] += terms[u]
            return carry

        lax.fori_loop(0, table_s[3, 0], some, 0)
        at = 0
        for ref in out_refs:
            lead = ref.shape[:-2]
            length = ref.shape[-2]
            for j in range(lead[0] if lead else 1):
                start = out_rows[at] if static_out else pl.multiple_of(out_s[at], length)
                at += 1
                for b in range(n_dst):
                    val = acc[b, pl.ds(start, length), :].astype(jnp.bfloat16)
                    if lead:
                        ref[j, :, b * width : (b + 1) * width] = val
                    else:
                        ref[:, b * width : (b + 1) * width] = val
        for copy in copies:
            copy.wait()

    smem = pl.BlockSpec(memory_space=pltpu.SMEM)
    vmem = pl.BlockSpec(memory_space=pltpu.VMEM)
    out_shapes = [shape + (n_dst * width,) for shape in out_lengths]
    return pl.pallas_call(
        body,
        in_specs=[smem] * 3 + [vmem] * (n_in + 1) + [pl.BlockSpec(memory_space=pltpu.HBM)] * m,
        out_specs=[vmem] * (n_out + m),
        scratch_shapes=[
            pltpu.VMEM((n_src + 1, tokens, width), jnp.bfloat16),
            pltpu.VMEM((n_dst + 1, tokens, width), jnp.float32),
        ]
        + [pltpu.SemaphoreType.DMA] * m,
        out_shape=[jax.ShapeDtypeStruct(shape, jnp.bfloat16) for shape in out_shapes]
        + [jax.ShapeDtypeStruct(array.shape, array.dtype) for array in stage],
        compiler_params=pltpu.CompilerParams(vmem_limit_bytes=8 * 1024 * 1024),
        cost_estimate=pl.CostEstimate(
            flops=2 * cap * tokens * width * width,
            bytes_accessed=cap * width * width * 2 + tokens * width * 2 * (n_src + n_dst),
            transcendentals=0,
        ),
        name="block_product",
    )(table, in_arr, out_arr, *pieces, blocks, *stage)


def block_grads(left, left_rows, right, right_rows, slots, part=0, parts=1, base=None):
    width, cap = 128, slots.shape[-1]
    n_left, n_right = left[0].shape[1] // width, right[0].shape[1] // width
    tokens = sum(piece.shape[0] for piece in left)
    chunk = largest_divisor(cap, 48)
    unroll = chunk
    steps = cap // chunk // parts
    skip = part * steps
    n_l, n_r = len(left), len(right)
    dims = (((1,), (0,)), ((), ()))
    zero_rows = jnp.zeros((1,), jnp.int32)
    left_arr = zero_rows if left_rows is None else left_rows
    right_arr = zero_rows if right_rows is None else right_rows

    def body(slot_s, left_s, right_s, *refs):
        l_refs = refs[:n_l]
        r_refs = refs[n_l : n_l + n_r]
        out, ls, lt, rs = refs[len(refs) - 4 :]
        step = pl.program_id(0)

        @pl.when(step == 0)
        def _():
            def place(given, table):
                if given is None:
                    return lambda i, length: i * length
                return lambda i, length: pl.multiple_of(table[i], length)

            load_pieces(l_refs, place(left_rows, left_s), ls, width)
            load_pieces(r_refs, place(right_rows, right_s), rs, width)
            rs[n_right] = jnp.zeros((tokens, width), rs.dtype)
            for b in range(n_left):
                lt[b] = ls[b].T

        def some(g, carry):
            at = g * unroll
            for u in range(unroll):
                k = (step + skip) * chunk + at + u
                pos = slot_s[0, 0, k]
                safe = jnp.maximum(pos, 0)
                row = (safe * (-(-65536 // n_right))) >> 16
                col = jnp.where(pos >= 0, safe - row * n_right, n_right)
                out[at + u] = lax.dot_general(
                    lt[row], rs[col], dims, preferred_element_type=jnp.float32
                )
            return carry

        lax.fori_loop(0, chunk // unroll, some, 0)

    extra = [] if base is None else [base]
    whole = lambda shape: pl.BlockSpec(shape, lambda i, *s: (0,) * len(shape))
    return pl.pallas_call(
        body,
        grid_spec=pltpu.PrefetchScalarGridSpec(
            num_scalar_prefetch=3,
            grid=(steps,),
            in_specs=[whole(piece.shape) for piece in left]
            + [whole(piece.shape) for piece in right]
            + [pl.BlockSpec(memory_space=pltpu.HBM)] * len(extra),
            out_specs=pl.BlockSpec((chunk, width, width), lambda i, *s: (i + skip, 0, 0)),
            scratch_shapes=[
                pltpu.VMEM((n_left, tokens, width), jnp.bfloat16),
                pltpu.VMEM((n_left, width, tokens), jnp.bfloat16),
                pltpu.VMEM((n_right + 1, tokens, width), jnp.bfloat16),
            ],
        ),
        out_shape=jax.ShapeDtypeStruct((cap, width, width), jnp.float32),
        compiler_params=pltpu.CompilerParams(
            dimension_semantics=("arbitrary",), vmem_limit_bytes=16 * 1024 * 1024
        ),
        cost_estimate=pl.CostEstimate(
            flops=2 * cap * tokens * width * width,
            bytes_accessed=cap * width * width * 4 + tokens * width * 2 * (n_left + n_right),
            transcendentals=0,
        ),
        input_output_aliases={3 + n_l + n_r: 0} if extra else {},
        name="block_grads",
    )(slots, left_arr, right_arr, *left, *right, *extra)


def on_device(tokens, in_blocks, in_slots, out_blocks, out_slots, cotangent, *, hidden_total):
    w_in = in_blocks.reshape(in_blocks.shape[2:])
    w_out = out_blocks.reshape(out_blocks.shape[2:])
    w_in = pltpu.with_memory_space_constraint(w_in, pltpu.HBM)
    w_out = pltpu.with_memory_space_constraint(w_out, pltpu.HBM)
    slots_in = in_slots
    slots_out = out_slots.reshape(in_slots.shape)
    width = w_in.shape[-1]
    tensor_count = lax.axis_size("tensor")
    seq_count = lax.axis_size("seq")
    feat_blocks = tokens.shape[1] // width
    hid_blocks = hidden_total // tensor_count // width
    tensor_rows = tokens.shape[0]
    token_count = tensor_rows * tensor_count
    seq_rows = token_count // seq_count
    far_t, far_s = tensor_count // 2, seq_count // 2

    def near_move(v, axis, count):
        return lax.ppermute(v, axis, [(i, i ^ 1) for i in range(count)])

    def far_move(v, axis, count, shift):
        half = count // 2
        pairs = [(o * 2 + c, ((o + shift) % half) * 2 + c) for o in range(half) for c in range(2)]
        return lax.ppermute(v, axis, pairs)

    me = lax.axis_index("seq")
    shifts = jnp.arange(seq_count, dtype=jnp.int32)
    far_of = (me // 2 + far_s - shifts // 2) % far_s
    seq_part = (far_of * 2 + (me % 2 + shifts % 2) % 2) * seq_rows
    near_order = jnp.concatenate([seq_part[0::2], seq_part[1::2]])

    def gather_far(own):
        pieces = [own]
        for k in range(1, far_t):
            pieces.append(far_move(own, "tensor", tensor_count, k))
        return pieces

    def gather_near(far):
        pieces = []
        for piece in far:
            pieces += [piece, near_move(piece, "tensor", tensor_count)]
        return pieces

    def pair_out(keep, got):
        pair = [keep[k].astype(jnp.float32) + got[k].astype(jnp.float32) for k in range(far_t)]
        return pair[0], [value.astype(jnp.bfloat16) for value in pair[1:]]

    def total_out(own, pairs):
        moved = [far_move(pairs[k - 1], "tensor", tensor_count, far_t - k) for k in range(1, far_t)]
        total = own
        for value in moved:
            total = total + value.astype(jnp.float32)
        return total.astype(jnp.bfloat16)

    def pair_hidden(keep, send):
        got = near_move(send, "seq", seq_count)
        pair = [keep[k].astype(jnp.float32) + got[k].astype(jnp.float32) for k in range(far_s)]
        return pair[0], [value.astype(jnp.bfloat16) for value in pair[1:]]

    def total_hidden(own, pairs, *earlier):
        moved = [far_move(pairs[k - 1], "seq", seq_count, far_s - k) for k in range(1, far_s)]
        total = own
        for value in moved:
            total = total + after(value, *earlier).astype(jnp.float32)
        return total

    def spread_far(own):
        return [own] + [far_move(own, "seq", seq_count, k) for k in range(1, far_s)]

    def spread_near(far):
        pieces = []
        for piece in far:
            pieces += [piece, near_move(piece, "seq", seq_count)]
        return pieces

    hidden_lengths = [(far_s, seq_rows)] * 2
    token_lengths = [(far_t, tensor_rows)] * 2
    token_rows = [(2 * k + flip) * tensor_rows for flip in range(2) for k in range(far_t)]

    tok_far = gather_far(tokens)
    cot_far = gather_far(cotangent)
    tok = gather_near(tok_far)
    cot = gather_near(cot_far)
    first_in, first_out = after((slots_in, slots_out), tok_far[1:])
    in_by_col, out_by_row, out_by_col, in_by_row, w_in_near = pair_tables(
        [
            (first_in, feat_blocks, hid_blocks, False),
            (first_out, hid_blocks, feat_blocks, True),
            (first_out, hid_blocks, feat_blocks, False),
            (first_in, feat_blocks, hid_blocks, True),
        ],
        [w_in],
    )
    keep_h, send_h, w_out_near = block_product(
        tok, None, w_in_near, in_by_col, hid_blocks, hidden_lengths, near_order, False, [w_out]
    )
    own_h, pairs_h = pair_hidden(keep_h, send_h)
    keep_g, send_g = block_product(
        after(cot, pairs_h), None, w_out_near, out_by_row, hid_blocks, hidden_lengths, near_order, True
    )
    hidden = total_hidden(own_h, pairs_h)
    own_act = gelu_value(hidden).astype(jnp.bfloat16)
    own_g, pairs_g = pair_hidden(keep_g, send_g)
    act_far = spread_far(own_act)
    grad_act = total_hidden(own_g, pairs_g, own_act)
    own_gh = (grad_act * gelu_slope(hidden)).astype(jnp.bfloat16)
    activated = spread_near(act_far)
    gh_far = spread_far(own_gh)
    grad_hidden = spread_near(gh_far)

    keep_o, send_o, w_in_near = block_product(
        activated,
        seq_part,
        w_out_near,
        out_by_col,
        feat_blocks,
        token_lengths,
        token_rows,
        False,
        [w_in],
    )
    got_o = near_move(send_o, "tensor", tensor_count)
    grad_out = block_grads(after(activated, keep_o), seq_part, cot, None, slots_out)
    keep_t, send_t = block_product(
        after(grad_hidden, grad_out), seq_part, w_in_near, in_by_row, feat_blocks, token_lengths, token_rows, True
    )
    got_t = near_move(send_t, "tensor", tensor_count)
    own_o, pairs_o = pair_out(keep_o, after(got_o, keep_t))
    own_t, pairs_t = pair_out(keep_t, after(got_t, pairs_o))
    grad_in = block_grads(tok, None, after(grad_hidden, pairs_t), seq_part, slots_in)
    output = total_out(own_o, pairs_o)
    grad_tokens = total_out(own_t, pairs_t)
    return (
        output,
        grad_tokens,
        grad_in.reshape(in_blocks.shape),
        grad_out.reshape(out_blocks.shape),
    )


HIDDEN_TOTAL = 24576


def solution(mesh):
    def program(*args):
        return on_device(*args, hidden_total=HIDDEN_TOTAL)

    return jax.shard_map(
        program,
        mesh=mesh,
        in_specs=(
            P("tensor", "seq"),
            P("seq", "tensor", None, None, None),
            P("seq", "tensor", None),
            P("tensor", "seq", None, None, None),
            P("tensor", "seq", None),
            P("tensor", "seq"),
        ),
        out_specs=(
            P("tensor", "seq"),
            P("tensor", "seq"),
            P("seq", "tensor", None, None, None),
            P("tensor", "seq", None, None, None),
        ),
        check_vma=False,
    )
```

```python
import jax
import jax.numpy as jnp
from jax import lax
from jax.experimental import pallas as pl
from jax.experimental.pallas import tpu as pltpu
from jax.sharding import PartitionSpec as P


GELU_SCALE = 0.7978845608028654
GELU_CUBE = 0.044715


def gelu_value(values):
    return (
        0.5
        * values
        * (1.0 + jnp.tanh(GELU_SCALE * (values + GELU_CUBE * values * values * values)))
    )


def gelu_slope(values):
    tangent = jnp.tanh(GELU_SCALE * (values + GELU_CUBE * values * values * values))
    return 0.5 * (1.0 + tangent) + 0.5 * values * (1.0 - tangent * tangent) * GELU_SCALE * (
        1.0 + 3.0 * GELU_CUBE * values * values
    )


def after(values, *earlier):
    return lax.optimization_barrier((values, earlier))[0]


def largest_divisor(number, limit):
    return max(d for d in range(1, limit + 1) if number % d == 0)


def load_pieces(piece_refs, offsets, store, width):
    for i, piece in enumerate(piece_refs):
        length = piece.shape[0]
        start = offsets(i, length)
        for b in range(piece.shape[1] // width):
            store[b, pl.ds(start, length), :] = piece[:, b * width : (b + 1) * width]


def pair_tables(jobs, weights):
    cap = jobs[0][0].shape[-1]
    lanes = -(-cap // 128) * 128
    specs = [job[1:] for job in jobs]
    n, m = len(jobs), len(weights)
    limits = [pair_limit(cap, rows if by_row else cols) for rows, cols, by_row in specs]

    def body(*refs):
        slot_refs, far, tables, near = refs[:n], refs[n : n + m], refs[n + m : 2 * n + m], refs[2 * n + m : 2 * n + 2 * m]
        padded, listed = refs[2 * n + 2 * m : 2 * n + 2 * m + 2]
        sems, list_sems = refs[2 * n + 2 * m + 2 : 2 * n + 3 * m + 2], refs[2 * n + 3 * m + 2 :]
        lists = [pltpu.make_async_copy(slot_refs[t], listed.at[t], list_sems[t]) for t in range(n)]
        copies = [pltpu.make_async_copy(*copy) for copy in zip(far, near, sems)]
        for copy in lists + copies:
            copy.start()
        iota = lambda shape, dim: lax.broadcasted_iota(jnp.int32, shape, dim)
        matmul = lambda x, y, dim: lax.dot_general(
            x.astype(jnp.bfloat16),
            y.astype(jnp.bfloat16),
            (((1,), (dim,)), ((), ())),
            preferred_element_type=jnp.float32,
        )
        flag = lambda x: jnp.where(x, 1.0, 0.0)
        upto = flag(iota((lanes, lanes), 0) <= iota((lanes, lanes), 1))
        index = iota((1, lanes), 1)
        for t, (rows, cols, by_row) in enumerate(specs):
            n_dst, n_src = (rows, cols) if by_row else (cols, rows)
            dst_pad, limit = -(-n_dst // 16) * 16, limits[t]
            padded[...] = jnp.full((1, lanes), -1, jnp.int32)
            lists[t].wait()
            padded[:, :cap] = listed[t, 0]
            pos = padded[...]
            filled = pos >= 0
            safe = jnp.maximum(pos, 0)
            row = (safe * (-(-65536 // cols))) >> 16
            col = safe - row * cols
            key, src = (row, col) if by_row else (col, row)
            key = jnp.where(filled, key, -1)
            hot = flag(iota((dst_pad, lanes), 0) == key)
            running = matmul(hot, upto, 0)
            rank = jnp.sum(hot * running, axis=0, keepdims=True).astype(jnp.int32) - 1
            count = running[:, lanes - 1 :].astype(jnp.int32)
            pairs = ((count + 1) >> 1).astype(jnp.float32)
            below = flag(iota((dst_pad, dst_pad), 1) < iota((dst_pad, dst_pad), 0))
            start = matmul(below, jnp.broadcast_to(pairs, (dst_pad, 128)), 0)[:, :1]
            first = jnp.sum(hot * start, axis=0, keepdims=True).astype(jnp.int32)
            place = jnp.where(filled, first + (rank >> 1), -1)
            line = iota((16, lanes), 0)
            facts = jnp.where(line == 0, index >> 4, jnp.where(line == 1, index & 15, jnp.where(line == 2, src + 1, key + 1)))
            facts = facts.astype(jnp.float32)
            got = []
            for side in range(2):
                goes = flag(iota((limit, lanes), 0) == jnp.where((rank & 1) == side, place, -1))
                got.append(matmul(facts, goes, 1).astype(jnp.int32))
            for side in range(2):
                words = got[side]
                there = words[2:3] > 0
                word = words[0:1] * 16 + words[1:2] + (words[2:3] - 1) * 4096
                tables[t][side : side + 1] = jnp.where(there, word, n_src * 4096)
            keys = got[0][3:4]
            tables[t][2:3] = jnp.where(keys > 0, keys - 1, n_dst)
            total = jnp.sum(pairs, axis=0, keepdims=True).astype(jnp.int32)
            tables[t][3:4] = jnp.broadcast_to((total + (PAIR_UNROLL - 1)) >> PAIR_SHIFT, (1, limit))
        for copy in copies:
            copy.wait()

    vmem = pl.BlockSpec(memory_space=pltpu.VMEM)
    return pl.pallas_call(
        body,
        in_specs=[pl.BlockSpec(memory_space=pltpu.HBM)] * (n + m),
        out_specs=[vmem] * (n + m),
        out_shape=[jax.ShapeDtypeStruct((4, limit), jnp.int32) for limit in limits]
        + [jax.ShapeDtypeStruct(weight.shape, weight.dtype) for weight in weights],
        scratch_shapes=[pltpu.VMEM((1, lanes), jnp.int32), pltpu.VMEM((n, 1, 1, cap), jnp.int32)]
        + [pltpu.SemaphoreType.DMA] * (m + n),
        compiler_params=pltpu.CompilerParams(vmem_limit_bytes=8 * 1024 * 1024),
        name="pair_tables",
    )(*[pltpu.with_memory_space_constraint(job[0], pltpu.HBM) for job in jobs], *weights)


PAIR_SHIFT = 4
PAIR_UNROLL = 1 << PAIR_SHIFT


def pair_limit(cap, n_dst):
    return -(-((cap + n_dst) // 2 + PAIR_UNROLL) // 128) * 128


def block_product(pieces, in_rows, blocks, table, n_dst, out_lengths, out_rows, transposed, stage=()):
    cap, width = blocks.shape[0], blocks.shape[1]
    n_src = pieces[0].shape[1] // width
    tokens = sum(piece.shape[0] for piece in pieces)
    dims = (((1,), (1 if transposed else 0,)), ((), ()))
    zero_rows = jnp.zeros((1,), jnp.int32)
    in_arr = zero_rows if in_rows is None else in_rows
    static_out = isinstance(out_rows, list)
    out_arr = zero_rows if static_out else out_rows
    n_in, n_out, m = len(pieces), len(out_lengths), len(stage)

    def body(table_s, in_s, out_s, *refs):
        piece_refs = refs[:n_in]
        w_ref = refs[n_in]
        far = refs[n_in + 1 : n_in + 1 + m]
        refs = refs[n_in + 1 + m :]
        out_refs, near = refs[:n_out], refs[n_out : n_out + m]
        xs, acc = refs[n_out + m : n_out + m + 2]
        copies = [pltpu.make_async_copy(*copy) for copy in zip(far, near, refs[n_out + m + 2 :])]
        for copy in copies:
            copy.start()
        if in_rows is None:
            place = lambda i, length: i * length
        else:
            place = lambda i, length: pl.multiple_of(in_s[i], length)
        load_pieces(piece_refs, place, xs, width)
        xs[n_src] = jnp.zeros((tokens, width), xs.dtype)
        acc[...] = jnp.zeros_like(acc)

        def some(g, carry):
            terms = []
            for u in range(PAIR_UNROLL):
                n = g * PAIR_UNROLL + u
                one, two = table_s[0, n], table_s[1, n]
                left = jnp.concatenate([xs[one >> 12], xs[two >> 12]], axis=1)
                right = jnp.concatenate(
                    [w_ref[one & 4095], w_ref[two & 4095]], axis=1 if transposed else 0
                )
                terms.append(lax.dot_general(left, right, dims, preferred_element_type=jnp.float32))
            for u in range(PAIR_UNROLL):
                acc[table_s[2, g * PAIR_UNROLL + u]] += terms[u]
            return carry

        lax.fori_loop(0, table_s[3, 0], some, 0)
        at = 0
        for ref in out_refs:
            lead = ref.shape[:-2]
            length = ref.shape[-2]
            for j in range(lead[0] if lead else 1):
                start = out_rows[at] if static_out else pl.multiple_of(out_s[at], length)
                at += 1
                for b in range(n_dst):
                    val = acc[b, pl.ds(start, length), :].astype(jnp.bfloat16)
                    if lead:
                        ref[j, :, b * width : (b + 1) * width] = val
                    else:
                        ref[:, b * width : (b + 1) * width] = val
        for copy in copies:
            copy.wait()

    smem = pl.BlockSpec(memory_space=pltpu.SMEM)
    vmem = pl.BlockSpec(memory_space=pltpu.VMEM)
    out_shapes = [shape + (n_dst * width,) for shape in out_lengths]
    return pl.pallas_call(
        body,
        in_specs=[smem] * 3 + [vmem] * (n_in + 1) + [pl.BlockSpec(memory_space=pltpu.HBM)] * m,
        out_specs=[vmem] * (n_out + m),
        scratch_shapes=[
            pltpu.VMEM((n_src + 1, tokens, width), jnp.bfloat16),
            pltpu.VMEM((n_dst + 1, tokens, width), jnp.float32),
        ]
        + [pltpu.SemaphoreType.DMA] * m,
        out_shape=[jax.ShapeDtypeStruct(shape, jnp.bfloat16) for shape in out_shapes]
        + [jax.ShapeDtypeStruct(array.shape, array.dtype) for array in stage],
        compiler_params=pltpu.CompilerParams(vmem_limit_bytes=8 * 1024 * 1024),
        cost_estimate=pl.CostEstimate(
            flops=2 * cap * tokens * width * width,
            bytes_accessed=cap * width * width * 2 + tokens * width * 2 * (n_src + n_dst),
            transcendentals=0,
        ),
        name="block_product",
    )(table, in_arr, out_arr, *pieces, blocks, *stage)


def block_grads(left, left_rows, right, right_rows, slots, part=0, parts=1, base=None):
    width, cap = 128, slots.shape[-1]
    n_left, n_right = left[0].shape[1] // width, right[0].shape[1] // width
    tokens = sum(piece.shape[0] for piece in left)
    chunk = largest_divisor(cap, 48)
    unroll = chunk
    steps = cap // chunk // parts
    skip = part * steps
    n_l, n_r = len(left), len(right)
    dims = (((1,), (0,)), ((), ()))
    zero_rows = jnp.zeros((1,), jnp.int32)
    left_arr = zero_rows if left_rows is None else left_rows
    right_arr = zero_rows if right_rows is None else right_rows

    def body(slot_s, left_s, right_s, *refs):
        l_refs = refs[:n_l]
        r_refs = refs[n_l : n_l + n_r]
        out, ls, lt, rs = refs[len(refs) - 4 :]
        step = pl.program_id(0)

        @pl.when(step == 0)
        def _():
            def place(given, table):
                if given is None:
                    return lambda i, length: i * length
                return lambda i, length: pl.multiple_of(table[i], length)

            load_pieces(l_refs, place(left_rows, left_s), ls, width)
            load_pieces(r_refs, place(right_rows, right_s), rs, width)
            rs[n_right] = jnp.zeros((tokens, width), rs.dtype)
            for b in range(n_left):
                lt[b] = ls[b].T

        def some(g, carry):
            at = g * unroll
            for u in range(unroll):
                k = (step + skip) * chunk + at + u
                pos = slot_s[0, 0, k]
                safe = jnp.maximum(pos, 0)
                row = (safe * (-(-65536 // n_right))) >> 16
                col = jnp.where(pos >= 0, safe - row * n_right, n_right)
                out[at + u] = lax.dot_general(
                    lt[row], rs[col], dims, preferred_element_type=jnp.float32
                )
            return carry

        lax.fori_loop(0, chunk // unroll, some, 0)

    extra = [] if base is None else [base]
    whole = lambda shape: pl.BlockSpec(shape, lambda i, *s: (0,) * len(shape))
    return pl.pallas_call(
        body,
        grid_spec=pltpu.PrefetchScalarGridSpec(
            num_scalar_prefetch=3,
            grid=(steps,),
            in_specs=[whole(piece.shape) for piece in left]
            + [whole(piece.shape) for piece in right]
            + [pl.BlockSpec(memory_space=pltpu.HBM)] * len(extra),
            out_specs=pl.BlockSpec((chunk, width, width), lambda i, *s: (i + skip, 0, 0)),
            scratch_shapes=[
                pltpu.VMEM((n_left, tokens, width), jnp.bfloat16),
                pltpu.VMEM((n_left, width, tokens), jnp.bfloat16),
                pltpu.VMEM((n_right + 1, tokens, width), jnp.bfloat16),
            ],
        ),
        out_shape=jax.ShapeDtypeStruct((cap, width, width), jnp.float32),
        compiler_params=pltpu.CompilerParams(
            dimension_semantics=("arbitrary",), vmem_limit_bytes=16 * 1024 * 1024
        ),
        cost_estimate=pl.CostEstimate(
            flops=2 * cap * tokens * width * width,
            bytes_accessed=cap * width * width * 4 + tokens * width * 2 * (n_left + n_right),
            transcendentals=0,
        ),
        input_output_aliases={3 + n_l + n_r: 0} if extra else {},
        name="block_grads",
    )(slots, left_arr, right_arr, *left, *right, *extra)


def on_device(tokens, in_blocks, in_slots, out_blocks, out_slots, cotangent, *, hidden_total):
    w_in = in_blocks.reshape(in_blocks.shape[2:])
    w_out = out_blocks.reshape(out_blocks.shape[2:])
    w_in = pltpu.with_memory_space_constraint(w_in, pltpu.HBM)
    w_out = pltpu.with_memory_space_constraint(w_out, pltpu.HBM)
    slots_in = in_slots
    slots_out = out_slots.reshape(in_slots.shape)
    width = w_in.shape[-1]
    tensor_count = lax.axis_size("tensor")
    seq_count = lax.axis_size("seq")
    feat_blocks = tokens.shape[1] // width
    hid_blocks = hidden_total // tensor_count // width
    tensor_rows = tokens.shape[0]
    token_count = tensor_rows * tensor_count
    seq_rows = token_count // seq_count
    far_t, far_s = tensor_count // 2, seq_count // 2

    def near_move(v, axis, count):
        return lax.ppermute(v, axis, [(i, i ^ 1) for i in range(count)])

    def far_move(v, axis, count, shift):
        half = count // 2
        pairs = [(o * 2 + c, ((o + shift) % half) * 2 + c) for o in range(half) for c in range(2)]
        return lax.ppermute(v, axis, pairs)

    me = lax.axis_index("seq")
    shifts = jnp.arange(seq_count, dtype=jnp.int32)
    far_of = (me // 2 + far_s - shifts // 2) % far_s
    seq_part = (far_of * 2 + (me % 2 + shifts % 2) % 2) * seq_rows
    near_order = jnp.concatenate([seq_part[0::2], seq_part[1::2]])

    def gather_far(own):
        pieces = [own]
        for k in range(1, far_t):
            pieces.append(far_move(own, "tensor", tensor_count, k))
        return pieces

    def gather_near(far):
        pieces = []
        for piece in far:
            pieces += [piece, near_move(piece, "tensor", tensor_count)]
        return pieces

    def pair_out(keep, got):
        pair = [keep[k].astype(jnp.float32) + got[k].astype(jnp.float32) for k in range(far_t)]
        return pair[0], [value.astype(jnp.bfloat16) for value in pair[1:]]

    def total_out(own, pairs):
        moved = [far_move(pairs[k - 1], "tensor", tensor_count, far_t - k) for k in range(1, far_t)]
        total = own
        for value in moved:
            total = total + value.astype(jnp.float32)
        return total.astype(jnp.bfloat16)

    def pair_hidden(keep, send):
        got = near_move(send, "seq", seq_count)
        pair = [keep[k].astype(jnp.float32) + got[k].astype(jnp.float32) for k in range(far_s)]
        return pair[0], [value.astype(jnp.bfloat16) for value in pair[1:]]

    def total_hidden(own, pairs, *earlier):
        moved = [far_move(pairs[k - 1], "seq", seq_count, far_s - k) for k in range(1, far_s)]
        total = own
        for value in moved:
            total = total + after(value, *earlier).astype(jnp.float32)
        return total

    def spread_far(own):
        return [own] + [far_move(own, "seq", seq_count, k) for k in range(1, far_s)]

    def spread_near(far):
        pieces = []
        for piece in far:
            pieces += [piece, near_move(piece, "seq", seq_count)]
        return pieces

    hidden_lengths = [(far_s, seq_rows)] * 2
    token_lengths = [(far_t, tensor_rows)] * 2
    token_rows = [(2 * k + flip) * tensor_rows for flip in range(2) for k in range(far_t)]

    tok_far = gather_far(tokens)
    cot_far = gather_far(cotangent)
    tok = gather_near(tok_far)
    cot = gather_near(cot_far)
    first_in, first_out = after((slots_in, slots_out), tok_far[1:])
    in_by_col, out_by_row, out_by_col, in_by_row, w_in_near = pair_tables(
        [
            (first_in, feat_blocks, hid_blocks, False),
            (first_out, hid_blocks, feat_blocks, True),
            (first_out, hid_blocks, feat_blocks, False),
            (first_in, feat_blocks, hid_blocks, True),
        ],
        [w_in],
    )
    keep_h, send_h, w_out_near = block_product(
        tok, None, w_in_near, in_by_col, hid_blocks, hidden_lengths, near_order, False, [w_out]
    )
    own_h, pairs_h = pair_hidden(keep_h, send_h)
    keep_g, send_g = block_product(
        after(cot, pairs_h), None, w_out_near, out_by_row, hid_blocks, hidden_lengths, near_order, True
    )
    hidden = total_hidden(own_h, pairs_h)
    own_act = gelu_value(hidden).astype(jnp.bfloat16)
    own_g, pairs_g = pair_hidden(keep_g, send_g)
    act_far = spread_far(own_act)
    grad_act = total_hidden(own_g, pairs_g, own_act)
    own_gh = (grad_act * gelu_slope(hidden)).astype(jnp.bfloat16)
    activated = spread_near([act_far[0]] + after(act_far[1:], own_gh))
    gh_far = spread_far(own_gh)
    grad_hidden = spread_near(gh_far)

    keep_o, send_o, w_in_near = block_product(
        after(activated, own_gh),
        seq_part,
        w_out_near,
        out_by_col,
        feat_blocks,
        token_lengths,
        token_rows,
        False,
        [w_in],
    )
    got_o = near_move(send_o, "tensor", tensor_count)
    keep_t, send_t = block_product(
        after(grad_hidden, keep_o), seq_part, w_in_near, in_by_row, feat_blocks, token_lengths, token_rows, True
    )
    got_t = near_move(send_t, "tensor", tensor_count)
    parts = 1
    act_t = after(activated, keep_t)
    grad_out = block_grads(act_t, seq_part, cot, None, slots_out, 0, parts)
    own_o, pairs_o = pair_out(keep_o, after(got_o, grad_out))
    for part in range(1, parts):
        grad_out = block_grads(
            after(act_t, pairs_o), seq_part, cot, None, slots_out, part, parts, grad_out
        )
    own_t, pairs_t = pair_out(keep_t, after(got_t, pairs_o))
    grad_in = block_grads(tok, None, after(grad_hidden, pairs_t), seq_part, slots_in)
    output = total_out(own_o, pairs_o)
    grad_tokens = total_out(own_t, pairs_t)
    return (
        output,
        grad_tokens,
        grad_in.reshape(in_blocks.shape),
        grad_out.reshape(out_blocks.shape),
    )


HIDDEN_TOTAL = 24576


def solution(mesh):
    def program(*args):
        return on_device(*args, hidden_total=HIDDEN_TOTAL)

    return jax.shard_map(
        program,
        mesh=mesh,
        in_specs=(
            P("tensor", "seq"),
            P("seq", "tensor", None, None, None),
            P("seq", "tensor", None),
            P("tensor", "seq", None, None, None),
            P("tensor", "seq", None),
            P("tensor", "seq"),
        ),
        out_specs=(
            P("tensor", "seq"),
            P("tensor", "seq"),
            P("seq", "tensor", None, None, None),
            P("tensor", "seq", None, None, None),
        ),
        check_vma=False,
    )
```
